32 devices in a mesh: dp: 8 (over z, x), blk: 4 (over y, core).
Axes of the slice: x: 2, y: 2, z: 4, core: 2. Of those that a mesh axis runs over, the one named last changes fastest.
Arguments:
- block_input: float32 [73728, 512], P('dp', 'blk'), may hold values from -6 to 6
- cotangent: float32 [73728, 512], P('dp', 'blk'), may hold values from -6 to 6
- item_sides: int32 [8], P('dp'), may hold values from 48 to 96, as said below
- item_modes: int32 [8], P('dp'), may hold values from 12 to 32, as said below
- ln1_gain: float32 [512], P('blk'), may hold values from 0.1 to 1.9
- ln1_bias: float32 [512], P('blk'), may hold values from -3 to 3
- spec_w1: float32 [2, 8, 64, 64], P(None, 'blk'), may hold values from -0.5 to 0.5
- spec_b1: float32 [2, 8, 64], P(None, 'blk'), may hold values from -3 to 3
- spec_w2: float32 [2, 8, 64, 64], P(None, 'blk'), may hold values from -0.5 to 0.5
- spec_b2: float32 [2, 8, 64], P(None, 'blk'), may hold values from -3 to 3
- ln2_gain: float32 [512], P('blk'), may hold values from 0.1 to 1.9
- ln2_bias: float32 [512], P('blk'), may hold values from -3 to 3
- mlp_w1: float32 [512, 2048], P(None, 'blk'), may hold values from -0.25 to 0.25
- mlp_b1: float32 [2048], P('blk'), may hold values from -3 to 3
- mlp_w2: float32 [2048, 512], P('blk'), may hold values from -0.125 to 0.125
- mlp_b2: float32 [512], P('blk'), may hold values from -3 to 3
Outputs:
- block_output: float32 [73728, 512], P('dp', 'blk')
- input_grad: float32 [73728, 512], P('dp', 'blk')
- ln1_gain_grad: float32 [512], P('blk')
- ln1_bias_grad: float32 [512], P('blk')
- spec_w1_grad: float32 [2, 8, 64, 64], P(None, 'blk')
- spec_b1_grad: float32 [2, 8, 64], P(None, 'blk')
- spec_w2_grad: float32 [2, 8, 64, 64], P(None, 'blk')
- spec_b2_grad: float32 [2, 8, 64], P(None, 'blk')
- ln2_gain_grad: float32 [512], P('blk')
- ln2_bias_grad: float32 [512], P('blk')
- mlp_w1_grad: float32 [512, 2048], P(None, 'blk')
- mlp_b1_grad: float32 [2048], P('blk')
- mlp_w2_grad: float32 [2048, 512], P('blk')
- mlp_b2_grad: float32 [512], P('blk')
The draws below stay inside these ranges and needn't reach their ends.
Inputs may be any that keep to these rules, and one draw needn't show every extreme that they name: `item_sides`: each item's side is 48, 72 or 96; at least one item has side 96. `item_modes`: an item of side s keeps m between max(1, s // 4) and min(32, s // 2); an item of side 96 with m = 32 is present.
All inputs are finite; a program needn't handle non-finite values.
Results may differ from the reference program's by a relative error of at most 0.0028.
Values sent between devices are 32-bit elements; how exact they have to be, the bound alone decides.
No kernel may reach another device: no remote copies, remote signals or barrier semaphores. Data moves between devices by JAX's collectives and lax.ppermute only.
A program may use at most 320 MiB of HBM per device.

```python
import math
import jax
import jax.numpy as jnp
from jax import lax

C = 512
BLOCKS = 8
HIDDEN_SIZE = 2048
MODES = 32
SMAX = 96
BLOCK = 64
ROWS = 73728
N_DP = 8


def item_layout(key):
    base = jax.random.fold_in(key, 4711)
    first, second, third = jax.random.split(base, 3)
    quarters = jax.random.randint(first, (N_DP,), 2, 5)
    chosen = jax.random.randint(third, (), 0, N_DP)
    hit = jnp.arange(N_DP, dtype=jnp.int32) == chosen
    quarters = jnp.where(hit, 4, quarters)
    side_vals = SMAX * quarters // 4
    lowest = jnp.maximum(side_vals // 4, 1)
    highest = jnp.minimum(side_vals // 2, MODES)
    raw = jax.random.randint(second, (N_DP,), 0, 1 << 20)
    mode_vals = lowest + raw % (highest - lowest + 1)
    mode_vals = jnp.where(hit, MODES, mode_vals)
    return (side_vals.astype(jnp.int32), mode_vals.astype(jnp.int32))


def draw_item_sides(key, part):
    return item_layout(key)[0]


def draw_item_modes(key, part):
    return item_layout(key)[1]


def block_levels(own_key, dims, cuts, low, largest):
    level, own = 1.0, jax.random.fold_in(own_key, 6)
    for dim, parts in cuts:
        draws = jnp.exp(jax.random.uniform(jax.random.fold_in(own, dim), (parts,), jnp.float32, low / len(cuts), largest / len(cuts)))
        level = level * jnp.repeat(draws, dims[dim] // parts).reshape([-1 if axis == dim else 1 for axis in range(len(dims))])
    return level


def noise(key, dims, scale, bound, cuts=(), kind=jnp.bfloat16):
    loudness = block_levels(key, dims, cuts, -0.22, 0.18) if cuts else 1.0
    entries = jax.random.normal(key, dims, jnp.float32) * scale * loudness
    return jnp.minimum(jnp.maximum(entries, -bound), bound).astype(kind)


def setup_inputs(seed: int = 0) -> dict:
    arg_keys = jax.random.split(jax.random.key(seed), 17)
    block_input = noise(arg_keys[0], (ROWS, C), 1.0, 6.0, ((0, 8), (1, 4)), jnp.float32)
    cotangent = noise(arg_keys[1], (ROWS, C), 1.0, 6.0, ((0, 8), (1, 4)), jnp.float32)
    item_sides = draw_item_sides(jax.random.fold_in(arg_keys[16], 71), 0)
    item_modes = draw_item_modes(jax.random.fold_in(arg_keys[16], 71), 0)
    ln1_gain = jnp.clip(1.0 + 0.18 * jax.random.normal(arg_keys[4], (C,), jnp.float32), 0.1, 1.9)
    ln1_bias = noise(arg_keys[5], (C,), 0.5, 3.0, ((0, 4),), jnp.float32)
    spec_w1 = noise(arg_keys[6], (2, BLOCKS, BLOCK, BLOCK), (2 * BLOCK) ** -0.5, 0.5, ((1, 4),), jnp.float32)
    spec_b1 = noise(arg_keys[7], (2, BLOCKS, BLOCK), 0.5, 3.0, ((1, 4),), jnp.float32)
    spec_w2 = noise(arg_keys[8], (2, BLOCKS, BLOCK, BLOCK), (2 * BLOCK) ** -0.5, 0.5, ((1, 4),), jnp.float32)
    spec_b2 = noise(arg_keys[9], (2, BLOCKS, BLOCK), 0.5, 3.0, ((1, 4),), jnp.float32)
    ln2_gain = jnp.clip(1.0 + 0.18 * jax.random.normal(arg_keys[10], (C,), jnp.float32), 0.1, 1.9)
    ln2_bias = noise(arg_keys[11], (C,), 0.5, 3.0, ((0, 4),), jnp.float32)
    mlp_w1 = noise(arg_keys[12], (C, HIDDEN_SIZE), C ** -0.5, 0.25, ((1, 4),), jnp.float32)
    mlp_b1 = noise(arg_keys[13], (HIDDEN_SIZE,), 0.5, 3.0, ((0, 4),), jnp.float32)
    mlp_w2 = noise(arg_keys[14], (HIDDEN_SIZE, C), HIDDEN_SIZE ** -0.5, 0.125, ((0, 4),), jnp.float32)
    mlp_b2 = noise(arg_keys[15], (C,), 0.5, 3.0, ((0, 4),), jnp.float32)
    return dict(block_input=block_input, cotangent=cotangent, item_sides=item_sides, item_modes=item_modes, ln1_gain=ln1_gain, ln1_bias=ln1_bias, spec_w1=spec_w1, spec_b1=spec_b1, spec_w2=spec_w2, spec_b2=spec_b2, ln2_gain=ln2_gain, ln2_bias=ln2_bias, mlp_w1=mlp_w1, mlp_b1=mlp_b1, mlp_w2=mlp_w2, mlp_b2=mlp_b2)


EPS = 1e-05
SHRINK = 0.01

@jax.custom_vjp
def low(v):
    return lax.optimization_barrier(v.astype(jnp.bfloat16)).astype(jnp.float32)

@jax.custom_vjp
def low_back(v):
    return v

def low_keep(v):
    return (low(v), None)

def low_pass(kept, grad):
    return (grad,)

def back_keep(v):
    return (v, None)

def back_low(kept, grad):
    return (low(grad),)
low.defvjp(low_keep, low_pass)
low_back.defvjp(back_keep, back_low)

def contract(form, left, right):
    return jnp.einsum(form, left, right, precision=lax.Precision.HIGHEST)

def tables(item_sides, item_modes):
    frequency = jnp.arange(2 * MODES - 1, dtype=jnp.int32) - (MODES - 1)
    cells = jnp.arange(SMAX, dtype=jnp.int32)
    extent = item_sides.astype(jnp.int32)[:, None, None]
    phase = frequency[None, :, None] * cells[None, None, :] % extent
    keep = (jnp.abs(frequency)[None, :, None] < item_modes.astype(jnp.int32)[:, None, None]) & (cells[None, None, :] < extent)
    length = extent.astype(jnp.float32)
    angle = 2.0 * math.pi * phase.astype(jnp.float32) / length
    scale = lax.rsqrt(length)
    cosine = jnp.where(keep, jnp.cos(angle) * scale, jnp.zeros_like(angle))
    sine = jnp.where(keep, -jnp.sin(angle) * scale, jnp.zeros_like(angle))
    return (cosine, sine)

def cell_mask(item_sides):
    cells = jnp.arange(SMAX, dtype=jnp.int32)
    extent = item_sides.astype(jnp.int32)[:, None, None]
    inside = (cells[None, :, None] < extent) & (cells[None, None, :] < extent)
    return inside.astype(jnp.float32)

def shrink(value):
    return jnp.where(value > SHRINK, value - SHRINK, jnp.where(value < -SHRINK, value + SHRINK, jnp.zeros_like(value)))

def gelu_exact(value):
    return jax.nn.gelu(value, approximate=False)

def complex_layer(real_in, imag_in, weight, bias):
    real_out = contract('...bc,bcd->...bd', real_in, weight[0]) - contract('...bc,bcd->...bd', imag_in, weight[1]) + bias[0]
    imag_out = contract('...bc,bcd->...bd', real_in, weight[1]) + contract('...bc,bcd->...bd', imag_in, weight[0]) + bias[1]
    return (real_out, imag_out)

def spectral(field, cosine, sine, first_w, first_b, second_w, second_b):
    real_a = contract('qjn,qnmc->qjmc', cosine, field)
    imag_a = contract('qjn,qnmc->qjmc', sine, field)
    real_x = contract('qkm,qjmc->qjkc', cosine, real_a) - contract('qkm,qjmc->qjkc', sine, imag_a)
    imag_x = contract('qkm,qjmc->qjkc', cosine, imag_a) + contract('qkm,qjmc->qjkc', sine, real_a)
    split = real_x.shape[:-1] + (first_w.shape[1], first_w.shape[2])
    real_h, imag_h = complex_layer(real_x.reshape(split), imag_x.reshape(split), first_w, first_b)
    real_h, imag_h = (gelu_exact(real_h), gelu_exact(imag_h))
    real_o, imag_o = complex_layer(real_h, imag_h, second_w, second_b)
    real_z = shrink(real_o).reshape(real_x.shape)
    imag_z = shrink(imag_o).reshape(real_x.shape)
    real_b = contract('qkm,qjkc->qjmc', cosine, real_z) + contract('qkm,qjkc->qjmc', sine, imag_z)
    imag_b = contract('qkm,qjkc->qjmc', cosine, imag_z) - contract('qkm,qjkc->qjmc', sine, real_z)
    return contract('qjn,qjmc->qnmc', cosine, real_b) + contract('qjn,qjmc->qnmc', sine, imag_b)

def layer_norm(value, gain, bias):
    center = lax.optimization_barrier(jnp.mean(value, axis=-1, keepdims=True))
    centered = value - center
    spread = lax.optimization_barrier(jnp.mean(centered * centered, axis=-1, keepdims=True))
    return centered * lax.rsqrt(spread + EPS) * gain + bias

def reference(block_input, cotangent, item_sides, item_modes, ln1_gain, ln1_bias, spec_w1, spec_b1, spec_w2, spec_b2, ln2_gain, ln2_bias, mlp_w1, mlp_b1, mlp_w2, mlp_b2):
    cosine, sine = tables(item_sides, item_modes)
    valid = cell_mask(item_sides).reshape(-1, 1)
    highest = lax.Precision.HIGHEST

    def forward(field_in, gain_one, bias_one, first_w, first_b, second_w, second_b, gain_two, bias_two, proj_in, bias_in, proj_out, bias_out):
        inputs = field_in * valid
        normed = layer_norm(inputs, gain_one, bias_one)
        field = normed.reshape(N_DP, SMAX, SMAX, C)
        mixed = spectral(field, cosine, sine, first_w, first_b, second_w, second_b).reshape(-1, C)
        middle = inputs + mixed + normed
        second = layer_norm(middle, gain_two, bias_two)
        hidden = gelu_exact(jnp.dot(second, proj_in, precision=highest) + bias_in)
        result = middle + jnp.dot(hidden, proj_out, precision=highest) + bias_out
        return result * valid
    block_output, pull = jax.vjp(forward, block_input, ln1_gain, ln1_bias, spec_w1, spec_b1, spec_w2, spec_b2, ln2_gain, ln2_bias, mlp_w1, mlp_b1, mlp_w2, mlp_b2)
    grads = pull(cotangent)
    return (block_output, grads[0], grads[1], grads[2], grads[3], grads[4], grads[5], grads[6], grads[7], grads[8], grads[9], grads[10], grads[11], grads[12])
```

```python
import functools
import math

import jax
import jax.numpy as jnp
from jax import lax
from jax.experimental import pallas as pl
from jax.experimental.pallas import tpu as pltpu
from jax.sharding import PartitionSpec as P

C = 512
MODES = 32
SMAX = 96
LANES = 128
FREQ = 64
PARTS = 4
CHUNKS = 3
SLABS = SMAX // (PARTS * CHUNKS)
PIECE = SLABS * SMAX
GROUP = PARTS * SLABS
STEPS = SMAX // SLABS
TILE = 256
HID = 512

EPS = 1e-05
SHRINK = 0.01
F32 = jnp.float32
BF16 = jnp.bfloat16
NN = (((1,), (0,)), ((), ()))
NT = (((1,), (1,)), ((), ()))
TN = (((0,), (0,)), ((), ()))
LIMIT = 56 * 1024 * 1024


def mm(left, right, dims=NN):
    return lax.dot_general(left, right, dims, preferred_element_type=F32)


def split2(value):
    high = value.astype(BF16)
    return high, (value - high.astype(F32)).astype(BF16)


def split3(value):
    high = value.astype(BF16)
    rest = value - high.astype(F32)
    mid = rest.astype(BF16)
    return high, mid, (rest - mid.astype(F32)).astype(BF16)


def left6(value):
    one, two, three = split3(value)
    return jnp.concatenate([one, one, two, one, two, three], axis=1)


def right6(value):
    one, two, three = split3(value)
    return jnp.concatenate([one, two, one, three, two, one], axis=0)


def left3(value):
    one, two = split2(value)
    return jnp.concatenate([one, one, two], axis=1)


def right3(value):
    one, two = split2(value)
    return jnp.concatenate([one, two, one], axis=0)


def phi_pair(value):
    cdf = 0.5 + 0.5 * lax.erf(value * math.sqrt(0.5))
    pdf = jnp.exp(value * value * -0.5) * (1.0 / math.sqrt(2.0 * math.pi))
    return cdf, pdf


def pad_rows(value):
    return jnp.concatenate([value, jnp.zeros((LANES - SMAX, value.shape[1]), F32)], axis=0)


def fold_rows(value):
    return jnp.sum(value.reshape(-1, 8, value.shape[-1]), axis=0)


def spread(row):
    return jnp.broadcast_to(row, (LANES, LANES)).T[:SMAX]


def call(body, out_shape, in_specs, out_specs, grid=(), scratch=(), aliases=None, cost=None):
    flops, moved = cost or (0, 0)
    return pl.pallas_call(
        body,
        out_shape=out_shape,
        grid=grid,
        in_specs=in_specs,
        out_specs=out_specs,
        scratch_shapes=list(scratch),
        input_output_aliases=aliases or {},
        compiler_params=pltpu.CompilerParams(vmem_limit_bytes=LIMIT),
        cost_estimate=pl.CostEstimate(flops=flops, bytes_accessed=moved, transcendentals=0),
    )


SMEM = pl.BlockSpec(memory_space=pltpu.SMEM)
VMEM = pl.BlockSpec(memory_space=pltpu.VMEM)
ANY = pl.BlockSpec(memory_space=pl.ANY)


def whole(shape):
    zeros = (0,) * len(shape)
    return pl.BlockSpec(shape, lambda *_: zeros)


def sds(shape, dtype=F32):
    return jax.ShapeDtypeStruct(shape, dtype)


def table(item_sides, item_modes):
    row = lax.broadcasted_iota(jnp.int32, (LANES, LANES), 0)
    cell = lax.broadcasted_iota(jnp.int32, (LANES, LANES), 1)
    index = row % FREQ
    frequency = index - (MODES - 1)
    extent = item_sides[0]
    phase = frequency * cell % extent
    keep = (jnp.abs(frequency) < item_modes[0]) & (cell < extent) & (index < 2 * MODES - 1)
    length = extent.astype(F32)
    angle = 2.0 * math.pi * phase.astype(F32) / length
    wave = jnp.where(row < FREQ, jnp.cos(angle), -jnp.sin(angle)) * lax.rsqrt(length)
    return jnp.where(keep, wave, jnp.zeros_like(wave))


def big_weight(weight, out):
    out[...] = jnp.zeros_like(out)
    for block in range(2):
        rows = pl.ds(block * 64, 64)
        later = pl.ds(128 + block * 64, 64)
        out[rows, rows] = weight[0, block]
        out[rows, later] = weight[1, block]
        out[later, rows] = -weight[1, block]
        out[later, later] = weight[0, block]


def prepare_body(f_ref, w1_ref, w2_ref, f6, g6, ft3, gt3, w1c, w2c, w1t, w2t, big):
    forward = f_ref[...]
    turned = jnp.concatenate([-forward[FREQ:], forward[:FREQ]], axis=0)
    f6[...] = left6(forward)
    g6[...] = left6(jnp.concatenate([forward, turned], axis=1))
    back = forward.T
    ft3[...] = left3(back)
    gt3[...] = left3(jnp.concatenate([back, turned.T], axis=0))
    for source, straight, across in ((w1_ref, w1c, w1t), (w2_ref, w2c, w2t)):
        big_weight(source, big)
        straight[...] = right6(big[...])
        across[...] = right3(big[...].T)


def prepare(forward, spec_w1, spec_w2):
    shapes = [
        sds((128, 768), BF16),
        sds((128, 1536), BF16),
        sds((128, 384), BF16),
        sds((256, 384), BF16),
        sds((1536, 256), BF16),
        sds((1536, 256), BF16),
        sds((768, 256), BF16),
        sds((768, 256), BF16),
    ]
    return call(
        prepare_body,
        shapes,
        [VMEM] * 3,
        [VMEM] * 8,
        scratch=[pltpu.VMEM((256, 256), F32)],
        cost=(10**6, 3 * 10**6),
    )(forward, spec_w1, spec_w2)


def slab_mask(first, side):
    cell = lax.broadcasted_iota(jnp.int32, (SMAX, LANES), 0)
    return (cell < side) & (first < side)


def moments_body(side_ref, x_ref, out_ref):
    step = pl.program_id(0)
    side = side_ref[0]
    for slab in range(SLABS):
        inside = slab_mask(step * SLABS + slab, side)
        value = pad_rows(jnp.where(inside, x_ref[slab], 0.0)).T
        mean = jnp.sum(value, axis=0, keepdims=True) * (1.0 / LANES)
        centered = value - mean
        out_ref[0, pl.ds(slab, 1), :] = mean
        out_ref[1, pl.ds(slab, 1), :] = jnp.sum(centered * centered, axis=0, keepdims=True)


def moments(side, x):
    return call(
        moments_body,
        sds((2, SMAX, LANES)),
        [SMEM, pl.BlockSpec((SLABS, SMAX, LANES), lambda i: (i, 0, 0))],
        pl.BlockSpec((2, SLABS, LANES), lambda i: (0, i, 0)),
        grid=(STEPS,),
        cost=(10**7, 5 * 10**6),
    )(side, x)


def cotangent_body(side_ref, own_ref, g_ref, *outs):
    side = side_ref[0]
    own = own_ref[0]
    total = outs[PARTS]
    total[...] = jnp.zeros_like(total)
    for chunk in range(CHUNKS):
        for part in range(PARTS):

            def one(slab, carry, chunk=chunk, part=part):
                first = chunk * GROUP + (own ^ part) * SLABS + slab
                value = jnp.where(slab_mask(first, side), g_ref[first], 0.0)
                outs[part][chunk, slab] = value
                return carry + fold_rows(value)

            total[...] += lax.fori_loop(0, SLABS, one, jnp.zeros((8, LANES), F32))


def cotangent_pieces(side, own, g):
    shapes = [sds((CHUNKS, SLABS, SMAX, LANES))] * PARTS + [sds((8, LANES))]
    return call(
        cotangent_body,
        shapes,
        [SMEM, SMEM, VMEM],
        [VMEM] * 5,
        cost=(10**7, 10**7),
    )(side, own, g)


def row_stats(stats):
    means = [stats[part, 0] for part in range(PARTS)]
    mean = (means[0] + means[1] + means[2] + means[3]) * (1.0 / PARTS)
    total = stats[0, 1] + stats[1, 1] + stats[2, 1] + stats[3, 1]
    for part in range(PARTS):
        gap = means[part] - mean
        total = total + LANES * (gap * gap)
    spread_ = total * (1.0 / C) + EPS
    inverse = lax.rsqrt(spread_)
    inverse = inverse * (1.5 - 0.5 * spread_ * inverse * inverse)
    return mean, inverse


def first_body(side_ref, x_ref, stats_ref, gain_ref, bias_ref, f6_ref, b_ref, xn_ref, xhat_ref, r_ref):
    step = pl.program_id(0)
    side = side_ref[0]
    mean, inverse = row_stats(stats_ref)
    r_ref[...] = inverse
    gain, bias = gain_ref[...], bias_ref[...]
    for pair in range(SLABS // 2):
        columns = []
        for slab in (2 * pair, 2 * pair + 1):
            value = jnp.where(slab_mask(step * SLABS + slab, side), x_ref[slab], 0.0)
            centered = value - spread(mean[slab : slab + 1])
            normal = centered * spread(inverse[slab : slab + 1])
            normed = normal * gain + bias
            xhat_ref[slab] = normal
            xn_ref[slab] = value + normed
            columns.append(pad_rows(normed))
        out = mm(f6_ref[...], right6(jnp.concatenate(columns, axis=1)))
        b_ref[2 * pair] = out[:, :LANES]
        b_ref[2 * pair + 1] = out[:, LANES:]


def first_stage(side, x, stats, gain, bias, f6):
    field = pl.BlockSpec((SLABS, SMAX, LANES), lambda i: (i, 0, 0))
    return call(
        first_body,
        [sds((SMAX, LANES, LANES)), sds((SMAX, SMAX, LANES)), sds((SMAX, SMAX, LANES)), sds((SMAX, LANES))],
        [
            SMEM,
            field,
            pl.BlockSpec((PARTS, 2, SLABS, LANES), lambda i: (0, 0, i, 0)),
            whole((1, LANES)),
            whole((1, LANES)),
            whole((128, 768)),
        ],
        [
            pl.BlockSpec((SLABS, LANES, LANES), lambda i: (i, 0, 0)),
            field,
            field,
            pl.BlockSpec((SLABS, LANES), lambda i: (i, 0)),
        ],
        grid=(STEPS,),
        cost=(2 * 10**9, 2 * 10**7),
    )(side, x, stats, gain, bias, f6)


def gather_columns(re_ref, im_ref, first):
    zeros = jnp.zeros((LANES - SMAX, LANES), F32)
    columns = []
    for j in range(first, first + 4):
        columns.append(jnp.concatenate([re_ref[:, j, :], zeros, im_ref[:, j, :], zeros], axis=0))
    return jnp.concatenate(columns, axis=1)


def to_rows(out):
    rows = []
    for j in range(4):
        lanes = slice(j * LANES, (j + 1) * LANES)
        rows.append(jnp.concatenate([out[:FREQ, lanes], out[FREQ:, lanes]], axis=1))
    return jnp.concatenate(rows, axis=0)


def to_columns(rows):
    columns = []
    for j in range(4):
        part = rows[j * FREQ : (j + 1) * FREQ]
        columns.append(jnp.concatenate([part[:, :LANES], part[:, LANES:]], axis=0))
    return jnp.concatenate(columns, axis=1)


def scatter_columns(re_ref, im_ref, first, out):
    for j in range(4):
        lanes = slice(j * LANES, (j + 1) * LANES)
        re_ref[:, first + j, :] = out[:SMAX, lanes]
        im_ref[:, first + j, :] = out[LANES : LANES + SMAX, lanes]


def shrink(value):
    return jnp.where(
        value > SHRINK,
        value - SHRINK,
        jnp.where(value < -SHRINK, value + SHRINK, jnp.zeros_like(value)),
    )


def mix_body(re_ref, im_ref, g6_ref, w1_ref, b1_ref, w2_ref, b2_ref, gt3_ref, bre, bim, a_out, p_out, o_out):
    for half in range(2):
        rows = pl.ds(half * TILE, TILE)
        spectrum = to_rows(mm(g6_ref[...], right6(gather_columns(re_ref, im_ref, 4 * half))))
        a_out[rows, :] = spectrum
        pre = mm(left6(spectrum), w1_ref[...]) + b1_ref[...]
        p_out[rows, :] = pre
        cdf = 0.5 + 0.5 * lax.erf(pre * math.sqrt(0.5))
        out = mm(left6(pre * cdf), w2_ref[...]) + b2_ref[...]
        o_out[rows, :] = out
        scatter_columns(bre, bim, 4 * half, mm(gt3_ref[...], right3(to_columns(shrink(out)))))


def mix_forward(b, g6, w1c, bias1, w2c, bias2, gt3):
    re = pl.BlockSpec((SMAX, 8, LANES), lambda j: (0, j, 0))
    im = pl.BlockSpec((SMAX, 8, LANES), lambda j: (0, 8 + j, 0))
    out = pl.BlockSpec((SMAX, 8, LANES), lambda j: (0, j, 0))
    rows = pl.BlockSpec((512, 256), lambda j: (j, 0))
    half = sds((SMAX, FREQ, LANES))
    return call(
        mix_body,
        [half, half] + [sds((4096, 256))] * 3,
        [
            re,
            im,
            whole((128, 1536)),
            whole((1536, 256)),
            whole((1, 256)),
            whole((1536, 256)),
            whole((1, 256)),
            whole((256, 384)),
        ],
        [out, out, rows, rows, rows],
        grid=(8,),
        cost=(10**10, 3 * 10**7),
    )(b, b, g6, w1c, bias1, w2c, bias2, gt3)


def last_body(own_ref, re_ref, im_ref, xn_ref, ft3_ref, *outs):
    own = own_ref[0]
    for part in range(PARTS):
        base = (own ^ part) * SLABS
        for pair in range(SLABS // 2):
            slabs = (base + 2 * pair, base + 2 * pair + 1)
            columns = [jnp.concatenate([re_ref[s], im_ref[s]], axis=0) for s in slabs]
            out = mm(ft3_ref[...], right3(jnp.concatenate(columns, axis=1)))[:SMAX]
            for index, s in enumerate(slabs):
                outs[part][2 * pair + index] = xn_ref[s] + out[:, index * LANES : (index + 1) * LANES]


def last_stage(own, bre, bim, xn, ft3, chunk):
    half = pl.BlockSpec((GROUP, FREQ, LANES), lambda i: (chunk, 0, 0))
    return call(
        last_body,
        [sds((SLABS, SMAX, LANES))] * PARTS,
        [SMEM, half, half, pl.BlockSpec((GROUP, SMAX, LANES), lambda i: (chunk, 0, 0)), whole((128, 384))],
        [whole((SLABS, SMAX, LANES))] * PARTS,
        grid=(1,),
        cost=(10**9, 5 * 10**6),
    )(own, bre, bim, xn, ft3)


def weights_body(w1_ref, w2_ref, w1h, w1l, w2h, w2l):
    w1h[...], w1l[...] = split2(w1_ref[...])
    w2h[...], w2l[...] = split2(w2_ref[...])


def split_weights(w1, w2):
    block = pl.BlockSpec((1, 512, 512), lambda i: (i, 0, 0))
    return call(
        weights_body,
        [sds((4, 512, 512), BF16)] * 4,
        [block] * 2,
        [block] * 4,
        grid=(4,),
        cost=(10**7, 16 * 10**6),
    )(w1, w2)


def feed_body(*refs):
    own_ref = refs[0]
    x_refs, g_refs = refs[1:5], refs[5:9]
    w1h, w1l, w2h, w2l, b1_ref, gain_ref, bias_ref = refs[9:16]
    refs = refs[16 + (len(refs) - 16 - 26) :]
    dx_refs, out_refs = refs[0:4], refs[4:8]
    hh, hl, ph, plo, nh, nl, gh, gl, db1, small = refs[8:18]
    n_h, n_l, g_h, g_l, xhat, scale, dn, acc = refs[18:26]
    step = pl.program_id(0)
    own = own_ref[0]
    last = pl.num_programs(0) - 1

    def lanes(part):
        return pl.ds(pl.multiple_of((own ^ part) * LANES, LANES), LANES)

    @pl.when(step == 0)
    def _():
        for part in range(PARTS):
            acc[:, lanes(part)] = g_refs[part][...]
            dn[:, lanes(part)] = x_refs[part][...]

        def norm(tile, carry):
            rows = pl.ds(tile * TILE, TILE)
            grad = acc[rows, :]
            high, low = split2(grad)
            g_h[rows, :] = high
            g_l[rows, :] = low
            gh[rows, :] = high
            gl[rows, :] = low
            value = dn[rows, :]
            centered = value - jnp.mean(value, axis=1, keepdims=True)
            spread_ = jnp.mean(centered * centered, axis=1, keepdims=True) + EPS
            inverse = lax.rsqrt(spread_)
            inverse = inverse * (1.5 - 0.5 * spread_ * inverse * inverse)
            normal = centered * inverse
            xhat[rows, :] = normal
            scale[rows, :] = jnp.broadcast_to(inverse, (TILE, LANES))
            high, low = split2(normal * gain_ref[...] + bias_ref[...])
            n_h[rows, :] = high
            n_l[rows, :] = low
            nh[rows, :] = high
            nl[rows, :] = low
            dn[rows, :] = jnp.zeros((TILE, C), F32)
            acc[rows, :] = jnp.zeros((TILE, C), F32)
            return carry

        lax.fori_loop(0, PIECE // TILE, norm, 0)

    def tile_step(tile, carry):
        rows = pl.ds(tile * TILE, TILE)
        a_h, a_l = n_h[rows, :], n_l[rows, :]
        pre = mm(a_h, w1h[0]) + mm(a_l, w1h[0]) + mm(a_h, w1l[0]) + b1_ref[0]
        c_h, c_l = g_h[rows, :], g_l[rows, :]
        dh = mm(c_h, w2h[0], NT) + mm(c_l, w2h[0], NT) + mm(c_h, w2l[0], NT)
        cdf, pdf = phi_pair(pre)
        high, low = split2(pre * cdf)
        hh[rows, :] = high
        hl[rows, :] = low
        acc[rows, :] += mm(high, w2h[0]) + mm(low, w2h[0]) + mm(high, w2l[0])
        grad = dh * (cdf + pre * pdf)
        high, low = split2(grad)
        ph[rows, :] = high
        plo[rows, :] = low
        dn[rows, :] += mm(high, w1h[0], NT) + mm(low, w1h[0], NT) + mm(high, w1l[0], NT)
        return carry + fold_rows(grad)

    db1[0] = lax.fori_loop(0, PIECE // TILE, tile_step, jnp.zeros((8, HID), F32))

    @pl.when(step == last)
    def _():
        small[...] = jnp.zeros_like(small)

        def back(tile, carry):
            rows = pl.ds(tile * TILE, TILE)
            grad = dn[rows, :]
            normal = xhat[rows, :]
            scaled = grad * gain_ref[...]
            first = jnp.mean(scaled, axis=1, keepdims=True)
            second = jnp.mean(scaled * normal, axis=1, keepdims=True)
            inverse = jnp.concatenate([scale[rows, :]] * 4, axis=1)
            top = g_h[rows, :].astype(F32) + g_l[rows, :].astype(F32)
            dn[rows, :] = inverse * (scaled - first - normal * second)
            small[0] += fold_rows(grad * normal)
            small[1] += fold_rows(grad)
            return carry

        lax.fori_loop(0, PIECE // TILE, back, 0)
        for part in range(PARTS):
            dx_refs[part][...] = g_refs[part][...] + dn[:, lanes(part)]
            out_refs[part][...] = acc[:, lanes(part)]


def feed(own, xs, gs, weights, b1, gain, bias, keep, chunk):
    piece = whole((PIECE, LANES))
    gpiece = pl.BlockSpec((PIECE, LANES), lambda i: (chunk, 0))
    weight = pl.BlockSpec((1, 512, 512), lambda i: (i, 0, 0))
    wide = pl.BlockSpec((PIECE, HID), lambda i: (chunk, i))
    narrow = pl.BlockSpec((PIECE, C), lambda i: (chunk, 0))
    rows = PIECE * CHUNKS
    shapes = [sds((PIECE, LANES))] * 8
    shapes += [sds((rows, 2048), BF16)] * 4 + [sds((rows, C), BF16)] * 4
    shapes += [sds((4, 8, HID)), sds((2, 8, C))]
    args = [own, *xs, *gs, *weights, b1, gain, bias]
    in_specs = [SMEM] + [piece] * 4 + [gpiece] * 4 + [weight] * 4
    in_specs += [pl.BlockSpec((1, 1, HID), lambda i: (i, 0, 0)), whole((1, C)), whole((1, C))]
    aliases = {}
    if keep is not None:
        for index, array in enumerate(keep):
            aliases[len(args)] = 8 + index
            args.append(array)
            in_specs.append(ANY)
    big = pltpu.VMEM((PIECE, C), F32)
    small = pltpu.VMEM((PIECE, C), BF16)
    return call(
        feed_body,
        shapes,
        in_specs,
        [piece] * 8
        + [wide] * 4
        + [narrow] * 4
        + [pl.BlockSpec((1, 8, HID), lambda i: (i, 0, 0)), whole((2, 8, C))],
        grid=(4,),
        scratch=[small] * 4 + [big, pltpu.VMEM((PIECE, LANES), F32), big, big],
        aliases=aliases,
        cost=(4 * 2 * 3 * PIECE * 512 * 2048, 40 * 10**6),
    )(*args)


def weight_body(hh, hl, ph, plo, nh, nl, gh, gl, *refs):
    b1s, smalls = refs[:CHUNKS], refs[CHUNKS : 2 * CHUNKS]
    out, n_h, n_l, g_h, g_l = refs[2 * CHUNKS :]
    step = pl.program_id(0)

    @pl.when(step == 0)
    def _():
        n_h[...] = nh[...].T
        n_l[...] = nl[...].T
        g_h[...] = gh[...].T
        g_l[...] = gl[...].T

    out[0, :C] = mm(n_h[...], ph[...]) + mm(n_l[...], ph[...]) + mm(n_h[...], plo[...])
    out[0, C : 2 * C] = mm(g_h[...], hh[...]) + mm(g_l[...], hh[...]) + mm(g_h[...], hl[...])
    first = b1s[0][0]
    norms = smalls[0][...]
    for chunk in range(1, CHUNKS):
        first = first + b1s[chunk][0]
        norms = norms + smalls[chunk][...]
    out[0, 2 * C : 2 * C + 8] = first
    tail = jnp.concatenate([norms[0], norms[1], jnp.zeros((8, 2 * LANES), F32)], axis=1)
    out[0, 2 * C + 8 :] = tail


def weight_grads(keep, b1s, smalls):
    rows = PIECE * CHUNKS
    wide = pl.BlockSpec((rows, HID), lambda i: (0, i))
    narrow = pl.BlockSpec((rows, C), lambda i: (0, 0), pipeline_mode=pl.Buffered(1))
    turned = pltpu.VMEM((C, rows), BF16)
    return call(
        weight_body,
        sds((4, 2 * C + 16, HID)),
        [wide] * 4
        + [narrow] * 4
        + [pl.BlockSpec((1, 8, HID), lambda i: (i, 0, 0))] * CHUNKS
        + [pl.BlockSpec((2, 8, LANES), lambda i: (0, 0, i))] * CHUNKS,
        pl.BlockSpec((1, 2 * C + 16, HID), lambda i: (i, 0, 0)),
        grid=(4,),
        scratch=[turned] * 4,
        cost=(2 * 2 * 3 * rows * 512 * 2048, 60 * 10**6),
    )(*keep, *b1s, *smalls)


def first_back_body(*refs):
    own_ref, pieces, f6_ref = refs[0], refs[1:5], refs[5]
    d_ref, dx_ref = refs[-2:]
    own = own_ref[0]
    table3 = f6_ref[...]
    for part in range(PARTS):
        base = (own ^ part) * SLABS
        for pair in range(SLABS // 2):
            slabs = (2 * pair, 2 * pair + 1)
            values = [pieces[part][s] for s in slabs]
            columns = jnp.concatenate([pad_rows(v) for v in values], axis=1)
            out = mm(table3, right3(columns))
            for index, s in enumerate(slabs):
                d_ref[base + s] = out[:, index * LANES : (index + 1) * LANES]
                dx_ref[base + s] = values[index]


def first_back(own, pieces, f6, keep, chunk):
    args = [own, *pieces, f6]
    in_specs = [SMEM] + [whole((SLABS, SMAX, LANES))] * 4 + [whole((128, 384))]
    aliases = {}
    if keep is not None:
        for index, array in enumerate(keep):
            aliases[len(args)] = index
            args.append(array)
            in_specs.append(ANY)
    return call(
        first_back_body,
        [sds((SMAX, LANES, LANES)), sds((SMAX, SMAX, LANES))],
        in_specs,
        [
            pl.BlockSpec((GROUP, LANES, LANES), lambda i: (chunk, 0, 0)),
            pl.BlockSpec((GROUP, SMAX, LANES), lambda i: (chunk, 0, 0)),
        ],
        grid=(1,),
        aliases=aliases,
        cost=(10**9, 5 * 10**6),
    )(*args)


def rows3(value):
    one, two = split2(value)
    return jnp.concatenate([one, one, two], axis=0)


def mix_back_body(re_ref, im_ref, a_ref, p_ref, o_ref, g3_ref, w1t, w2t, gt3_ref, dre, dim, dw1, dw2, db1, db2):
    @pl.when(pl.program_id(0) == 0)
    def _():
        for ref in (dw1, dw2, db1, db2):
            ref[...] = jnp.zeros_like(ref)

    for half in range(2):
        rows = pl.ds(half * TILE, TILE)
        dz = to_rows(mm(g3_ref[...], right3(gather_columns(re_ref, im_ref, 4 * half))))
        do = jnp.where(jnp.abs(o_ref[rows, :]) > SHRINK, dz, 0.0)
        pre = p_ref[rows, :]
        cdf, pdf = phi_pair(pre)
        dw2[...] += mm(rows3(pre * cdf), right3(do), TN)
        db2[...] += fold_rows(do)
        dp = mm(left3(do), w2t[...]) * (cdf + pre * pdf)
        dw1[...] += mm(rows3(a_ref[rows, :]), right3(dp), TN)
        db1[...] += fold_rows(dp)
        dx = mm(left3(dp), w1t[...])
        scatter_columns(dre, dim, 4 * half, mm(gt3_ref[...], right3(to_columns(dx))))


def mix_backward(d, a, p, o, g6, w1t, w2t, gt3):
    re = pl.BlockSpec((SMAX, 8, LANES), lambda j: (0, j, 0))
    im = pl.BlockSpec((SMAX, 8, LANES), lambda j: (0, 8 + j, 0))
    out = pl.BlockSpec((SMAX, 8, LANES), lambda j: (0, j, 0))
    rows = pl.BlockSpec((512, 256), lambda j: (j, 0))
    half = sds((SMAX, FREQ, LANES))
    return call(
        mix_back_body,
        [half, half, sds((256, 256)), sds((256, 256)), sds((8, 256)), sds((8, 256))],
        [
            re,
            im,
            rows,
            rows,
            rows,
            whole((128, 768)),
            whole((768, 256)),
            whole((768, 256)),
            whole((256, 384)),
        ],
        [out, out, whole((256, 256)), whole((256, 256)), whole((8, 256)), whole((8, 256))],
        grid=(8,),
        cost=(10**10, 3 * 10**7),
    )(d, d, a, p, o, g6, w1t, w2t, gt3)


def last_back_body(re_ref, im_ref, dx_ref, xhat_ref, gain_ref, ft3_ref, dn_ref, sums_ref, small):
    @pl.when(pl.program_id(0) == 0)
    def _():
        small[...] = jnp.zeros_like(small)

    gain = gain_ref[...]
    for pair in range(SLABS // 2):
        slabs = (2 * pair, 2 * pair + 1)
        columns = [jnp.concatenate([re_ref[s], im_ref[s]], axis=0) for s in slabs]
        out = mm(ft3_ref[...], right3(jnp.concatenate(columns, axis=1)))[:SMAX]
        for index, s in enumerate(slabs):
            grad = dx_ref[s] + out[:, index * LANES : (index + 1) * LANES]
            dn_ref[s] = grad
            normal = xhat_ref[s]
            product = grad * normal
            small[0] += fold_rows(product)
            small[1] += fold_rows(grad)
            sums_ref[0, pl.ds(s, 1), :] = jnp.sum(pad_rows(grad * gain).T, axis=0, keepdims=True)
            sums_ref[1, pl.ds(s, 1), :] = jnp.sum(pad_rows(product * gain).T, axis=0, keepdims=True)


def last_back(dre, dim, dx, xhat, gain, ft3):
    half = pl.BlockSpec((SLABS, FREQ, LANES), lambda i: (i, 0, 0))
    field = pl.BlockSpec((SLABS, SMAX, LANES), lambda i: (i, 0, 0))
    return call(
        last_back_body,
        [sds((SMAX, SMAX, LANES)), sds((2, SMAX, LANES)), sds((2, 8, LANES))],
        [half, half, field, field, whole((1, LANES)), whole((128, 384))],
        [field, pl.BlockSpec((2, SLABS, LANES), lambda i: (0, i, 0)), whole((2, 8, LANES))],
        grid=(STEPS,),
        cost=(2 * 10**9, 2 * 10**7),
    )(dre, dim, dx, xhat, gain, ft3)


def final_body(side_ref, dx_ref, dn_ref, xhat_ref, sums_ref, r_ref, gain_ref, out_ref):
    step = pl.program_id(0)
    side = side_ref[0]
    total = sums_ref[0] + sums_ref[1] + sums_ref[2] + sums_ref[3]
    inverse = r_ref[...]
    first = total[0] * (inverse * (1.0 / C))
    second = total[1] * (inverse * (1.0 / C))
    for slab in range(SLABS):
        row = slice(slab, slab + 1)
        normal = xhat_ref[slab]
        scaled = dn_ref[slab] * gain_ref[...]
        back = spread(inverse[row]) * scaled - spread(first[row]) - normal * spread(second[row])
        value = dx_ref[slab] + back
        out_ref[slab] = jnp.where(slab_mask(step * SLABS + slab, side), value, 0.0)


def final_stage(side, dx, dn, xhat, sums, r, gain):
    field = pl.BlockSpec((SLABS, SMAX, LANES), lambda i: (i, 0, 0))
    return call(
        final_body,
        sds((SMAX, SMAX, LANES)),
        [
            SMEM,
            field,
            field,
            field,
            pl.BlockSpec((PARTS, 2, SLABS, LANES), lambda i: (0, 0, i, 0)),
            pl.BlockSpec((SLABS, LANES), lambda i: (i, 0)),
            whole((1, LANES)),
        ],
        field,
        grid=(STEPS,),
        cost=(10**8, 2 * 10**7),
    )(side, dx, dn, xhat, sums, r, gain)


def make_output_body(chunk):
    def body(*refs):
        side_ref, own_ref = refs[:2]
        xs, outs, b2_ref, result = refs[2:6], refs[6:10], refs[10], refs[-1]
        side, own = side_ref[0], own_ref[0]
        for part in range(PARTS):
            base = (own ^ part) * SLABS
            for slab in range(SLABS):
                value = xs[part][slab] + outs[part][slab] + b2_ref[...]
                inside = slab_mask(chunk * GROUP + base + slab, side)
                result[base + slab] = jnp.where(inside, value, 0.0)

    return body


def output_stage(side, own, xs, outs, b2, keep, chunk):
    args = [side, own, *xs, *outs, b2]
    piece = whole((SLABS, SMAX, LANES))
    in_specs = [SMEM, SMEM] + [piece] * 8 + [whole((1, LANES))]
    aliases = {}
    if keep is not None:
        aliases[len(args)] = 0
        args.append(keep)
        in_specs.append(ANY)
    return call(
        make_output_body(chunk),
        sds((SMAX, SMAX, LANES)),
        in_specs,
        pl.BlockSpec((GROUP, SMAX, LANES), lambda i: (chunk, 0, 0)),
        grid=(1,),
        aliases=aliases,
        cost=(10**7, 6 * 10**6),
    )(*args)


def swap(value, axis, size, distance):
    return lax.ppermute(value, axis, [(i, i ^ distance) for i in range(size)])


def exchange(pieces):
    return [pieces[0]] + [swap(pieces[part], "blk", PARTS, part) for part in range(1, PARTS)]


def doubling_sum(value, size):
    distance = 1
    while distance < size:
        value = value + swap(value, "dp", size, distance)
        distance *= 2
    return value


def per_device(
    dp_size,
    block_input,
    cotangent,
    item_sides,
    item_modes,
    ln1_gain,
    ln1_bias,
    spec_w1,
    spec_b1,
    spec_w2,
    spec_b2,
    ln2_gain,
    ln2_bias,
    mlp_w1,
    mlp_b1,
    mlp_w2,
    mlp_b2,
):
    own = lax.axis_index("blk").astype(jnp.int32).reshape(1)
    cube = (SMAX, SMAX, LANES)
    x = block_input.reshape(cube)
    gain1, bias1 = ln1_gain.reshape(1, LANES), ln1_bias.reshape(1, LANES)

    stats = lax.all_gather(moments(item_sides, x), "blk", axis=0)
    *g_pieces, grad_b2 = cotangent_pieces(item_sides, own, cotangent.reshape(cube))
    gs = [piece.reshape(CHUNKS * PIECE, LANES) for piece in exchange(g_pieces)]
    vectors = lax.all_gather(jnp.concatenate([mlp_b1, ln2_gain, ln2_bias]), "blk", axis=0)
    b1_full = vectors[:, :HID].reshape(4, 1, HID)
    gain2 = vectors[:, HID : HID + LANES].reshape(1, C)
    bias2 = vectors[:, HID + LANES :].reshape(1, C)
    w1_full = lax.all_gather(mlp_w1, "blk", axis=0)
    w2_full = lax.all_gather(mlp_w2, "blk", axis=0)

    f6, g6, ft3, gt3, w1c, w2c, w1t, w2t = prepare(table(item_sides, item_modes), spec_w1, spec_w2)
    b, xn, xhat, r = first_stage(item_sides, x, stats, gain1, bias1, f6)
    bre, bim, a, p, o = mix_forward(
        b, g6, w1c, spec_b1.reshape(1, 256), w2c, spec_b2.reshape(1, 256), gt3
    )
    x1 = [last_stage(own, bre, bim, xn, ft3, chunk) for chunk in range(CHUNKS)]
    x1_in = [exchange(pieces) for pieces in x1]

    weights = split_weights(w1_full, w2_full)
    keep = None
    dx_in, out_in, b1s, smalls = [], [], [], []
    for chunk in range(CHUNKS):
        xs = [piece.reshape(PIECE, LANES) for piece in x1_in[chunk]]
        results = feed(own, xs, gs, weights, b1_full, gain2, bias2, keep, chunk)
        dx_in.append([v.reshape(SLABS, SMAX, LANES) for v in exchange(results[:4])])
        out_in.append(results[4:8])
        keep = results[8:16]
        b1s.append(results[16])
        smalls.append(results[17])
    out_in = [[v.reshape(SLABS, SMAX, LANES) for v in exchange(pieces)] for pieces in out_in]

    partial = weight_grads(keep, b1s, smalls)
    mine = lax.psum_scatter(partial, "blk", scatter_dimension=0, tiled=False)
    mine = lax.psum(mine, "dp")

    back = None
    for chunk in range(CHUNKS):
        back = first_back(own, dx_in[chunk], f6, back, chunk)
    d, dx = back
    dre, dim, dw1, dw2, db1, db2 = mix_backward(d, a, p, o, g6, w1t, w2t, gt3)
    dn, sums, small1 = last_back(dre, dim, dx, xhat, gain1, ft3)
    sums = lax.all_gather(sums, "blk", axis=0)
    input_grad = final_stage(item_sides, dx, dn, xhat, sums, r, gain1)

    block_output = None
    for chunk in range(CHUNKS):
        block_output = output_stage(
            item_sides, own, x1[chunk], out_in[chunk], mlp_b2.reshape(1, LANES), block_output, chunk
        )

    blocks = []
    for full in (dw1, dw2):
        for block in range(2):
            low, high = slice(block * 64, block * 64 + 64), slice(128 + block * 64, 192 + block * 64)
            blocks.append(full[low, low] + full[high, high])
            blocks.append(full[low, high] - full[high, low])
    packed = jnp.concatenate(
        [jnp.stack(blocks).reshape(-1), db1.sum(0), db2.sum(0), small1.sum(1).reshape(-1), grad_b2.sum(0)]
    )
    packed = doubling_sum(packed.reshape(-1, LANES), dp_size).reshape(-1)
    spec = packed[: 8 * 4096].reshape(2, 2, 2, 64, 64).transpose(0, 2, 1, 3, 4)
    rest = packed[8 * 4096 :]
    tail = mine[2 * C :]
    return (
        block_output.reshape(SMAX * SMAX, LANES),
        input_grad.reshape(SMAX * SMAX, LANES),
        rest[512:640],
        rest[640:768],
        spec[0],
        rest[:256].reshape(2, 2, 64),
        spec[1],
        rest[256:512].reshape(2, 2, 64),
        tail[8:, :LANES].sum(0),
        tail[8:, LANES : 2 * LANES].sum(0),
        mine[:C],
        tail[:8].sum(0),
        mine[C : 2 * C].T,
        rest[768:896],
    )


def solution(mesh):
    in_specs = (
        P("dp", "blk"),
        P("dp", "blk"),
        P("dp"),
        P("dp"),
        P("blk"),
        P("blk"),
        P(None, "blk", None, None),
        P(None, "blk", None),
        P(None, "blk", None, None),
        P(None, "blk", None),
        P("blk"),
        P("blk"),
        P(None, "blk"),
        P("blk"),
        P("blk", None),
        P("blk"),
    )
    out_specs = (
        P("dp", "blk"),
        P("dp", "blk"),
        P("blk"),
        P("blk"),
        P(None, "blk", None, None),
        P(None, "blk", None),
        P(None, "blk", None, None),
        P(None, "blk", None),
        P("blk"),
        P("blk"),
        P(None, "blk"),
        P("blk"),
        P("blk", None),
        P("blk"),
    )
    return jax.shard_map(
        functools.partial(per_device, mesh.shape["dp"]),
        mesh=mesh,
        in_specs=in_specs,
        out_specs=out_specs,
        check_vma=False,
    )
```

```python
import functools
import math

import jax
import jax.numpy as jnp
from jax import lax
from jax.experimental import pallas as pl
from jax.experimental.pallas import tpu as pltpu
from jax.sharding import PartitionSpec as P

C = 512
MODES = 32
SMAX = 96
LANES = 128
FREQ = 64
PARTS = 4
CHUNKS = 3
SLABS = SMAX // (PARTS * CHUNKS)
PIECE = SLABS * SMAX
GROUP = PARTS * SLABS
STEPS = SMAX // SLABS
STAGE = 24
THIRDS = STAGE // SLABS
WIDTH = 8
TILE = 256
SUB = 768
HID = 512
PACK = 4 * FREQ + 8

EPS = 1e-05
SHRINK = 0.01
F32 = jnp.float32
BF16 = jnp.bfloat16
NN = (((1,), (0,)), ((), ()))
NT = (((1,), (1,)), ((), ()))
TN = (((0,), (0,)), ((), ()))
LIMIT = 56 * 1024 * 1024


def mm(left, right, dims=NN):
    return lax.dot_general(left, right, dims, preferred_element_type=F32)


def split2(value):
    high = value.astype(BF16)
    return high, (value - high.astype(F32)).astype(BF16)


def split3(value):
    high = value.astype(BF16)
    rest = value - high.astype(F32)
    mid = rest.astype(BF16)
    return high, mid, (rest - mid.astype(F32)).astype(BF16)


def left6(value):
    one, two, three = split3(value)
    return jnp.concatenate([one, one, two, one, two, three], axis=1)


def right6(value):
    one, two, three = split3(value)
    return jnp.concatenate([one, two, one, three, two, one], axis=0)


def left3(value):
    one, two = split2(value)
    return jnp.concatenate([one, one, two], axis=1)


def right3(value):
    one, two = split2(value)
    return jnp.concatenate([one, two, one], axis=0)


def phi_pair(value):
    cdf = 0.5 + 0.5 * lax.erf(value * math.sqrt(0.5))
    pdf = jnp.exp(value * value * -0.5) * (1.0 / math.sqrt(2.0 * math.pi))
    return cdf, pdf


def pad_rows(value):
    return jnp.concatenate([value, jnp.zeros((LANES - SMAX, value.shape[1]), F32)], axis=0)


def fold_rows(value):
    return jnp.sum(value.reshape(-1, 8, value.shape[-1]), axis=0)


def spread8(rows):
    one, two, three = split3(rows)
    parts = [value.astype(F32) for value in (one, two, three)]
    left = jnp.concatenate(parts + [jnp.zeros_like(rows)], axis=0).astype(BF16)
    index = lax.broadcasted_iota(jnp.int32, (32, SLABS * LANES), 0)
    lane = lax.broadcasted_iota(jnp.int32, (32, SLABS * LANES), 1)
    pick = (index % SLABS == lane // LANES) & (index < 3 * SLABS)
    return mm(left, jnp.where(pick, 1.0, 0.0).astype(BF16), TN)


def slab_of(wide, slab):
    return wide[:SMAX, slab * LANES : (slab + 1) * LANES]


def us(time):
    return (int(time * 1e9), int(time * 3e6))


def call(body, out_shape, in_specs, out_specs, grid=(), scratch=(), aliases=None, cost=None):
    flops, moved = cost or (0, 0)
    return pl.pallas_call(
        body,
        out_shape=out_shape,
        grid=grid,
        in_specs=in_specs,
        out_specs=out_specs,
        scratch_shapes=list(scratch),
        input_output_aliases=aliases or {},
        compiler_params=pltpu.CompilerParams(vmem_limit_bytes=LIMIT),
        cost_estimate=pl.CostEstimate(flops=flops, bytes_accessed=moved, transcendentals=0),
    )


SMEM = pl.BlockSpec(memory_space=pltpu.SMEM)
VMEM = pl.BlockSpec(memory_space=pltpu.VMEM)
ANY = pl.BlockSpec(memory_space=pl.ANY)


def whole(shape):
    zeros = (0,) * len(shape)
    return pl.BlockSpec(shape, lambda *_: zeros)


def sds(shape, dtype=F32):
    return jax.ShapeDtypeStruct(shape, dtype)


def table(item_sides, item_modes):
    row = lax.broadcasted_iota(jnp.int32, (LANES, LANES), 0)
    cell = lax.broadcasted_iota(jnp.int32, (LANES, LANES), 1)
    index = row % FREQ
    frequency = index - (MODES - 1)
    extent = item_sides[0]
    phase = frequency * cell % extent
    keep = (jnp.abs(frequency) < item_modes[0]) & (cell < extent) & (index < 2 * MODES - 1)
    length = extent.astype(F32)
    angle = 2.0 * math.pi * phase.astype(F32) / length
    wave = jnp.where(row < FREQ, jnp.cos(angle), -jnp.sin(angle)) * lax.rsqrt(length)
    return jnp.where(keep, wave, jnp.zeros_like(wave))


def big_weight(weight, out):
    out[...] = jnp.zeros_like(out)
    for block in range(2):
        rows = pl.ds(block * 64, 64)
        later = pl.ds(128 + block * 64, 64)
        out[rows, rows] = weight[0, block]
        out[rows, later] = weight[1, block]
        out[later, rows] = -weight[1, block]
        out[later, later] = weight[0, block]


def prepare_body(f_ref, w1_ref, w2_ref, f6, g6, ft3, gt3, w1c, w2c, w1t, w2t, big):
    forward = f_ref[...]
    turned = jnp.concatenate([-forward[FREQ:], forward[:FREQ]], axis=0)
    f6[...] = left6(forward)
    g6[...] = left6(jnp.concatenate([forward, turned], axis=1))
    back = forward.T
    ft3[...] = left3(back)
    gt3[...] = left3(jnp.concatenate([back, turned.T], axis=0))
    for source, straight, across in ((w1_ref, w1c, w1t), (w2_ref, w2c, w2t)):
        big_weight(source, big)
        straight[...] = right6(big[...])
        across[...] = right3(big[...].T)


def prepare(forward, spec_w1, spec_w2):
    shapes = [
        sds((128, 768), BF16),
        sds((128, 1536), BF16),
        sds((128, 384), BF16),
        sds((256, 384), BF16),
        sds((1536, 256), BF16),
        sds((1536, 256), BF16),
        sds((768, 256), BF16),
        sds((768, 256), BF16),
    ]
    return call(
        prepare_body,
        shapes,
        [VMEM] * 3,
        [VMEM] * 8,
        scratch=[pltpu.VMEM((256, 256), F32)],
        cost=us(3),
    )(forward, spec_w1, spec_w2)


def slab_mask(first, side):
    cell = lax.broadcasted_iota(jnp.int32, (SMAX, LANES), 0)
    return (cell < side) & (first < side)


def moments_body(side_ref, x_ref, b1_ref, gain_ref, bias_ref, out_ref):
    step = pl.program_id(0)
    side = side_ref[0]

    @pl.when(step == 0)
    def _():
        vectors = [b1_ref[...], gain_ref[...], bias_ref[...], jnp.zeros((2, LANES), F32)]
        out_ref[2 * STEPS] = jnp.concatenate(vectors, axis=0)

    for slab in range(STAGE):
        inside = slab_mask(step * STAGE + slab, side)
        value = pad_rows(jnp.where(inside, x_ref[slab], 0.0)).T
        mean = jnp.sum(value, axis=0, keepdims=True) * (1.0 / LANES)
        centered = value - mean
        block, row = step * THIRDS + slab // SLABS, pl.ds(slab % SLABS, 1)
        out_ref[block, row, :] = mean
        out_ref[STEPS + block, row, :] = jnp.sum(centered * centered, axis=0, keepdims=True)


def moments(side, x, b1, gain, bias):
    return call(
        moments_body,
        sds((2 * STEPS + 1, SLABS, LANES)),
        [
            SMEM,
            pl.BlockSpec((STAGE, SMAX, LANES), lambda i: (i, 0, 0)),
            whole((4, LANES)),
            whole((1, LANES)),
            whole((1, LANES)),
        ],
        whole((2 * STEPS + 1, SLABS, LANES)),
        grid=(SMAX // STAGE,),
        cost=us(6),
    )(side, x, b1, gain, bias)


def cotangent_body(side_ref, g_ref, out_ref, total):
    chunk = pl.program_id(0)
    side = side_ref[0]

    @pl.when(chunk == 0)
    def _():
        total[...] = jnp.zeros_like(total)

    carry = jnp.zeros((8, LANES), F32)
    for part in range(PARTS):
        for slab in range(SLABS):
            first = part * SLABS + slab
            value = jnp.where(slab_mask(chunk * GROUP + first, side), g_ref[first], 0.0)
            out_ref[part, 0, slab] = value
            carry = carry + fold_rows(value)
    total[...] += carry


def cotangent_pieces(side, g):
    return call(
        cotangent_body,
        [sds((PARTS, CHUNKS, SLABS, SMAX, LANES)), sds((8, LANES))],
        [SMEM, pl.BlockSpec((GROUP, SMAX, LANES), lambda i: (i, 0, 0))],
        [
            pl.BlockSpec((PARTS, 1, SLABS, SMAX, LANES), lambda i: (0, i, 0, 0, 0)),
            whole((8, LANES)),
        ],
        grid=(CHUNKS,),
        cost=us(5),
    )(side, g)


def row_stats(means, totals):
    mean = (means[0] + means[1] + means[2] + means[3]) * (1.0 / PARTS)
    total = totals[0] + totals[1] + totals[2] + totals[3]
    for part in range(PARTS):
        gap = means[part] - mean
        total = total + LANES * (gap * gap)
    spread_ = total * (1.0 / C) + EPS
    inverse = lax.rsqrt(spread_)
    inverse = inverse * (1.5 - 0.5 * spread_ * inverse * inverse)
    return mean, inverse


def first_body(side_ref, x_ref, *refs):
    stats = refs[:PARTS]
    gain_ref, bias_ref, f6_ref, b_ref, xn_ref, xhat_ref, r_ref = refs[PARTS:]
    step = pl.program_id(0)
    side = side_ref[0]
    gain, bias = gain_ref[...], bias_ref[...]
    for third in range(THIRDS):
        block = step * THIRDS + third
        mean, inverse = row_stats([ref[block] for ref in stats], [ref[STEPS + block] for ref in stats])
        r_ref[pl.ds(third * SLABS, SLABS), :] = inverse
        means, scales = spread8(mean), spread8(inverse)
        for pair in range(SLABS // 2):
            columns = []
            for inner in (2 * pair, 2 * pair + 1):
                slab = third * SLABS + inner
                value = jnp.where(slab_mask(step * STAGE + slab, side), x_ref[slab], 0.0)
                centered = value - slab_of(means, inner)
                normal = centered * slab_of(scales, inner)
                normed = normal * gain + bias
                xhat_ref[slab] = normal
                xn_ref[slab] = value + normed
                columns.append(pad_rows(normed))
            out = mm(f6_ref[...], right6(jnp.concatenate(columns, axis=1)))
            b_ref[slab - 1] = out[:, :LANES]
            b_ref[slab] = out[:, LANES:]


def first_stage(side, x, stats, gain, bias, f6):
    field = pl.BlockSpec((STAGE, SMAX, LANES), lambda i: (i, 0, 0))
    return call(
        first_body,
        [sds((SMAX, LANES, LANES)), sds((SMAX, SMAX, LANES)), sds((SMAX, SMAX, LANES)), sds((SMAX, LANES))],
        [SMEM, field]
        + [whole((2 * STEPS + 1, SLABS, LANES))] * PARTS
        + [whole((1, LANES)), whole((1, LANES)), whole((128, 768))],
        [
            pl.BlockSpec((STAGE, LANES, LANES), lambda i: (i, 0, 0)),
            field,
            field,
            pl.BlockSpec((STAGE, LANES), lambda i: (i, 0)),
        ],
        grid=(SMAX // STAGE,),
        cost=us(3),
    )(side, x, *stats, gain, bias, f6)


def gather_columns(re_ref, im_ref, first):
    zeros = jnp.zeros((LANES - SMAX, LANES), F32)
    re, im = [ref.reshape(SMAX * WIDTH, LANES) for ref in (re_ref, im_ref)]
    columns = []
    for j in range(first, first + 4):
        rows = pl.ds(j, SMAX, stride=WIDTH)
        columns.append(jnp.concatenate([re[rows, :], zeros, im[rows, :], zeros], axis=0))
    return jnp.concatenate(columns, axis=1)


def to_rows(out):
    rows = []
    for j in range(4):
        lanes = slice(j * LANES, (j + 1) * LANES)
        rows.append(jnp.concatenate([out[:FREQ, lanes], out[FREQ:, lanes]], axis=1))
    return jnp.concatenate(rows, axis=0)


def to_columns(rows):
    columns = []
    for j in range(4):
        part = rows[j * FREQ : (j + 1) * FREQ]
        columns.append(jnp.concatenate([part[:, :LANES], part[:, LANES:]], axis=0))
    return jnp.concatenate(columns, axis=1)


def scatter_columns(re_ref, im_ref, first, out):
    re, im = [ref.reshape(SMAX * WIDTH, LANES) for ref in (re_ref, im_ref)]
    for j in range(4):
        lanes = slice(j * LANES, (j + 1) * LANES)
        rows = pl.ds(first + j, SMAX, stride=WIDTH)
        re[rows, :] = out[:SMAX, lanes]
        im[rows, :] = out[LANES : LANES + SMAX, lanes]


def shrink(value):
    return jnp.where(
        value > SHRINK,
        value - SHRINK,
        jnp.where(value < -SHRINK, value + SHRINK, jnp.zeros_like(value)),
    )


def mix_body(re_ref, im_ref, g6_ref, w1_ref, b1_ref, w2_ref, b2_ref, gt3_ref, bre, bim, a_out, p_out, o_out):
    for half in range(WIDTH // 4):
        rows = pl.ds(half * TILE, TILE)
        spectrum = to_rows(mm(g6_ref[...], right6(gather_columns(re_ref, im_ref, 4 * half))))
        a_out[rows, :] = spectrum
        pre = mm(left6(spectrum), w1_ref[...]) + b1_ref[...]
        p_out[rows, :] = pre
        cdf = 0.5 + 0.5 * lax.erf(pre * math.sqrt(0.5))
        out = mm(left6(pre * cdf), w2_ref[...]) + b2_ref[...]
        o_out[rows, :] = out
        scatter_columns(bre, bim, 4 * half, mm(gt3_ref[...], right3(to_columns(shrink(out)))))


def mix_forward(b, g6, w1c, bias1, w2c, bias2, gt3):
    count = FREQ // WIDTH
    re = pl.BlockSpec((SMAX, WIDTH, LANES), lambda j: (0, j, 0))
    im = pl.BlockSpec((SMAX, WIDTH, LANES), lambda j: (0, count + j, 0))
    out = pl.BlockSpec((SMAX, WIDTH, LANES), lambda j: (0, j, 0))
    rows = pl.BlockSpec((WIDTH * FREQ, 256), lambda j: (j, 0))
    half = sds((SMAX, FREQ, LANES))
    return call(
        mix_body,
        [half, half] + [sds((4096, 256))] * 3,
        [
            re,
            im,
            whole((128, 1536)),
            whole((1536, 256)),
            whole((1, 256)),
            whole((1536, 256)),
            whole((1, 256)),
            whole((256, 384)),
        ],
        [out, out, rows, rows, rows],
        grid=(count,),
        cost=us(4),
    )(b, b, g6, w1c, bias1, w2c, bias2, gt3)


def last_body(own_ref, re_ref, im_ref, xn_ref, ft3_ref, *refs):
    full = refs[-1]
    outs = refs[-1 - PARTS : -1] if len(refs) > PARTS else None
    tip = None if outs else refs[-2]
    own = own_ref[0]
    for part in range(PARTS):
        base = (own ^ part) * SLABS
        for pair in range(SLABS // 2):
            slabs = (base + 2 * pair, base + 2 * pair + 1)
            columns = [jnp.concatenate([re_ref[s], im_ref[s]], axis=0) for s in slabs]
            out = mm(ft3_ref[...], right3(jnp.concatenate(columns, axis=1)))[:SMAX]
            for index, s in enumerate(slabs):
                value = xn_ref[s] + out[:, index * LANES : (index + 1) * LANES]
                full[s] = value
                if outs:
                    outs[part][2 * pair + index] = value
                else:
                    tip[own ^ part, 2 * pair + index] = value


def last_stage(own, bre, bim, xn, ft3, keep, chunk):
    half = pl.BlockSpec((GROUP, FREQ, LANES), lambda i: (chunk, 0, 0))
    field = pl.BlockSpec((GROUP, SMAX, LANES), lambda i: (chunk, 0, 0))
    args = [own, bre, bim, xn, ft3]
    in_specs = [SMEM, half, half, field, whole((128, 384))]
    aliases = {}
    piece = (SLABS, SMAX, LANES)
    pieces = [piece] * PARTS if chunk < CHUNKS - 1 else [(PARTS,) + piece]
    if keep is not None:
        aliases[len(args)] = len(pieces)
        args.append(keep)
        in_specs.append(ANY)
    *pieces, full = call(
        last_body,
        [sds(shape) for shape in pieces] + [sds((SMAX, SMAX, LANES))],
        in_specs,
        [whole(shape) for shape in pieces] + [field],
        grid=(1,),
        aliases=aliases,
        cost=us(3.5),
    )(*args)
    return pieces, full


def weights_body(own_ref, *refs):
    step = pl.program_id(0)
    own = own_ref[0]
    one, two = refs[0:2], refs[2:4]
    far = refs[4:6]
    w1h, w1l, w2h, w2l = refs[6:]

    def emit(first, second):
        for part in range(PARTS):
            source = pl.ds(pl.multiple_of((own ^ part) * LANES, LANES), LANES)
            target = slice(part * LANES, (part + 1) * LANES)
            w1h[0, target, :], w1l[0, target, :] = split2(first(source))
            w2h[0, :, target], w2l[0, :, target] = split2(second(source))

    for index in range(2):

        @pl.when(step == index)
        def _(index=index):
            emit(lambda rows: one[index][rows, :], lambda lanes: two[index][:, lanes])

        @pl.when(step == 2 + index)
        def _(index=index):
            ref = far[index]
            depth = ref.shape[0] // PARTS

            def rows_of(rows):
                first = pl.multiple_of(rows.start // ref.shape[2], depth)
                return ref[pl.ds(first, depth), 0].reshape(LANES, 512)

            emit(rows_of, lambda lanes: ref[:, 1, :, lanes].reshape(512, LANES))


def split_weights(own, one, two, far):
    block = pl.BlockSpec((1, 512, 512), lambda i: (i, 0, 0))
    return call(
        weights_body,
        [sds((4, 512, 512), BF16)] * 4,
        [SMEM] + [whole((512, 512))] * 4 + [whole(far[0].shape)] * 2,
        [block] * 4,
        grid=(4,),
        cost=us(7),
    )(own, *one, *two, *far)


def row_mean(parts):
    total = parts[0] + parts[1] + parts[2] + parts[3]
    return jnp.sum(total, axis=1, keepdims=True) * (1.0 / C)


def part_lanes(part):
    return slice(part * LANES, (part + 1) * LANES)


def norm_tiles(load, vectors, n_h, n_l, nh, nl, xhat, scale):
    def norm(tile, carry):
        rows = pl.ds(tile * TILE, TILE)
        values = [load(part, rows) for part in range(PARTS)]
        mean = row_mean(values)
        centered = [value - mean for value in values]
        spread_ = row_mean([value * value for value in centered]) + EPS
        inverse = lax.rsqrt(spread_)
        inverse = inverse * (1.5 - 0.5 * spread_ * inverse * inverse)
        scale[rows, :] = jnp.broadcast_to(inverse, (TILE, LANES))
        for part in range(PARTS):
            lanes = part_lanes(part)
            normal = centered[part] * inverse
            xhat[rows, lanes] = normal
            gain, bias = vectors[part][0, 4:5, :], vectors[part][0, 5:6, :]
            high, low = split2(normal * gain + bias)
            n_h[rows, lanes] = high
            n_l[rows, lanes] = low
            nh[rows, lanes] = high
            nl[rows, lanes] = low
        return carry

    lax.fori_loop(0, PIECE // TILE, norm, 0)


def bias_of(vectors, step):
    row = jnp.zeros((4, LANES), F32)
    for part in range(PARTS):
        row = jnp.where(step == part, vectors[part][0, 0:4, :], row)
    return jnp.concatenate([row[i : i + 1] for i in range(4)], axis=1)


def grad_tiles(own, g_ref, vectors, dn, xhat, scale, store, small):
    small[...] = jnp.zeros_like(small)

    def back(tile, carry):
        rows = pl.ds(tile * TILE, TILE)
        inverse = scale[rows, :]
        scaled, normals = [], []
        for part in range(PARTS):
            lanes = part_lanes(part)
            grad = dn[rows, lanes]
            normal = xhat[rows, lanes]
            small[0, :, lanes] += fold_rows(grad * normal)
            small[1, :, lanes] += fold_rows(grad)
            scaled.append(grad * vectors[part][0, 4:5, :])
            normals.append(normal)
        first = row_mean(scaled)
        second = row_mean([s * n for s, n in zip(scaled, normals)])
        for part in range(PARTS):
            delta = inverse * (scaled[part] - first - normals[part] * second)
            store(part, rows, g_ref[own ^ part, rows, :] + delta)
        return carry

    lax.fori_loop(0, PIECE // TILE, back, 0)


def split_cotangent(own, g_ref, g_h, g_l):
    for part in range(PARTS):
        lanes = part_lanes(part)
        g_h[:, lanes], g_l[:, lanes] = split2(g_ref[own ^ part])


def product3(high, low, w_h, w_l, dims=NN):
    return mm(high, w_h[0], dims) + mm(low, w_h[0], dims) + mm(high, w_l[0], dims)


def add_to(ref, step, value):
    @pl.when(step == 0)
    def _():
        ref[...] = value

    @pl.when(step > 0)
    def _():
        ref[...] += value


def feed_body(*refs):
    own = refs[0][0]
    x_refs, g_ref = refs[1:5], refs[5]
    w1h, w1l, w2h, w2l = refs[6:10]
    vectors = refs[10:14]
    refs = refs[len(refs) - 21 :]
    hh, hl, nh, nl, out_ref, ph, plo = refs[0:7]
    dx_refs, db1, small = refs[7:11], refs[11], refs[12]
    n_h, n_l, g_h, g_l, xhat, scale, dn, acc = refs[13:21]
    step = pl.program_id(0)

    @pl.when(step == 0)
    def _():
        norm_tiles(lambda part, rows: x_refs[part][rows, :], vectors, n_h, n_l, nh, nl, xhat, scale)
        split_cotangent(own, g_ref, g_h, g_l)

    pre = product3(n_h[...], n_l[...], w1h, w1l) + bias_of(vectors, step)
    dh = product3(g_h[...], g_l[...], w2h, w2l, NT)
    cdf, pdf = phi_pair(pre)
    high, low = split2(pre * cdf)
    hh[...] = high
    hl[...] = low
    grad = dh * (cdf + pre * pdf)
    add_to(acc, step, product3(high, low, w2h, w2l))
    high, low = split2(grad)
    ph[...] = high
    plo[...] = low
    db1[0] = fold_rows(grad)
    add_to(dn, step, product3(high, low, w1h, w1l, NT))

    @pl.when(step == pl.num_programs(0) - 1)
    def _():
        for part in range(PARTS):
            out_ref[own ^ part, 0] = acc[:, part_lanes(part)]

        def store(part, rows, value):
            dx_refs[part][rows, :] = value

        grad_tiles(own, g_ref, vectors, dn, xhat, scale, store, small)


def forward_body(*refs):
    own = refs[0][0]
    x_ref = refs[1]
    w1h, w1l, w2h, w2l = refs[2:6]
    vectors = refs[6:10]
    hh, hl, nh, nl, out_ref, slope, xhat, scale, n_h, n_l, acc = refs[len(refs) - 11 :]
    step = pl.program_id(0)

    @pl.when(step == 0)
    def _():
        norm_tiles(lambda part, rows: x_ref[own ^ part, rows, :], vectors, n_h, n_l, nh, nl, xhat, scale)

    pre = product3(n_h[...], n_l[...], w1h, w1l) + bias_of(vectors, step)
    cdf, pdf = phi_pair(pre)
    slope[...] = cdf + pre * pdf
    high, low = split2(pre * cdf)
    hh[...] = high
    hl[...] = low
    add_to(acc, step, product3(high, low, w2h, w2l))

    @pl.when(step == pl.num_programs(0) - 1)
    def _():
        for part in range(PARTS):
            out_ref[own ^ part, 0] = acc[:, part_lanes(part)]


def backward_body(*refs):
    own = refs[0][0]
    g_ref, w1h, w1l, w2h, w2l, slope, xhat, scale = refs[1:9]
    vectors = refs[9:13]
    ph, plo, dx_ref, db1, small, g_h, g_l, dn = refs[len(refs) - 8 :]
    step = pl.program_id(0)

    @pl.when(step == 0)
    def _():
        split_cotangent(own, g_ref, g_h, g_l)

    grad = product3(g_h[...], g_l[...], w2h, w2l, NT) * slope[...]
    high, low = split2(grad)
    ph[...] = high
    plo[...] = low
    db1[0] = fold_rows(grad)
    add_to(dn, step, product3(high, low, w1h, w1l, NT))

    @pl.when(step == pl.num_programs(0) - 1)
    def _():

        def store(part, rows, value):
            dx_ref[own ^ part, rows, :] = value

        grad_tiles(own, g_ref, vectors, dn, xhat, scale, store, small)


def feed_call(body, head, heads, weights, stats, local, keep, kinds, chunk, cost):
    rows = PIECE * CHUNKS
    specs = {
        "x": (sds((PIECE, LANES)), whole((PIECE, LANES))),
        "g": (None, pl.BlockSpec((PARTS, PIECE, LANES), lambda i: (0, chunk, 0))),
        "out": (
            sds((PARTS, CHUNKS - 1, PIECE, LANES)),
            pl.BlockSpec((PARTS, 1, PIECE, LANES), lambda i: (0, chunk, 0, 0)),
        ),
        "last": (sds((PARTS, 1, PIECE, LANES)), whole((PARTS, 1, PIECE, LANES))),
        "wide": (sds((rows, 2048), BF16), pl.BlockSpec((PIECE, HID), lambda i: (chunk, i))),
        "narrow": (sds((rows, C), BF16), pl.BlockSpec((PIECE, C), lambda i: (chunk, 0))),
        "slope": (sds((PIECE, 2048)), pl.BlockSpec((PIECE, HID), lambda i: (0, i))),
        "four": (sds((PARTS, PIECE, LANES)), whole((PARTS, PIECE, LANES))),
        "full": (sds((PIECE, C)), whole((PIECE, C))),
        "db1": (sds((4, 8, HID)), pl.BlockSpec((1, 8, HID), lambda i: (i, 0, 0))),
        "small": (sds((2, 8, C)), whole((2, 8, C))),
    }
    weight = pl.BlockSpec((1, 512, 512), lambda i: (i, 0, 0))
    vector = pl.BlockSpec((1, SLABS, LANES), lambda i: (2 * STEPS, 0, 0))
    args = [*head, *weights, *(value for _, value in local), *stats]
    in_specs = [SMEM] + [specs[kind][1] for kind in heads] + [weight] * 4
    in_specs += [specs[kind][1] for kind, _ in local] + [vector] * 4
    aliases = {}
    for index, array in enumerate(keep or ()):
        aliases[len(args)] = index
        args.append(array)
        in_specs.append(ANY)
    bf, big = pltpu.VMEM((PIECE, C), BF16), pltpu.VMEM((PIECE, C), F32)
    scratch = {
        "feed": [bf] * 4 + [big, pltpu.VMEM((PIECE, LANES), F32), big, big],
        "fore": [bf, bf, big],
        "back": [bf, bf, big],
    }[kinds]
    outs = {
        "feed": ["wide"] * 2 + ["narrow"] * 2 + ["out", "wide", "wide"] + ["x"] * 4 + ["db1", "small"],
        "fore": ["wide"] * 2 + ["narrow"] * 2 + ["last", "slope", "full", "x"],
        "back": ["wide", "wide", "four", "db1", "small"],
    }[kinds]
    return call(
        body,
        [specs[kind][0] for kind in outs],
        in_specs,
        [specs[kind][1] for kind in outs],
        grid=(4,),
        scratch=scratch,
        aliases=aliases,
        cost=us(cost),
    )(*args)


def feed(own, xs, g, weights, stats, keep, chunk):
    head, heads = [own, *xs, g], ["x"] * 4 + ["g"]
    return feed_call(feed_body, head, heads, weights, stats, [], keep, "feed", chunk, 28)


def feed_forward(own, x, weights, stats, keep, chunk):
    return feed_call(forward_body, [own, x], ["four"], weights, stats, [], keep, "fore", chunk, 18)


def feed_backward(own, g, weights, local, stats, keep, chunk):
    local = list(zip(("slope", "full", "x"), local))
    return feed_call(backward_body, [own, g], ["g"], weights, stats, local, keep, "back", chunk, 1)


def weight_body(own_ref, place_ref, th, tl, *refs):
    send, held, t_h, t_l = refs[-4:]
    step = pl.program_id(0)
    own, place = own_ref[0], place_ref[0]

    @pl.when(step == 0)
    def _():
        if len(refs) == 6:
            t_h[...] = refs[0][...].T
            t_l[...] = refs[1][...].T
        else:
            for part in range(PARTS):
                high, low = split2(refs[0][own ^ part])
                t_h[part_lanes(part), :] = high.T
                t_l[part_lanes(part), :] = low.T

    out = mm(t_h[...], th[...]) + mm(t_l[...], th[...]) + mm(t_h[...], tl[...])
    count, depth = send.shape[1], send.shape[2]

    def store(ref):
        for index in range(count):
            part, inner = divmod(index, count // PARTS)
            apart = ((own ^ part) * (count // PARTS) + inner) ^ place
            where = (apart & 1) * (count // 2) + (apart >> 1)
            ref[0, where] = out[index * depth : (index + 1) * depth]

    @pl.when(step < 2)
    def _():
        store(send)

    @pl.when(step >= 2)
    def _():
        store(held)


def weight_grads(own, place, dp_size, left, th, tl):
    rows = PIECE * CHUNKS
    wide = pl.BlockSpec((rows, HID), lambda i: (0, (i % 2) * 2 + 1 - i // 2))
    block = (1, dp_size, C // dp_size, HID)
    shape = sds((2,) + block[1:])
    return call(
        weight_body,
        [shape, shape],
        [SMEM, SMEM]
        + [wide] * 2
        + [pl.BlockSpec(v.shape, lambda i, n=v.ndim: (0,) * n, pipeline_mode=pl.Buffered(1)) for v in left],
        [
            pl.BlockSpec(block, lambda i: (jnp.minimum(i, 1), 0, 0, 0)),
            pl.BlockSpec(block, lambda i: (jnp.maximum(i - 2, 0), 0, 0, 0)),
        ],
        grid=(4,),
        scratch=[pltpu.VMEM((C, rows), BF16)] * 2,
        cost=us(20),
    )(own, place, th, tl, *left)


def assemble_body(place_ref, near2, far2, near1, far1, w1_ref, w2_ref, turned):
    place = place_ref[0]
    half, depth = near1.shape[0], near1.shape[1]
    for side, (first, second) in enumerate(((near1, near2), (far1, far2))):
        for index in range(half):
            rows = pl.ds(pl.multiple_of((place ^ (2 * index + side)) * depth, depth), depth)
            w1_ref[rows, :] = first[index]
            turned[rows, :] = second[index]
    w2_ref[...] = turned[...].T


def assemble(place, near2, far2, near1, far1):
    return call(
        assemble_body,
        [sds((C, HID)), sds((HID, C))],
        [SMEM] + [VMEM] * 4,
        [VMEM] * 2,
        scratch=[pltpu.VMEM((C, HID), F32)],
        cost=us(3),
    )(place, near2, far2, near1, far1)


def first_back_body(*refs):
    own_ref, f6_ref, first = refs[:3]
    d_ref, dx_ref = refs[-2:]
    own = own_ref[0]
    pieces = refs[2 : 2 + PARTS] if len(first.shape) == 3 else None
    table3 = f6_ref[...]
    for part in range(PARTS):
        base = (own ^ part) * SLABS if pieces else part * SLABS
        for pair in range(SLABS // 2):
            slabs = (2 * pair, 2 * pair + 1)
            values = [pieces[part][s] if pieces else first[part, s] for s in slabs]
            columns = jnp.concatenate([pad_rows(v) for v in values], axis=1)
            out = mm(table3, right3(columns))
            for index, s in enumerate(slabs):
                d_ref[base + s] = out[:, index * LANES : (index + 1) * LANES]
                dx_ref[base + s] = values[index]


def first_back(own, pieces, f6, keep, chunk):
    args = [own, f6, *pieces]
    in_specs = [SMEM, whole((128, 384))] + [whole(piece.shape) for piece in pieces]
    aliases = {}
    if keep is not None:
        for index, array in enumerate(keep):
            aliases[len(args)] = index
            args.append(array)
            in_specs.append(ANY)
    return call(
        first_back_body,
        [sds((SMAX, LANES, LANES)), sds((SMAX, SMAX, LANES))],
        in_specs,
        [
            pl.BlockSpec((GROUP, LANES, LANES), lambda i: (chunk, 0, 0)),
            pl.BlockSpec((GROUP, SMAX, LANES), lambda i: (chunk, 0, 0)),
        ],
        grid=(1,),
        aliases=aliases,
        cost=us(4),
    )(*args)


def rows3(value):
    one, two = split2(value)
    return jnp.concatenate([one, one, two], axis=0)


def mix_back_body(*refs):
    re_ref, im_ref, a_ref, p_ref, o_ref, g3_ref, w1t, w2t, gt3_ref = refs[:9]
    sums = refs[-4:]
    dw1, dw2, db1, db2 = sums
    if len(refs) == 15:
        dre, dim = refs[9:11]
    else:
        gb_ref = refs[13]
        dre, dim, pack = refs[14:17]

    @pl.when(pl.program_id(0) == 0)
    def _():
        for index, ref in enumerate(sums):
            ref[...] = jnp.zeros_like(ref) if len(refs) == 15 else refs[9 + index][...]

    for half in range(WIDTH // 4):
        rows = pl.ds(half * TILE, TILE)
        dz = to_rows(mm(g3_ref[...], right3(gather_columns(re_ref, im_ref, 4 * half))))
        do = jnp.where(jnp.abs(o_ref[rows, :]) > SHRINK, dz, 0.0)
        pre = p_ref[rows, :]
        cdf, pdf = phi_pair(pre)
        dw2[...] += mm(rows3(pre * cdf), right3(do), TN)
        db2[...] += fold_rows(do)
        dp = mm(left3(do), w2t[...]) * (cdf + pre * pdf)
        dw1[...] += mm(rows3(a_ref[rows, :]), right3(dp), TN)
        db1[...] += fold_rows(dp)
        dx = mm(left3(dp), w1t[...])
        scatter_columns(dre, dim, 4 * half, mm(gt3_ref[...], right3(to_columns(dx))))

    if len(refs) == 15:
        return

    @pl.when(pl.program_id(0) == pl.num_programs(0) - 1)
    def _():
        low = lax.broadcasted_iota(jnp.int32, (FREQ, LANES), 1) < FREQ
        for index, ref in enumerate((dw1, dw2)):
            full = ref[...]
            same = full[:LANES, :LANES] + full[LANES:, LANES:]
            cross = full[:LANES, LANES:] - full[LANES:, :LANES]
            for inner, value in enumerate((same, cross)):
                rows = pl.ds((2 * index + inner) * FREQ, FREQ)
                pack[rows, :] = jnp.where(low, value[:FREQ], value[FREQ:])
        sums = [jnp.sum(ref[...], axis=0, keepdims=True) for ref in (db1, db2)]
        lines = [sums[0][:, :LANES], sums[0][:, LANES:], sums[1][:, :LANES], sums[1][:, LANES:]]
        lines.append(jnp.sum(gb_ref[...], axis=0, keepdims=True))
        pack[4 * FREQ : 4 * FREQ + 8] = jnp.concatenate(lines + [jnp.zeros((3, LANES), F32)], axis=0)


def mix_backward(d, a, p, o, g6, w1t, w2t, gt3, carry, grad_b2):
    count = FREQ // WIDTH
    skip = 0 if carry is None else count // 2
    re = pl.BlockSpec((SMAX, WIDTH, LANES), lambda j: (0, skip + j, 0))
    im = pl.BlockSpec((SMAX, WIDTH, LANES), lambda j: (0, count + skip + j, 0))
    out = pl.BlockSpec((SMAX, WIDTH, LANES), lambda j: (0, j, 0))
    rows = pl.BlockSpec((WIDTH * FREQ, 256), lambda j: (skip + j, 0))
    half = sds((SMAX, FREQ // 2, LANES))
    args = [d, d, a, p, o, g6, w1t, w2t, gt3]
    in_specs = [re, im, rows, rows, rows, whole((128, 768))]
    in_specs += [whole((768, 256)), whole((768, 256)), whole((256, 384))]
    sums = [(256, 256), (256, 256), (8, 256), (8, 256)]
    shapes, out_specs, scratch = [half, half], [out, out], []
    if carry is None:
        shapes += [sds(shape) for shape in sums]
        out_specs += [whole(shape) for shape in sums]
    else:
        args += [*carry, grad_b2]
        in_specs += [whole(shape) for shape in sums] + [whole((8, LANES))]
        shapes.append(sds((PACK, LANES)))
        out_specs.append(whole((PACK, LANES)))
        scratch = [pltpu.VMEM(shape, F32) for shape in sums]
    return call(
        mix_back_body, shapes, in_specs, out_specs, grid=(count // 2,), scratch=scratch, cost=us(13)
    )(*args)


def last_back_body(re0, re1, im0, im1, dx_ref, xhat_ref, gain_ref, ft3_ref, pack_ref, *refs):
    b1_refs, norm_refs = refs[:CHUNKS], refs[CHUNKS : 2 * CHUNKS]
    dn_ref, pack = refs[2 * CHUNKS : 2 * CHUNKS + 2]
    sums, small = refs[-1 - PARTS : -1], refs[-1]
    step = pl.program_id(0)

    @pl.when(step == 0)
    def _():
        small[...] = jnp.zeros_like(small)
        norms = norm_refs[0][...]
        for ref in norm_refs[1:]:
            norms = norms + ref[...]
        norms = [jnp.sum(norms[i], axis=0, keepdims=True) for i in range(2)]
        for part in range(PARTS):
            total = b1_refs[0][part]
            for ref in b1_refs[1:]:
                total = total + ref[part]
            total = jnp.sum(total, axis=0, keepdims=True)
            lines = [total[:, part_lanes(i)] for i in range(4)]
            lines += [value[:, part_lanes(part)] for value in norms]
            lines.append(jnp.zeros((2, LANES), F32))
            sums[part][2 * STEPS] = jnp.concatenate(lines, axis=0)

    gain = gain_ref[...]
    for pair in range(STAGE // 2):
        slabs = (2 * pair, 2 * pair + 1)
        columns = [jnp.concatenate([re0[s], re1[s], im0[s], im1[s]], axis=0) for s in slabs]
        out = mm(ft3_ref[...], right3(jnp.concatenate(columns, axis=1)))[:SMAX]
        for index, s in enumerate(slabs):
            grad = dx_ref[s] + out[:, index * LANES : (index + 1) * LANES]
            dn_ref[s] = grad
            product = grad * xhat_ref[s]
            small[0] += fold_rows(product)
            small[1] += fold_rows(grad)
            for which, value in enumerate((grad, product)):
                row = jnp.sum(pad_rows(value * gain).T, axis=0, keepdims=True)
                for ref in sums:
                    block = which * STEPS + step * THIRDS + s // SLABS
                    ref[block, pl.ds(s % SLABS, 1), :] = row

    @pl.when(step == pl.num_programs(0) - 1)
    def _():
        pack[...] = pack_ref[...]
        for index in range(2):
            where = pl.ds(4 * FREQ + 5 + index, 1)
            pack[where, :] = jnp.sum(small[index], axis=0, keepdims=True)


def last_back(quarters, dx, xhat, gain, ft3, pack, b1s, norms):
    half = pl.BlockSpec((STAGE, FREQ // 2, LANES), lambda i: (i, 0, 0))
    field = pl.BlockSpec((STAGE, SMAX, LANES), lambda i: (i, 0, 0))
    shape = (2 * STEPS + 1, SLABS, LANES)
    return call(
        last_back_body,
        [sds((SMAX, SMAX, LANES)), sds((PACK, LANES))] + [sds(shape)] * PARTS,
        [half] * 4
        + [field, field, whole((1, LANES)), whole((128, 384)), whole((PACK, LANES))]
        + [whole((4, 8, HID))] * CHUNKS
        + [whole((2, 8, C))] * CHUNKS,
        [field, whole((PACK, LANES))] + [whole(shape)] * PARTS,
        grid=(SMAX // STAGE,),
        scratch=[pltpu.VMEM((2, 8, LANES), F32)],
        cost=us(13),
    )(*quarters, dx, xhat, gain, ft3, pack, *b1s, *norms)


def final_body(side_ref, dx_ref, dn_ref, xhat_ref, r_ref, gain_ref, *refs):
    sums, out_ref = refs[:PARTS], refs[PARTS]
    step = pl.program_id(0)
    side = side_ref[0]
    for third in range(THIRDS):
        block = step * THIRDS + third
        inverse = r_ref[pl.ds(third * SLABS, SLABS), :]
        total = [sum(ref[which * STEPS + block] for ref in sums) for which in range(2)]
        first = total[0] * (inverse * (1.0 / C))
        second = total[1] * (inverse * (1.0 / C))
        wide = [spread8(value) for value in (inverse, first, second)]
        for inner in range(SLABS):
            slab = third * SLABS + inner
            scaled = dn_ref[slab] * gain_ref[...]
            scale, shift, slope = [slab_of(value, inner) for value in wide]
            value = dx_ref[slab] + (scale * scaled - shift - xhat_ref[slab] * slope)
            out_ref[slab] = jnp.where(slab_mask(step * STAGE + slab, side), value, 0.0)


def final_stage(side, dx, dn, xhat, sums, r, gain):
    field = pl.BlockSpec((STAGE, SMAX, LANES), lambda i: (i, 0, 0))
    return call(
        final_body,
        sds((SMAX, SMAX, LANES)),
        [SMEM, field, field, field, pl.BlockSpec((STAGE, LANES), lambda i: (i, 0)), whole((1, LANES))]
        + [whole((2 * STEPS + 1, SLABS, LANES))] * PARTS,
        field,
        grid=(SMAX // STAGE,),
        cost=us(13),
    )(side, dx, dn, xhat, r, gain, *sums)


def output_body(side_ref, x_ref, y_ref, tip_ref, b2_ref, out_ref):
    step = pl.program_id(0)
    side = side_ref[0]
    for part in range(PARTS):
        for inner in range(SLABS):
            slab = part * SLABS + inner
            branch = jnp.where(step < CHUNKS - 1, y_ref[part, 0, inner], tip_ref[part, inner])
            value = x_ref[slab] + branch + b2_ref[...]
            out_ref[slab] = jnp.where(slab_mask(step * GROUP + slab, side), value, 0.0)


def output_stage(side, x1, y, tip, b2):
    field = pl.BlockSpec((GROUP, SMAX, LANES), lambda i: (i, 0, 0))
    early = pl.BlockSpec(
        (PARTS, 1, SLABS, SMAX, LANES), lambda i: (0, jnp.minimum(i, CHUNKS - 2), 0, 0, 0)
    )
    return call(
        output_body,
        sds((SMAX, SMAX, LANES)),
        [SMEM, field, early, whole((PARTS, SLABS, SMAX, LANES)), whole((1, LANES))],
        field,
        grid=(CHUNKS,),
        cost=us(5),
    )(side, x1, y, tip, b2)


def swap(value, axis, size, distance):
    return lax.ppermute(value, axis, [(i, i ^ distance) for i in range(size)])


def exchange(pieces):
    return [pieces[0]] + [swap(pieces[part], "blk", PARTS, part) for part in range(1, PARTS)]


def after(value, *others):
    return lax.optimization_barrier((value, *others))[0]


def scatter_one(send, held, size):
    half = size // 2
    got = held + swap(send, "blk", PARTS, 1)
    gate = yield got
    mine = got[:, :half] + swap(after(got[:, half:], gate), "dp", size, 1)
    yield mine
    yield mine[0] + swap(mine[1], "blk", PARTS, 2)


def scatter_two(send, held, size):
    half, cut = size // 2, send.shape[2] // 2
    got = held + swap(send, "blk", PARTS, 1)
    yield got
    one = got[:, :half, :cut] + swap(got[:, half:, :cut], "dp", size, 1)
    two = got[0, :, cut:] + swap(got[1, :, cut:], "blk", PARTS, 2)
    yield one, two
    one = one[0] + swap(one[1], "blk", PARTS, 2)
    two = two[:half] + swap(two[half:], "dp", size, 1)
    yield one, two
    yield jnp.concatenate([one, two], axis=1)


def scatter_last(mine, size, gate):
    total = after(mine[0], gate)
    for index in range(1, size // 2):
        total = total + swap(mine[index], "dp", size, 2 * index)
    return total


def gather_near(piece, size, gate):
    return jnp.stack([after(piece, gate)] + [swap(piece, "dp", size, 2 * index) for index in range(1, size // 2)])


def per_device(
    dp_size,
    block_input,
    cotangent,
    item_sides,
    item_modes,
    ln1_gain,
    ln1_bias,
    spec_w1,
    spec_b1,
    spec_w2,
    spec_b2,
    ln2_gain,
    ln2_bias,
    mlp_w1,
    mlp_b1,
    mlp_w2,
    mlp_b2,
):
    own = lax.axis_index("blk").astype(jnp.int32).reshape(1)
    place = lax.axis_index("dp").astype(jnp.int32).reshape(1)
    cube = (SMAX, SMAX, LANES)
    x = block_input.reshape(cube)
    gain1, bias1 = ln1_gain.reshape(1, LANES), ln1_bias.reshape(1, LANES)

    depth = C // dp_size
    share = jnp.stack([lax.dynamic_slice_in_dim(w, place[0] * depth, depth) for w in (mlp_w1, mlp_w2)])
    share = swap(share, "blk", PARTS, 2)

    moment = moments(
        item_sides, x, mlp_b1.reshape(4, LANES), ln2_gain.reshape(1, LANES), ln2_bias.reshape(1, LANES)
    )
    stats = exchange([moment] * PARTS)
    f6, g6, ft3, gt3, w1c, w2c, w1t, w2t = prepare(table(item_sides, item_modes), spec_w1, spec_w2)
    g_parts, grad_b2 = cotangent_pieces(item_sides, after(cotangent.reshape(cube), f6, *stats[1:]))
    g = lax.all_to_all(g_parts, "blk", 0, 0).reshape(PARTS, CHUNKS * PIECE, LANES)
    far = lax.all_gather(after(share, moment), "dp", axis=0)
    mlp_w1, mlp_w2, _ = lax.optimization_barrier((mlp_w1, mlp_w2, stats[3]))
    one = [mlp_w1, swap(mlp_w1, "blk", PARTS, 1)]
    two = [mlp_w2, swap(mlp_w2, "blk", PARTS, 1)]

    b, xn, xhat, r = first_stage(item_sides, after(x, g_parts), stats, gain1, bias1, f6)
    bre, bim, a, p, o = mix_forward(
        b, g6, w1c, spec_b1.reshape(1, 256), w2c, spec_b2.reshape(1, 256), gt3
    )
    far = after(far, bre)
    far = [far, swap(far, "blk", PARTS, 1)]
    x1, x1_in = None, []
    for chunk in range(CHUNKS):
        field = after(xn, g, *x1_in[0]) if chunk == CHUNKS - 1 else xn
        pieces, x1 = last_stage(own, bre, bim, field, ft3, x1, chunk)
        if chunk < CHUNKS - 1:
            x1_in.append(exchange(pieces))
    x1_last = lax.all_to_all(pieces[0].reshape(PARTS, PIECE, LANES), "blk", 0, 0)

    weights = split_weights(own, one, two, far)
    keep, dx_in, b1s, norms = None, [], [], []

    def take(results):
        dx_in.append([v.reshape(SLABS, SMAX, LANES) for v in exchange(results[:4])])
        b1s.append(results[4])
        norms.append(results[5])

    xs = [[piece.reshape(PIECE, LANES) for piece in pieces] for pieces in x1_in]
    xs[0][0] = after(xs[0][0], x1)
    for chunk in range(CHUNKS - 1):
        results = feed(own, xs[chunk], g, weights, stats, keep, chunk)
        keep = results[:7]
        take(results[7:])
    branch = lax.all_to_all(keep[4], "blk", 0, 0)
    results = feed_forward(own, after(x1_last, *dx_in[0]), weights, stats, keep[:4], CHUNKS - 1)
    hh, hl, nh, nl = results[:4]
    tip = results[4]
    send2, held2 = weight_grads(own, place, dp_size, [g], hh, hl)
    chain2 = scatter_one(send2, held2, dp_size)
    local = list(results[5:])
    got2 = chain2.send(None)
    local[1] = after(local[1], held2)
    results = feed_backward(own, g, weights, local, stats, keep[5:], CHUNKS - 1)
    ph, plo, dx_last = results[:3]
    dx_in.append([lax.all_to_all(dx_last, "blk", 0, 0).reshape(PARTS, SLABS, SMAX, LANES)])
    b1s.append(results[3])
    norms.append(results[4])

    chain1 = scatter_two(*weight_grads(own, place, dp_size, [nh, nl], after(ph, got2, branch, *dx_in[1]), plo), dp_size)

    mine2 = chain2.send(ph)
    dx_in[0][0] = after(dx_in[0][0], mine2, *dx_in[2])
    back = first_back(own, dx_in[0], f6, None, 0)
    back = first_back(own, dx_in[1], f6, back, 1)
    dx_in[2][0] = after(dx_in[2][0], chain1.send(None))
    d, dx = first_back(own, dx_in[2], f6, back, 2)
    tip = lax.all_to_all(after(tip, d), "blk", 0, 0)
    mine2 = chain2.send(None)
    early = mix_backward(after(d, mine2), a, p, o, g6, w1t, w2t, gt3, None, None)
    second = scatter_last(after(mine2, d), dp_size, early[0])
    d_late = after(d, second, *chain1.send(None))
    late = mix_backward(d_late, a, p, o, g6, w1t, w2t, gt3, early[2:], grad_b2)
    near2 = gather_near(after(second, early[0]), dp_size, late[0])
    dx_last = after(dx, near2, tip, *chain1.send(None))
    quarters = [early[0], late[0], early[1], late[1]]
    dn, pack, *sums = last_back(quarters, dx_last, xhat, gain1, ft3, late[2], b1s, norms)
    first = scatter_last(chain1.send(None), dp_size, dn)
    sums = exchange([after(value, first) for value in sums])
    far2 = swap(after(near2, *sums[1:]), "dp", dp_size, 1)
    input_grad = final_stage(item_sides, dx, dn, xhat, sums, r, gain1)
    tail = sums[0][-1] + sums[1][-1] + sums[2][-1] + sums[3][-1]
    pack = jnp.concatenate([pack, tail], axis=0)
    near1 = gather_near(first, dp_size, input_grad)
    pack = after(pack, input_grad) + swap(pack, "dp", dp_size, 1)
    block_output = output_stage(
        item_sides,
        after(x1, input_grad, near1),
        branch.reshape(PARTS, CHUNKS - 1, SLABS, SMAX, LANES),
        tip.reshape(PARTS, SLABS, SMAX, LANES),
        mlp_b2.reshape(1, LANES),
    )
    distance = 2
    while distance < dp_size:
        pack = pack + swap(pack, "dp", dp_size, distance)
        distance *= 2
    far1 = swap(near1, "dp", dp_size, 1)
    w1_grad, w2_grad = assemble(place, near2, far2, near1, far1)

    spec = pack[: 4 * FREQ].reshape(2, 2, FREQ, 2, FREQ).transpose(0, 1, 3, 2, 4)
    rest = pack[4 * FREQ :]
    return (
        block_output.reshape(SMAX * SMAX, LANES),
        input_grad.reshape(SMAX * SMAX, LANES),
        rest[5],
        rest[6],
        spec[0],
        rest[0:2].reshape(2, 2, 64),
        spec[1],
        rest[2:4].reshape(2, 2, 64),
        rest[12],
        rest[13],
        w1_grad,
        rest[8:12].reshape(HID),
        w2_grad,
        rest[4],
    )


def solution(mesh):
    in_specs = (
        P("dp", "blk"),
        P("dp", "blk"),
        P("dp"),
        P("dp"),
        P("blk"),
        P("blk"),
        P(None, "blk", None, None),
        P(None, "blk", None),
        P(None, "blk", None, None),
        P(None, "blk", None),
        P("blk"),
        P("blk"),
        P(None, "blk"),
        P("blk"),
        P("blk", None),
        P("blk"),
    )
    out_specs = (
        P("dp", "blk"),
        P("dp", "blk"),
        P("blk"),
        P("blk"),
        P(None, "blk", None, None),
        P(None, "blk", None),
        P(None, "blk", None, None),
        P(None, "blk", None),
        P("blk"),
        P("blk"),
        P(None, "blk"),
        P("blk"),
        P("blk", None),
        P("blk"),
    )
    return jax.shard_map(
        functools.partial(per_device, mesh.shape["dp"]),
        mesh=mesh,
        in_specs=in_specs,
        out_specs=out_specs,
        check_vma=False,
    )
```

```python
import functools
import math

import jax
import jax.numpy as jnp
from jax import lax
from jax.experimental import pallas as pl
from jax.experimental.pallas import tpu as pltpu
from jax.sharding import PartitionSpec as P

C = 512
MODES = 32
SMAX = 96
LANES = 128
FREQ = 64
HALF = 32
PARTS = 4
CHUNKS = 3
SLABS = SMAX // (PARTS * CHUNKS)
PIECE = SLABS * SMAX
GROUP = PARTS * SLABS
STEPS = SMAX // SLABS
STAGE = 24
THIRDS = STAGE // SLABS
WIDTH = 8
BATCH = 4
TILE = 256
SUB = 768
HID = 512
PACK = 4 * FREQ + 8

EPS = 1e-05
SHRINK = 0.01
F32 = jnp.float32
BF16 = jnp.bfloat16
NN = (((1,), (0,)), ((), ()))
NT = (((1,), (1,)), ((), ()))
TN = (((0,), (0,)), ((), ()))
LIMIT = 56 * 1024 * 1024


def mm(left, right, dims=NN):
    return lax.dot_general(left, right, dims, preferred_element_type=F32)


def split2(value):
    high = value.astype(BF16)
    return high, (value - high.astype(F32)).astype(BF16)


def split3(value):
    high = value.astype(BF16)
    rest = value - high.astype(F32)
    mid = rest.astype(BF16)
    return high, mid, (rest - mid.astype(F32)).astype(BF16)


def left6(value):
    one, two, three = split3(value)
    return jnp.concatenate([one, one, two, one, two, three], axis=1)


def right6(value):
    one, two, three = split3(value)
    return jnp.concatenate([one, two, one, three, two, one], axis=0)


def left3(value):
    one, two = split2(value)
    return jnp.concatenate([one, one, two], axis=1)


def right3(value):
    one, two = split2(value)
    return jnp.concatenate([one, two, one], axis=0)


def phi_pair(value):
    cdf = 0.5 + 0.5 * lax.erf(value * math.sqrt(0.5))
    pdf = jnp.exp(value * value * -0.5) * (1.0 / math.sqrt(2.0 * math.pi))
    return cdf, pdf


def pad_rows(value):
    return jnp.concatenate([value, jnp.zeros((LANES - SMAX, value.shape[1]), F32)], axis=0)


def fold_rows(value):
    return jnp.sum(value.reshape(-1, 8, value.shape[-1]), axis=0)


def spread8(rows):
    one, two, three = split3(rows)
    parts = [value.astype(F32) for value in (one, two, three)]
    left = jnp.concatenate(parts + [jnp.zeros_like(rows)], axis=0).astype(BF16)
    index = lax.broadcasted_iota(jnp.int32, (32, SLABS * LANES), 0)
    lane = lax.broadcasted_iota(jnp.int32, (32, SLABS * LANES), 1)
    pick = (index % SLABS == lane // LANES) & (index < 3 * SLABS)
    return mm(left, jnp.where(pick, 1.0, 0.0).astype(BF16), TN)


def slab_of(wide, slab):
    return wide[:SMAX, slab * LANES : (slab + 1) * LANES]


def us(time):
    return (int(time * 1e9), int(time * 3e6))


def call(body, out_shape, in_specs, out_specs, grid=(), scratch=(), aliases=None, cost=None):
    flops, moved = cost or (0, 0)
    return pl.pallas_call(
        body,
        out_shape=out_shape,
        grid=grid,
        in_specs=in_specs,
        out_specs=out_specs,
        scratch_shapes=list(scratch),
        input_output_aliases=aliases or {},
        compiler_params=pltpu.CompilerParams(vmem_limit_bytes=LIMIT),
        cost_estimate=pl.CostEstimate(flops=flops, bytes_accessed=moved, transcendentals=0),
    )


SMEM = pl.BlockSpec(memory_space=pltpu.SMEM)
VMEM = pl.BlockSpec(memory_space=pltpu.VMEM)
ANY = pl.BlockSpec(memory_space=pl.ANY)


def whole(shape):
    zeros = (0,) * len(shape)
    return pl.BlockSpec(shape, lambda *_: zeros)


def sds(shape, dtype=F32):
    return jax.ShapeDtypeStruct(shape, dtype)


def table(item_sides, item_modes):
    row = lax.broadcasted_iota(jnp.int32, (LANES, LANES), 0)
    cell = lax.broadcasted_iota(jnp.int32, (LANES, LANES), 1)
    index = row % FREQ
    frequency = index - (MODES - 1)
    extent = item_sides[0]
    phase = frequency * cell % extent
    keep = (jnp.abs(frequency) < item_modes[0]) & (cell < extent) & (index < 2 * MODES - 1)
    length = extent.astype(F32)
    angle = 2.0 * math.pi * phase.astype(F32) / length
    wave = jnp.where(row < FREQ, jnp.cos(angle), -jnp.sin(angle)) * lax.rsqrt(length)
    return jnp.where(keep, wave, jnp.zeros_like(wave))


def big_weight(weight, out):
    out[...] = jnp.zeros_like(out)
    for block in range(2):
        rows = pl.ds(block * 64, 64)
        later = pl.ds(128 + block * 64, 64)
        out[rows, rows] = weight[0, block]
        out[rows, later] = weight[1, block]
        out[later, rows] = -weight[1, block]
        out[later, later] = weight[0, block]


def prepare_body(f_ref, w1_ref, w2_ref, f6, g6, ft3, gt3, w1c, w2c, w1t, w2t, big):
    full = f_ref[...]
    cosine, sine = full[:FREQ], full[FREQ:]
    half = jnp.concatenate([cosine[HALF - 1 : FREQ - 1], sine[HALF - 1 : FREQ - 1]], axis=0)
    f6[...] = left6(half)
    ft3[...] = left3(half.T)
    lines = [(cosine, -sine), (sine, cosine), (cosine, sine), (sine, -cosine)]
    table_ = jnp.concatenate([jnp.concatenate(line, axis=1) for line in lines], axis=0)
    g6[...] = left6(table_)
    gt3[...] = left3(table_.T)
    for source, straight, across in ((w1_ref, w1c, w1t), (w2_ref, w2c, w2t)):
        big_weight(source, big)
        straight[...] = right6(big[...])
        across[...] = right3(big[...].T)


def prepare(forward, spec_w1, spec_w2):
    shapes = [
        sds((64, 768), BF16),
        sds((256, 1536), BF16),
        sds((128, 192), BF16),
        sds((256, 768), BF16),
        sds((1536, 256), BF16),
        sds((1536, 256), BF16),
        sds((768, 256), BF16),
        sds((768, 256), BF16),
    ]
    return call(
        prepare_body,
        shapes,
        [VMEM] * 3,
        [VMEM] * 8,
        scratch=[pltpu.VMEM((256, 256), F32)],
        cost=us(3),
    )(forward, spec_w1, spec_w2)


def slab_mask(first, side):
    cell = lax.broadcasted_iota(jnp.int32, (SMAX, LANES), 0)
    return (cell < side) & (first < side)


def moments_body(side_ref, x_ref, b1_ref, gain_ref, bias_ref, out_ref):
    step = pl.program_id(0)
    side = side_ref[0]

    @pl.when(step == 0)
    def _():
        vectors = [b1_ref[...], gain_ref[...], bias_ref[...], jnp.zeros((2, LANES), F32)]
        out_ref[2 * STEPS] = jnp.concatenate(vectors, axis=0)

    for slab in range(STAGE):
        inside = slab_mask(step * STAGE + slab, side)
        value = pad_rows(jnp.where(inside, x_ref[slab], 0.0)).T
        mean = jnp.sum(value, axis=0, keepdims=True) * (1.0 / LANES)
        centered = value - mean
        block, row = step * THIRDS + slab // SLABS, pl.ds(slab % SLABS, 1)
        out_ref[block, row, :] = mean
        out_ref[STEPS + block, row, :] = jnp.sum(centered * centered, axis=0, keepdims=True)


def moments(side, x, b1, gain, bias):
    return call(
        moments_body,
        sds((2 * STEPS + 1, SLABS, LANES)),
        [
            SMEM,
            pl.BlockSpec((STAGE, SMAX, LANES), lambda i: (i, 0, 0)),
            whole((4, LANES)),
            whole((1, LANES)),
            whole((1, LANES)),
        ],
        whole((2 * STEPS + 1, SLABS, LANES)),
        grid=(SMAX // STAGE,),
        cost=us(6),
    )(side, x, b1, gain, bias)


def cotangent_body(side_ref, g_ref, out_ref, total):
    chunk = pl.program_id(0)
    side = side_ref[0]

    @pl.when(chunk == 0)
    def _():
        total[...] = jnp.zeros_like(total)

    carry = jnp.zeros((8, LANES), F32)
    for part in range(PARTS):
        for slab in range(SLABS):
            first = part * SLABS + slab
            value = jnp.where(slab_mask(chunk * GROUP + first, side), g_ref[first], 0.0)
            out_ref[part, 0, slab] = value
            carry = carry + fold_rows(value)
    total[...] += carry


def cotangent_pieces(side, g):
    return call(
        cotangent_body,
        [sds((PARTS, CHUNKS, SLABS, SMAX, LANES)), sds((8, LANES))],
        [SMEM, pl.BlockSpec((GROUP, SMAX, LANES), lambda i: (i, 0, 0))],
        [
            pl.BlockSpec((PARTS, 1, SLABS, SMAX, LANES), lambda i: (0, i, 0, 0, 0)),
            whole((8, LANES)),
        ],
        grid=(CHUNKS,),
        cost=us(5),
    )(side, g)


def row_stats(means, totals):
    mean = (means[0] + means[1] + means[2] + means[3]) * (1.0 / PARTS)
    total = totals[0] + totals[1] + totals[2] + totals[3]
    for part in range(PARTS):
        gap = means[part] - mean
        total = total + LANES * (gap * gap)
    spread_ = total * (1.0 / C) + EPS
    inverse = lax.rsqrt(spread_)
    inverse = inverse * (1.5 - 0.5 * spread_ * inverse * inverse)
    return mean, inverse


def first_body(side_ref, x_ref, *refs):
    stats = refs[:PARTS]
    gain_ref, bias_ref, f6_ref, b_ref, xn_ref, xhat_ref, r_ref = refs[PARTS:]
    step = pl.program_id(0)
    side = side_ref[0]
    gain, bias = gain_ref[...], bias_ref[...]
    for third in range(THIRDS):
        block = step * THIRDS + third
        mean, inverse = row_stats([ref[block] for ref in stats], [ref[STEPS + block] for ref in stats])
        r_ref[pl.ds(third * SLABS, SLABS), :] = inverse
        means, scales = spread8(mean), spread8(inverse)
        for pair in range(SLABS // 2):
            columns = []
            for inner in (2 * pair, 2 * pair + 1):
                slab = third * SLABS + inner
                value = jnp.where(slab_mask(step * STAGE + slab, side), x_ref[slab], 0.0)
                centered = value - slab_of(means, inner)
                normal = centered * slab_of(scales, inner)
                normed = normal * gain + bias
                xhat_ref[slab] = normal
                xn_ref[slab] = value + normed
                columns.append(pad_rows(normed))
            out = mm(f6_ref[...], right6(jnp.concatenate(columns, axis=1)))
            b_ref[slab - 1] = out[:, :LANES]
            b_ref[slab] = out[:, LANES:]


def first_stage(side, x, stats, gain, bias, f6):
    field = pl.BlockSpec((STAGE, SMAX, LANES), lambda i: (i, 0, 0))
    return call(
        first_body,
        [sds((SMAX, FREQ, LANES)), sds((SMAX, SMAX, LANES)), sds((SMAX, SMAX, LANES)), sds((SMAX, LANES))],
        [SMEM, field]
        + [whole((2 * STEPS + 1, SLABS, LANES))] * PARTS
        + [whole((1, LANES)), whole((1, LANES)), whole((64, 768))],
        [
            pl.BlockSpec((STAGE, FREQ, LANES), lambda i: (i, 0, 0)),
            field,
            field,
            pl.BlockSpec((STAGE, LANES), lambda i: (i, 0)),
        ],
        grid=(SMAX // STAGE,),
        cost=us(3),
    )(side, x, *stats, gain, bias, f6)


def gather_columns(re_ref, im_ref, first):
    zeros = jnp.zeros((LANES - SMAX, LANES), F32)
    re, im = [ref.reshape(SMAX * WIDTH, LANES) for ref in (re_ref, im_ref)]
    columns = []
    for j in range(first, first + BATCH):
        rows = pl.ds(j, SMAX, stride=WIDTH)
        columns.append(jnp.concatenate([re[rows, :], zeros, im[rows, :], zeros], axis=0))
    return jnp.concatenate(columns, axis=1)


def to_rows(out):
    rows = []
    for j in range(BATCH):
        lanes = part_lanes(j)
        for base in (0, 2 * FREQ):
            parts = [out[base : base + FREQ, lanes], out[base + FREQ : base + 2 * FREQ, lanes]]
            rows.append(jnp.concatenate(parts, axis=1))
    return jnp.concatenate(rows, axis=0)


def to_columns(rows):
    columns = []
    for j in range(BATCH):
        parts = []
        for sign in range(2):
            first = (2 * j + sign) * FREQ
            part = rows[first : first + FREQ]
            parts += [part[:, :LANES], part[:, LANES:]]
        columns.append(jnp.concatenate(parts, axis=0))
    return jnp.concatenate(columns, axis=1)


def counted(step, half, shape):
    row = lax.broadcasted_iota(jnp.int32, shape, 0)
    twice = (step == 0) & (half == 0)
    return (row < FREQ) | (row >= 2 * FREQ) | jnp.logical_not(twice)


def scatter_columns(re_ref, im_ref, first, out):
    re, im = [ref.reshape(SMAX * WIDTH, LANES) for ref in (re_ref, im_ref)]
    for j in range(BATCH):
        lanes = slice(j * LANES, (j + 1) * LANES)
        rows = pl.ds(first + j, SMAX, stride=WIDTH)
        re[rows, :] = out[:SMAX, lanes]
        im[rows, :] = out[LANES : LANES + SMAX, lanes]


def shrink(value):
    return jnp.where(
        value > SHRINK,
        value - SHRINK,
        jnp.where(value < -SHRINK, value + SHRINK, jnp.zeros_like(value)),
    )


def mix_body(re_ref, im_ref, g6_ref, w1_ref, b1_ref, w2_ref, b2_ref, gt3_ref, bre, bim, a_out, p_out, o_out):
    for half in range(WIDTH // BATCH):
        rows = pl.ds(half * 2 * BATCH * FREQ, 2 * BATCH * FREQ)
        spectrum = to_rows(mm(g6_ref[...], right6(gather_columns(re_ref, im_ref, BATCH * half))))
        a_out[rows, :] = spectrum
        pre = mm(left6(spectrum), w1_ref[...]) + b1_ref[...]
        p_out[rows, :] = pre
        cdf = 0.5 + 0.5 * lax.erf(pre * math.sqrt(0.5))
        out = mm(left6(pre * cdf), w2_ref[...]) + b2_ref[...]
        o_out[rows, :] = out
        if half == 0:
            out = jnp.where(counted(pl.program_id(0), half, out.shape), out, 0.0)
        scatter_columns(bre, bim, BATCH * half, mm(gt3_ref[...], right3(to_columns(shrink(out)))))


def mix_forward(b, g6, w1c, bias1, w2c, bias2, gt3):
    count = HALF // WIDTH
    re = pl.BlockSpec((SMAX, WIDTH, LANES), lambda j: (0, j, 0))
    im = pl.BlockSpec((SMAX, WIDTH, LANES), lambda j: (0, count + j, 0))
    out = pl.BlockSpec((SMAX, WIDTH, LANES), lambda j: (0, j, 0))
    rows = pl.BlockSpec((2 * WIDTH * FREQ, 256), lambda j: (j, 0))
    half = sds((SMAX, HALF, LANES))
    return call(
        mix_body,
        [half, half] + [sds((4096, 256))] * 3,
        [
            re,
            im,
            whole((256, 1536)),
            whole((1536, 256)),
            whole((1, 256)),
            whole((1536, 256)),
            whole((1, 256)),
            whole((256, 768)),
        ],
        [out, out, rows, rows, rows],
        grid=(count,),
        cost=us(4),
    )(b, b, g6, w1c, bias1, w2c, bias2, gt3)


def last_body(own_ref, re_ref, im_ref, xn_ref, ft3_ref, *refs):
    full, outs = refs[-1], refs[-1 - PARTS : -1]
    own = own_ref[0]
    for part in range(PARTS):
        base = (own ^ part) * SLABS
        for pair in range(SLABS // 2):
            slabs = (base + 2 * pair, base + 2 * pair + 1)
            columns = [jnp.concatenate([re_ref[s], im_ref[s]], axis=0) for s in slabs]
            out = mm(ft3_ref[...], right3(jnp.concatenate(columns, axis=1)))[:SMAX]
            for index, s in enumerate(slabs):
                value = xn_ref[s] + out[:, index * LANES : (index + 1) * LANES]
                full[s] = value
                if len(outs[part].shape) == 3:
                    outs[part][2 * pair + index] = value
                else:
                    outs[part][0, 2 * pair + index] = value


def last_stage(own, bre, bim, xn, ft3, keep, chunk):
    half = pl.BlockSpec((GROUP, HALF, LANES), lambda i: (chunk + i, 0, 0))
    field = pl.BlockSpec((GROUP, SMAX, LANES), lambda i: (chunk + i, 0, 0))
    args = [own, bre, bim, xn, ft3]
    in_specs = [SMEM, half, half, field, whole((128, 192))]
    aliases = {}
    steps = 1 if chunk == 0 else CHUNKS - 1
    if keep is not None:
        aliases[len(args)] = PARTS
        args.append(keep)
        in_specs.append(ANY)
    piece = (SLABS, SMAX, LANES)
    shape = piece if chunk == 0 else (steps,) + piece
    spec = whole(piece)
    if chunk > 0:
        spec = pl.BlockSpec((1,) + piece, lambda i: (i, 0, 0, 0))
    *pieces, full = call(
        last_body,
        [sds(shape)] * PARTS + [sds((SMAX, SMAX, LANES))],
        in_specs,
        [spec] * PARTS + [field],
        grid=(steps,),
        aliases=aliases,
        cost=us(4 * steps),
    )(*args)
    return pieces, full


def weights_body(own_ref, *refs):
    step = pl.program_id(0)
    own = own_ref[0]
    one, two = refs[0:2], refs[2:4]
    far = refs[4:6]
    w1h, w1l, w2h, w2l = refs[6:]

    def emit(first, second):
        for part in range(PARTS):
            source = pl.ds(pl.multiple_of((own ^ part) * LANES, LANES), LANES)
            target = slice(part * LANES, (part + 1) * LANES)
            w1h[0, target, :], w1l[0, target, :] = split2(first(source))
            w2h[0, :, target], w2l[0, :, target] = split2(second(source))

    for index in range(2):

        @pl.when(step == index)
        def _(index=index):
            emit(lambda rows: one[index][rows, :], lambda lanes: two[index][:, lanes])

        @pl.when(step == 2 + index)
        def _(index=index):
            ref = far[index]
            depth = ref.shape[0] // PARTS

            def rows_of(rows):
                first = pl.multiple_of(rows.start // ref.shape[2], depth)
                return ref[pl.ds(first, depth), 0].reshape(LANES, 512)

            emit(rows_of, lambda lanes: ref[:, 1, :, lanes].reshape(512, LANES))


def split_weights(own, one, two, far):
    block = pl.BlockSpec((1, 512, 512), lambda i: (i, 0, 0))
    return call(
        weights_body,
        [sds((4, 512, 512), BF16)] * 4,
        [SMEM] + [whole((512, 512))] * 4 + [whole(far[0].shape)] * 2,
        [block] * 4,
        grid=(4,),
        cost=us(7),
    )(own, *one, *two, *far)


def row_mean(parts):
    total = parts[0] + parts[1] + parts[2] + parts[3]
    return jnp.sum(total, axis=1, keepdims=True) * (1.0 / C)


def part_lanes(part):
    return slice(part * LANES, (part + 1) * LANES)


def norm_tiles(load, vectors, n_h, n_l, nh, nl, xhat, scale):
    def norm(tile, carry):
        rows = pl.ds(tile * TILE, TILE)
        values = [load(part, rows) for part in range(PARTS)]
        mean = row_mean(values)
        centered = [value - mean for value in values]
        spread_ = row_mean([value * value for value in centered]) + EPS
        inverse = lax.rsqrt(spread_)
        inverse = inverse * (1.5 - 0.5 * spread_ * inverse * inverse)
        scale[rows, :] = jnp.broadcast_to(inverse, (TILE, LANES))
        for part in range(PARTS):
            lanes = part_lanes(part)
            normal = centered[part] * inverse
            xhat[rows, lanes] = normal
            gain, bias = vectors[part][0, 4:5, :], vectors[part][0, 5:6, :]
            high, low = split2(normal * gain + bias)
            n_h[rows, lanes] = high
            n_l[rows, lanes] = low
            nh[rows, lanes] = high
            nl[rows, lanes] = low
        return carry

    lax.fori_loop(0, PIECE // TILE, norm, 0)


def bias_of(vectors, step):
    row = jnp.zeros((4, LANES), F32)
    for part in range(PARTS):
        row = jnp.where(step == part, vectors[part][0, 0:4, :], row)
    return jnp.concatenate([row[i : i + 1] for i in range(4)], axis=1)


def grad_tiles(own, g_ref, vectors, dn, xhat, scale, store, small):
    small[...] = jnp.zeros_like(small)

    def back(tile, carry):
        rows = pl.ds(tile * TILE, TILE)
        inverse = scale[rows, :]
        scaled, normals = [], []
        for part in range(PARTS):
            lanes = part_lanes(part)
            grad = dn[rows, lanes]
            normal = xhat[rows, lanes]
            small[0, :, lanes] += fold_rows(grad * normal)
            small[1, :, lanes] += fold_rows(grad)
            scaled.append(grad * vectors[part][0, 4:5, :])
            normals.append(normal)
        first = row_mean(scaled)
        second = row_mean([s * n for s, n in zip(scaled, normals)])
        for part in range(PARTS):
            delta = inverse * (scaled[part] - first - normals[part] * second)
            store(part, rows, g_ref[own ^ part, rows, :] + delta)
        return carry

    lax.fori_loop(0, PIECE // TILE, back, 0)


def split_cotangent(own, g_ref, g_h, g_l):
    for part in range(PARTS):
        lanes = part_lanes(part)
        g_h[:, lanes], g_l[:, lanes] = split2(g_ref[own ^ part])


def product3(high, low, w_h, w_l, dims=NN):
    return mm(high, w_h[0], dims) + mm(low, w_h[0], dims) + mm(high, w_l[0], dims)


def add_to(ref, step, value):
    @pl.when(step == 0)
    def _():
        ref[...] = value

    @pl.when(step > 0)
    def _():
        ref[...] += value


def feed_body(*refs):
    own = refs[0][0]
    x_refs, g_ref = refs[1:5], refs[5]
    w1h, w1l, w2h, w2l = refs[6:10]
    vectors = refs[10:14]
    refs = refs[len(refs) - 21 :]
    hh, hl, nh, nl, out_ref, ph, plo = refs[0:7]
    dx_refs, db1, small = refs[7:11], refs[11], refs[12]
    n_h, n_l, g_h, g_l, xhat, scale, dn, acc = refs[13:21]
    step = pl.program_id(0)

    @pl.when(step == 0)
    def _():
        norm_tiles(lambda part, rows: x_refs[part][rows, :], vectors, n_h, n_l, nh, nl, xhat, scale)
        split_cotangent(own, g_ref, g_h, g_l)

    pre = product3(n_h[...], n_l[...], w1h, w1l) + bias_of(vectors, step)
    dh = product3(g_h[...], g_l[...], w2h, w2l, NT)
    cdf, pdf = phi_pair(pre)
    high, low = split2(pre * cdf)
    hh[...] = high
    hl[...] = low
    grad = dh * (cdf + pre * pdf)
    add_to(acc, step, product3(high, low, w2h, w2l))
    high, low = split2(grad)
    ph[...] = high
    plo[...] = low
    db1[0] = fold_rows(grad)
    add_to(dn, step, product3(high, low, w1h, w1l, NT))

    @pl.when(step == pl.num_programs(0) - 1)
    def _():
        for part in range(PARTS):
            out_ref[own ^ part, 0] = acc[:, part_lanes(part)]

        def store(part, rows, value):
            dx_refs[part][rows, :] = value

        grad_tiles(own, g_ref, vectors, dn, xhat, scale, store, small)


def forward_body(*refs):
    own = refs[0][0]
    x_refs = refs[1:5]
    w1h, w1l, w2h, w2l = refs[5:9]
    vectors = refs[9:13]
    hh, hl, nh, nl, out_ref, slope, xhat, scale, n_h, n_l, acc = refs[len(refs) - 11 :]
    step = pl.program_id(0)

    @pl.when(step == 0)
    def _():
        norm_tiles(lambda part, rows: x_refs[part][rows, :], vectors, n_h, n_l, nh, nl, xhat, scale)

    pre = product3(n_h[...], n_l[...], w1h, w1l) + bias_of(vectors, step)
    cdf, pdf = phi_pair(pre)
    slope[...] = cdf + pre * pdf
    high, low = split2(pre * cdf)
    hh[...] = high
    hl[...] = low
    add_to(acc, step, product3(high, low, w2h, w2l))

    @pl.when(step == pl.num_programs(0) - 1)
    def _():
        for part in range(PARTS):
            out_ref[own ^ part, 0] = acc[:, part_lanes(part)]


def backward_body(*refs):
    own = refs[0][0]
    g_ref, w1h, w1l, w2h, w2l, slope, xhat, scale = refs[1:9]
    vectors = refs[9:13]
    ph, plo, dx_ref, db1, small, g_h, g_l, dn = refs[len(refs) - 8 :]
    step = pl.program_id(0)

    @pl.when(step == 0)
    def _():
        split_cotangent(own, g_ref, g_h, g_l)

    grad = product3(g_h[...], g_l[...], w2h, w2l, NT) * slope[...]
    high, low = split2(grad)
    ph[...] = high
    plo[...] = low
    db1[0] = fold_rows(grad)
    add_to(dn, step, product3(high, low, w1h, w1l, NT))

    @pl.when(step == pl.num_programs(0) - 1)
    def _():

        def store(part, rows, value):
            dx_ref[own ^ part, rows, :] = value

        grad_tiles(own, g_ref, vectors, dn, xhat, scale, store, small)


def feed_call(body, head, heads, weights, stats, local, keep, kinds, chunk, cost):
    rows = PIECE * CHUNKS
    specs = {
        "x": (sds((PIECE, LANES)), whole((PIECE, LANES))),
        "later": (None, pl.BlockSpec((PIECE, LANES), lambda i: (chunk - 1, 0))),
        "g": (None, pl.BlockSpec((PARTS, PIECE, LANES), lambda i: (0, chunk, 0))),
        "out": (
            sds((PARTS, CHUNKS, PIECE, LANES)),
            pl.BlockSpec((PARTS, 1, PIECE, LANES), lambda i: (0, chunk, 0, 0)),
        ),
        "wide": (sds((rows, 2048), BF16), pl.BlockSpec((PIECE, HID), lambda i: (chunk, i))),
        "narrow": (sds((rows, C), BF16), pl.BlockSpec((PIECE, C), lambda i: (chunk, 0))),
        "slope": (sds((PIECE, 2048)), pl.BlockSpec((PIECE, HID), lambda i: (0, i))),
        "four": (sds((PARTS, PIECE, LANES)), whole((PARTS, PIECE, LANES))),
        "full": (sds((PIECE, C)), whole((PIECE, C))),
        "db1": (sds((4, 8, HID)), pl.BlockSpec((1, 8, HID), lambda i: (i, 0, 0))),
        "small": (sds((2, 8, C)), whole((2, 8, C))),
    }
    weight = pl.BlockSpec((1, 512, 512), lambda i: (i, 0, 0))
    vector = pl.BlockSpec((1, SLABS, LANES), lambda i: (2 * STEPS, 0, 0))
    args = [*head, *weights, *(value for _, value in local), *stats]
    in_specs = [SMEM] + [specs[kind][1] for kind in heads] + [weight] * 4
    in_specs += [specs[kind][1] for kind, _ in local] + [vector] * 4
    aliases = {}
    for index, array in enumerate(keep or ()):
        aliases[len(args)] = index
        args.append(array)
        in_specs.append(ANY)
    bf, big = pltpu.VMEM((PIECE, C), BF16), pltpu.VMEM((PIECE, C), F32)
    scratch = {
        "feed": [bf] * 4 + [big, pltpu.VMEM((PIECE, LANES), F32), big, big],
        "fore": [bf, bf, big],
        "back": [bf, bf, big],
    }[kinds]
    outs = {
        "feed": ["wide"] * 2 + ["narrow"] * 2 + ["out", "wide", "wide"] + ["x"] * 4 + ["db1", "small"],
        "fore": ["wide"] * 2 + ["narrow"] * 2 + ["out", "slope", "full", "x"],
        "back": ["wide", "wide", "four", "db1", "small"],
    }[kinds]
    return call(
        body,
        [specs[kind][0] for kind in outs],
        in_specs,
        [specs[kind][1] for kind in outs],
        grid=(4,),
        scratch=scratch,
        aliases=aliases,
        cost=us(cost),
    )(*args)


def feed(own, xs, g, weights, stats, keep, chunk):
    head, heads = [own, *xs, g], ["x" if chunk == 0 else "later"] * 4 + ["g"]
    return feed_call(feed_body, head, heads, weights, stats, [], keep, "feed", chunk, 28)


def feed_forward(own, xs, weights, stats, keep, chunk):
    return feed_call(forward_body, [own, *xs], ["later"] * 4, weights, stats, [], keep, "fore", chunk, 18)


def feed_backward(own, g, weights, local, stats, keep, chunk):
    local = list(zip(("slope", "full", "x"), local))
    return feed_call(backward_body, [own, g], ["g"], weights, stats, local, keep, "back", chunk, 16)


def weight_body(own_ref, place_ref, th, tl, *refs):
    send, held, t_h, t_l = refs[-4:]
    step = pl.program_id(0)
    own, place = own_ref[0], place_ref[0]

    @pl.when(step == 0)
    def _():
        if len(refs) == 6:
            t_h[...] = refs[0][...].T
            t_l[...] = refs[1][...].T
        else:
            for part in range(PARTS):
                high, low = split2(refs[0][own ^ part])
                t_h[part_lanes(part), :] = high.T
                t_l[part_lanes(part), :] = low.T

    out = mm(t_h[...], th[...]) + mm(t_l[...], th[...]) + mm(t_h[...], tl[...])
    count, depth = send.shape[1], send.shape[2]

    def store(ref):
        for index in range(count):
            part, inner = divmod(index, count // PARTS)
            apart = ((own ^ part) * (count // PARTS) + inner) ^ place
            where = (apart & 1) * (count // 2) + (apart >> 1)
            ref[0, where] = out[index * depth : (index + 1) * depth]

    @pl.when(step < 2)
    def _():
        store(send)

    @pl.when(step >= 2)
    def _():
        store(held)


def weight_grads(own, place, dp_size, left, th, tl, cost):
    rows = PIECE * CHUNKS
    wide = pl.BlockSpec((rows, HID), lambda i: (0, (i % 2) * 2 + 1 - i // 2))
    block = (1, dp_size, C // dp_size, HID)
    shape = sds((2,) + block[1:])
    return call(
        weight_body,
        [shape, shape],
        [SMEM, SMEM]
        + [wide] * 2
        + [pl.BlockSpec(v.shape, lambda i, n=v.ndim: (0,) * n, pipeline_mode=pl.Buffered(1)) for v in left],
        [
            pl.BlockSpec(block, lambda i: (jnp.minimum(i, 1), 0, 0, 0)),
            pl.BlockSpec(block, lambda i: (jnp.maximum(i - 2, 0), 0, 0, 0)),
        ],
        grid=(4,),
        scratch=[pltpu.VMEM((C, rows), BF16)] * 2,
        cost=us(cost),
    )(own, place, th, tl, *left)


def assemble_body(place_ref, near2, far2, near1, far1, w1_ref, w2_ref, turned):
    place = place_ref[0]
    half, depth = near1.shape[0], near1.shape[1]
    for side, (first, second) in enumerate(((near1, near2), (far1, far2))):
        for index in range(half):
            rows = pl.ds(pl.multiple_of((place ^ (2 * index + side)) * depth, depth), depth)
            w1_ref[rows, :] = first[index]
            turned[rows, :] = second[index]
    w2_ref[...] = turned[...].T


def assemble(place, near2, far2, near1, far1):
    return call(
        assemble_body,
        [sds((C, HID)), sds((HID, C))],
        [SMEM] + [VMEM] * 4,
        [VMEM] * 2,
        scratch=[pltpu.VMEM((C, HID), F32)],
        cost=us(3),
    )(place, near2, far2, near1, far1)


def first_back_body(*refs):
    own_ref, f6_ref, last = refs[:3]
    d_ref, dx_ref = refs[-2:]
    own = own_ref[0]
    step = pl.program_id(0)

    def emit(load, base):
        for pair in range(SLABS // 2):
            slabs = (2 * pair, 2 * pair + 1)
            values = [load(s) for s in slabs]
            columns = jnp.concatenate([pad_rows(v) for v in values], axis=1)
            out = mm(f6_ref[...], right3(columns))
            for index, s in enumerate(slabs):
                d_ref[base + s] = out[:, index * LANES : (index + 1) * LANES]
                dx_ref[base + s] = values[index]

    for chunk in range(CHUNKS - 1):
        pieces = refs[3 + PARTS * chunk : 3 + PARTS * (chunk + 1)]

        @pl.when(step == chunk)
        def _(pieces=pieces):
            for part in range(PARTS):
                emit(lambda s, part=part: pieces[part][0, s], (own ^ part) * SLABS)

    @pl.when(step == CHUNKS - 1)
    def _():
        for part in range(PARTS):
            emit(lambda s, part=part: last[part, s], part * SLABS)


def first_back(own, early, last, f6):
    pieces = [piece for group in early for piece in group]
    return call(
        first_back_body,
        [sds((SMAX, FREQ, LANES)), sds((SMAX, SMAX, LANES))],
        [SMEM, whole((64, 384)), whole(last.shape)] + [whole(piece.shape) for piece in pieces],
        [
            pl.BlockSpec((GROUP, FREQ, LANES), lambda i: (i, 0, 0)),
            pl.BlockSpec((GROUP, SMAX, LANES), lambda i: (i, 0, 0)),
        ],
        grid=(CHUNKS,),
        cost=us(8),
    )(own, f6, last, *pieces)


def rows3(value):
    one, two = split2(value)
    return jnp.concatenate([one, one, two], axis=0)


def mix_back_body(*refs):
    re_ref, im_ref, a_ref, p_ref, o_ref, g3_ref, w1t, w2t, gt3_ref = refs[:9]
    sums = refs[-4:]
    dw1, dw2, db1, db2 = sums
    if len(refs) == 15:
        dre, dim = refs[9:11]
    else:
        gb_ref = refs[13]
        dre, dim, pack = refs[14:17]

    @pl.when(pl.program_id(0) == 0)
    def _():
        for index, ref in enumerate(sums):
            ref[...] = jnp.zeros_like(ref) if len(refs) == 15 else refs[9 + index][...]

    for half in range(WIDTH // BATCH):
        rows = pl.ds(half * 2 * BATCH * FREQ, 2 * BATCH * FREQ)
        dz = to_rows(mm(g3_ref[...], right3(gather_columns(re_ref, im_ref, BATCH * half))))
        do = jnp.where(jnp.abs(o_ref[rows, :]) > SHRINK, dz, 0.0)
        if half == 0 and len(refs) == 15:
            do = jnp.where(counted(pl.program_id(0), half, do.shape), do, 0.0)
        pre = p_ref[rows, :]
        cdf, pdf = phi_pair(pre)
        dw2[...] += mm(rows3(pre * cdf), right3(do), TN)
        db2[...] += fold_rows(do)
        dp = mm(left3(do), w2t[...]) * (cdf + pre * pdf)
        dw1[...] += mm(rows3(a_ref[rows, :]), right3(dp), TN)
        db1[...] += fold_rows(dp)
        dx = mm(left3(dp), w1t[...])
        if half == 0 and len(refs) == 15:
            dx = jnp.where(counted(pl.program_id(0), half, dx.shape), dx, 0.0)
        scatter_columns(dre, dim, BATCH * half, mm(gt3_ref[...], right3(to_columns(dx))))

    if len(refs) == 15:
        return

    @pl.when(pl.program_id(0) == pl.num_programs(0) - 1)
    def _():
        low = lax.broadcasted_iota(jnp.int32, (FREQ, LANES), 1) < FREQ
        for index, ref in enumerate((dw1, dw2)):
            full = ref[...]
            same = full[:LANES, :LANES] + full[LANES:, LANES:]
            cross = full[:LANES, LANES:] - full[LANES:, :LANES]
            for inner, value in enumerate((same, cross)):
                rows = pl.ds((2 * index + inner) * FREQ, FREQ)
                pack[rows, :] = jnp.where(low, value[:FREQ], value[FREQ:])
        sums = [jnp.sum(ref[...], axis=0, keepdims=True) for ref in (db1, db2)]
        lines = [sums[0][:, :LANES], sums[0][:, LANES:], sums[1][:, :LANES], sums[1][:, LANES:]]
        lines.append(jnp.sum(gb_ref[...], axis=0, keepdims=True))
        pack[4 * FREQ : 4 * FREQ + 8] = jnp.concatenate(lines + [jnp.zeros((3, LANES), F32)], axis=0)


def mix_backward(d, a, p, o, g6, w1t, w2t, gt3, carry, grad_b2):
    count = HALF // WIDTH
    skip = 0 if carry is None else count // 2
    re = pl.BlockSpec((SMAX, WIDTH, LANES), lambda j: (0, skip + j, 0))
    im = pl.BlockSpec((SMAX, WIDTH, LANES), lambda j: (0, count + skip + j, 0))
    out = pl.BlockSpec((SMAX, WIDTH, LANES), lambda j: (0, j, 0))
    rows = pl.BlockSpec((2 * WIDTH * FREQ, 256), lambda j: (skip + j, 0))
    half = sds((SMAX, HALF // 2, LANES))
    args = [d, d, a, p, o, g6, w1t, w2t, gt3]
    in_specs = [re, im, rows, rows, rows, whole((256, 768))]
    in_specs += [whole((768, 256)), whole((768, 256)), whole((256, 768))]
    sums = [(256, 256), (256, 256), (8, 256), (8, 256)]
    shapes, out_specs, scratch = [half, half], [out, out], []
    if carry is None:
        shapes += [sds(shape) for shape in sums]
        out_specs += [whole(shape) for shape in sums]
    else:
        args += [*carry, grad_b2]
        in_specs += [whole(shape) for shape in sums] + [whole((8, LANES))]
        shapes.append(sds((PACK, LANES)))
        out_specs.append(whole((PACK, LANES)))
        scratch = [pltpu.VMEM(shape, F32) for shape in sums]
    return call(
        mix_back_body, shapes, in_specs, out_specs, grid=(count // 2,), scratch=scratch, cost=us(13)
    )(*args)


def last_back_body(re0, re1, im0, im1, dx_ref, xhat_ref, gain_ref, ft3_ref, pack_ref, *refs):
    b1_refs, norm_refs = refs[:CHUNKS], refs[CHUNKS : 2 * CHUNKS]
    dn_ref, pack = refs[2 * CHUNKS : 2 * CHUNKS + 2]
    sums, small = refs[-1 - PARTS : -1], refs[-1]
    step = pl.program_id(0)

    @pl.when(step == 0)
    def _():
        small[...] = jnp.zeros_like(small)
        norms = norm_refs[0][...]
        for ref in norm_refs[1:]:
            norms = norms + ref[...]
        norms = [jnp.sum(norms[i], axis=0, keepdims=True) for i in range(2)]
        for part in range(PARTS):
            total = b1_refs[0][part]
            for ref in b1_refs[1:]:
                total = total + ref[part]
            total = jnp.sum(total, axis=0, keepdims=True)
            lines = [total[:, part_lanes(i)] for i in range(4)]
            lines += [value[:, part_lanes(part)] for value in norms]
            lines.append(jnp.zeros((2, LANES), F32))
            sums[part][2 * STEPS] = jnp.concatenate(lines, axis=0)

    gain = gain_ref[...]
    for pair in range(STAGE // 2):
        slabs = (2 * pair, 2 * pair + 1)
        columns = [jnp.concatenate([re0[s], re1[s], im0[s], im1[s]], axis=0) for s in slabs]
        out = mm(ft3_ref[...], right3(jnp.concatenate(columns, axis=1)))[:SMAX]
        for index, s in enumerate(slabs):
            grad = dx_ref[s] + out[:, index * LANES : (index + 1) * LANES]
            dn_ref[s] = grad
            product = grad * xhat_ref[s]
            small[0] += fold_rows(product)
            small[1] += fold_rows(grad)
            for which, value in enumerate((grad, product)):
                row = jnp.sum(pad_rows(value * gain).T, axis=0, keepdims=True)
                for ref in sums:
                    block = which * STEPS + step * THIRDS + s // SLABS
                    ref[block, pl.ds(s % SLABS, 1), :] = row

    @pl.when(step == pl.num_programs(0) - 1)
    def _():
        pack[...] = pack_ref[...]
        for index in range(2):
            where = pl.ds(4 * FREQ + 5 + index, 1)
            pack[where, :] = jnp.sum(small[index], axis=0, keepdims=True)


def last_back(quarters, dx, xhat, gain, ft3, pack, b1s, norms):
    half = pl.BlockSpec((STAGE, HALF // 2, LANES), lambda i: (i, 0, 0))
    field = pl.BlockSpec((STAGE, SMAX, LANES), lambda i: (i, 0, 0))
    shape = (2 * STEPS + 1, SLABS, LANES)
    return call(
        last_back_body,
        [sds((SMAX, SMAX, LANES)), sds((PACK, LANES))] + [sds(shape)] * PARTS,
        [half] * 4
        + [field, field, whole((1, LANES)), whole((128, 192)), whole((PACK, LANES))]
        + [whole((4, 8, HID))] * CHUNKS
        + [whole((2, 8, C))] * CHUNKS,
        [field, whole((PACK, LANES))] + [whole(shape)] * PARTS,
        grid=(SMAX // STAGE,),
        scratch=[pltpu.VMEM((2, 8, LANES), F32)],
        cost=us(13),
    )(*quarters, dx, xhat, gain, ft3, pack, *b1s, *norms)


def final_body(side_ref, dx_ref, dn_ref, xhat_ref, r_ref, gain_ref, *refs):
    sums, out_ref = refs[:PARTS], refs[PARTS]
    step = pl.program_id(0)
    side = side_ref[0]
    for third in range(THIRDS):
        block = step * THIRDS + third
        inverse = r_ref[pl.ds(third * SLABS, SLABS), :]
        total = [sum(ref[which * STEPS + block] for ref in sums) for which in range(2)]
        first = total[0] * (inverse * (1.0 / C))
        second = total[1] * (inverse * (1.0 / C))
        wide = [spread8(value) for value in (inverse, first, second)]
        for inner in range(SLABS):
            slab = third * SLABS + inner
            scaled = dn_ref[slab] * gain_ref[...]
            scale, shift, slope = [slab_of(value, inner) for value in wide]
            value = dx_ref[slab] + (scale * scaled - shift - xhat_ref[slab] * slope)
            out_ref[slab] = jnp.where(slab_mask(step * STAGE + slab, side), value, 0.0)


def final_stage(side, dx, dn, xhat, sums, r, gain):
    field = pl.BlockSpec((STAGE, SMAX, LANES), lambda i: (i, 0, 0))
    return call(
        final_body,
        sds((SMAX, SMAX, LANES)),
        [SMEM, field, field, field, pl.BlockSpec((STAGE, LANES), lambda i: (i, 0)), whole((1, LANES))]
        + [whole((2 * STEPS + 1, SLABS, LANES))] * PARTS,
        field,
        grid=(SMAX // STAGE,),
        cost=us(13),
    )(side, dx, dn, xhat, r, gain, *sums)


def output_body(side_ref, x_ref, y_ref, b2_ref, out_ref):
    step = pl.program_id(0)
    side = side_ref[0]
    for part in range(PARTS):
        for inner in range(SLABS):
            slab = part * SLABS + inner
            value = x_ref[slab] + y_ref[part, 0, inner] + b2_ref[...]
            out_ref[slab] = jnp.where(slab_mask(step * GROUP + slab, side), value, 0.0)


def output_stage(side, x1, y, b2):
    field = pl.BlockSpec((GROUP, SMAX, LANES), lambda i: (i, 0, 0))
    return call(
        output_body,
        sds((SMAX, SMAX, LANES)),
        [
            SMEM,
            field,
            pl.BlockSpec((PARTS, 1, SLABS, SMAX, LANES), lambda i: (0, i, 0, 0, 0)),
            whole((1, LANES)),
        ],
        field,
        grid=(CHUNKS,),
        cost=us(5),
    )(side, x1, y, b2)


def swap(value, axis, size, distance):
    return lax.ppermute(value, axis, [(i, i ^ distance) for i in range(size)])


def exchange(pieces):
    return [pieces[0]] + [swap(pieces[part], "blk", PARTS, part) for part in range(1, PARTS)]


def after(value, *others):
    return lax.optimization_barrier((value, *others))[0]


def halve(value, size, distance, gate):
    cut = value.shape[0] // 2
    return after(value[:cut], gate) + swap(value[cut:], "dp", size, distance)


def scatter_last(mine, size, gate):
    total = after(mine[0], gate)
    for index in range(1, size // 2):
        total = total + swap(mine[index], "dp", size, 2 * index)
    return total


def gather_near(piece, size, gate):
    return jnp.stack([after(piece, gate)] + [swap(piece, "dp", size, 2 * index) for index in range(1, size // 2)])


def per_device(
    dp_size,
    block_input,
    cotangent,
    item_sides,
    item_modes,
    ln1_gain,
    ln1_bias,
    spec_w1,
    spec_b1,
    spec_w2,
    spec_b2,
    ln2_gain,
    ln2_bias,
    mlp_w1,
    mlp_b1,
    mlp_w2,
    mlp_b2,
):
    own = lax.axis_index("blk").astype(jnp.int32).reshape(1)
    place = lax.axis_index("dp").astype(jnp.int32).reshape(1)
    cube = (SMAX, SMAX, LANES)
    x = block_input.reshape(cube)
    gain1, bias1 = ln1_gain.reshape(1, LANES), ln1_bias.reshape(1, LANES)

    depth = C // dp_size
    share = jnp.stack([lax.dynamic_slice_in_dim(w, place[0] * depth, depth) for w in (mlp_w1, mlp_w2)])
    share = swap(share, "blk", PARTS, 2)
    moment = moments(
        item_sides, x, mlp_b1.reshape(4, LANES), ln2_gain.reshape(1, LANES), ln2_bias.reshape(1, LANES)
    )
    stats = exchange([moment] * PARTS)
    g_parts, grad_b2 = cotangent_pieces(item_sides, after(cotangent.reshape(cube), moment))
    g = lax.all_to_all(after(g_parts, *stats[1:]), "blk", 0, 0).reshape(PARTS, CHUNKS * PIECE, LANES)
    sides = after(item_sides, g_parts)
    f6, g6, ft3, gt3, w1c, w2c, w1t, w2t = prepare(table(sides, item_modes), spec_w1, spec_w2)
    far = lax.all_gather(after(share, moment), "dp", axis=0)
    mlp_w1, mlp_w2, _ = lax.optimization_barrier((mlp_w1, mlp_w2, stats[3]))
    one = [mlp_w1, swap(mlp_w1, "blk", PARTS, 1)]
    two = [mlp_w2, swap(mlp_w2, "blk", PARTS, 1)]

    b, xn, xhat, r = first_stage(item_sides, after(x, g_parts), stats, gain1, bias1, f6)
    bre, bim, a, p, o = mix_forward(
        b, g6, w1c, spec_b1.reshape(1, 256), w2c, spec_b2.reshape(1, 256), gt3
    )
    far = after(far, bre)
    far = [far, swap(far, "blk", PARTS, 1)]
    first_pieces, x1 = last_stage(own, bre, bim, xn, ft3, None, 0)
    x1_first = [piece.reshape(PIECE, LANES) for piece in exchange(first_pieces)]
    weights = split_weights(own, one, two, far)
    field = after(xn, g, *weights)
    pieces, x1 = last_stage(own, bre, bim, field, ft3, x1, 1)
    x1_later = [piece.reshape((CHUNKS - 1) * PIECE, LANES) for piece in exchange(pieces)]

    keep, b1s, norms, dx_early = None, [], [], []
    for chunk in range(CHUNKS - 1):
        results = feed(own, x1_later if chunk else x1_first, g, weights, stats, keep, chunk)
        keep = results[:7]
        dx_early.append([v.reshape(1, SLABS, SMAX, LANES) for v in exchange(results[7:11])])
        b1s.append(results[11])
        norms.append(results[12])
    results = feed_forward(own, x1_later, weights, stats, keep[:5], CHUNKS - 1)
    hh, hl, nh, nl, branch = results[:5]
    branch = lax.all_to_all(branch, "blk", 0, 0)
    send2, held2 = weight_grads(own, place, dp_size, [after(g, *dx_early[0][1:], *dx_early[1][1:])], hh, hl, 20)
    local = list(results[5:])
    local[1] = after(local[1], held2)
    results = feed_backward(own, g, weights, local, stats, keep[5:7], CHUNKS - 1)
    ph, plo, dx_last = results[:3]
    b1s.append(results[3])
    norms.append(results[4])
    got2 = after(held2, ph) + swap(send2, "blk", PARTS, 1)
    dx_last = lax.all_to_all(dx_last, "blk", 0, 0).reshape(PARTS, SLABS, SMAX, LANES)
    ph = after(ph, got2, branch)
    send1, held1 = weight_grads(own, place, dp_size, [nh, nl], ph, plo, 20)

    half, cut = dp_size // 2, send1.shape[2] // 2
    mine2 = got2[:, :half] + swap(got2[:, half:], "dp", dp_size, 1)
    got1 = after(held1, dx_last) + swap(send1, "blk", PARTS, 1)
    d, dx = first_back(own, dx_early, after(dx_last, mine2), f6)
    mine2 = after(mine2[0], d) + swap(mine2[1], "blk", PARTS, 2)
    early = mix_backward(after(d, got1, mine2), a, p, o, g6, w1t, w2t, gt3, None, None)
    kept = after(got1, early[0])
    one = kept[:, :half, :cut] + swap(got1[:, half:, :cut], "dp", dp_size, 1)
    two = kept[0, :, cut:] + swap(got1[1, :, cut:], "blk", PARTS, 2)
    second = scatter_last(after(mine2, d), dp_size, early[0])
    d_late = after(d, early[0], second, one, two)
    late = mix_backward(d_late, a, p, o, g6, w1t, w2t, gt3, early[2:], grad_b2)
    near2 = gather_near(after(second, early[0]), dp_size, late[0])
    one = after(one[0], late[0]) + swap(one[1], "blk", PARTS, 2)
    two = after(two[:half], late[0]) + swap(two[half:], "dp", dp_size, 1)
    quarters = [early[0], late[0], early[1], late[1]]
    dx_gated = after(dx, near2, one, two)
    dn, pack, *sums = last_back(quarters, dx_gated, xhat, gain1, ft3, late[2], b1s, norms)
    first = scatter_last(jnp.concatenate([one, two], axis=1), dp_size, dn)
    far2 = swap(after(near2, late[0]), "dp", dp_size, 1)
    sums = exchange([after(value, first) for value in sums])
    input_grad = final_stage(item_sides, after(dx, far2), dn, xhat, sums, r, gain1)
    tail = sums[0][-1] + sums[1][-1] + sums[2][-1] + sums[3][-1]
    pack = jnp.concatenate([pack, tail], axis=0)
    near1 = gather_near(first, dp_size, input_grad)
    pack = after(pack, input_grad) + swap(pack, "dp", dp_size, 1)
    block_output = output_stage(
        item_sides,
        after(x1, input_grad, near1),
        branch.reshape(PARTS, CHUNKS, SLABS, SMAX, LANES),
        mlp_b2.reshape(1, LANES),
    )
    distance = 2
    while distance < dp_size:
        pack = pack + swap(pack, "dp", dp_size, distance)
        distance *= 2
    far1 = swap(near1, "dp", dp_size, 1)
    w1_grad, w2_grad = assemble(place, near2, far2, near1, far1)

    spec = pack[: 4 * FREQ].reshape(2, 2, FREQ, 2, FREQ).transpose(0, 1, 3, 2, 4)
    rest = pack[4 * FREQ :]
    return (
        block_output.reshape(SMAX * SMAX, LANES),
        input_grad.reshape(SMAX * SMAX, LANES),
        rest[5],
        rest[6],
        spec[0],
        rest[0:2].reshape(2, 2, 64),
        spec[1],
        rest[2:4].reshape(2, 2, 64),
        rest[12],
        rest[13],
        w1_grad,
        rest[8:12].reshape(HID),
        w2_grad,
        rest[4],
    )


def solution(mesh):
    in_specs = (
        P("dp", "blk"),
        P("dp", "blk"),
        P("dp"),
        P("dp"),
        P("blk"),
        P("blk"),
        P(None, "blk", None, None),
        P(None, "blk", None),
        P(None, "blk", None, None),
        P(None, "blk", None),
        P("blk"),
        P("blk"),
        P(None, "blk"),
        P("blk"),
        P("blk", None),
        P("blk"),
    )
    out_specs = (
        P("dp", "blk"),
        P("dp", "blk"),
        P("blk"),
        P("blk"),
        P(None, "blk", None, None),
        P(None, "blk", None),
        P(None, "blk", None, None),
        P(None, "blk", None),
        P("blk"),
        P("blk"),
        P(None, "blk"),
        P("blk"),
        P("blk", None),
        P("blk"),
    )
    return jax.shard_map(
        functools.partial(per_device, mesh.shape["dp"]),
        mesh=mesh,
        in_specs=in_specs,
        out_specs=out_specs,
        check_vma=False,
    )
```

```python
import functools
import math

import jax
import jax.numpy as jnp
from jax import lax
from jax.experimental import pallas as pl
from jax.experimental.pallas import tpu as pltpu
from jax.sharding import PartitionSpec as P

C = 512
MODES = 32
SMAX = 96
LANES = 128
FREQ = 64
HALF = 32
PARTS = 4
CHUNKS = 3
SLABS = SMAX // (PARTS * CHUNKS)
PIECE = SLABS * SMAX
GROUP = PARTS * SLABS
STEPS = SMAX // SLABS
STAGE = 24
THIRDS = STAGE // SLABS
WIDTH = 8
BATCH = 4
TILE = 256
SUB = 768
HID = 512
PACK = 4 * FREQ + 8

EPS = 1e-05
SHRINK = 0.01
F32 = jnp.float32
BF16 = jnp.bfloat16
NN = (((1,), (0,)), ((), ()))
NT = (((1,), (1,)), ((), ()))
TN = (((0,), (0,)), ((), ()))
LIMIT = 56 * 1024 * 1024


def mm(left, right, dims=NN):
    return lax.dot_general(left, right, dims, preferred_element_type=F32)


def split2(value):
    high = value.astype(BF16)
    return high, (value - high.astype(F32)).astype(BF16)


def split3(value):
    high = value.astype(BF16)
    rest = value - high.astype(F32)
    mid = rest.astype(BF16)
    return high, mid, (rest - mid.astype(F32)).astype(BF16)


def left6(value):
    one, two, three = split3(value)
    return jnp.concatenate([one, one, two, one, two, three], axis=1)


def right6(value):
    one, two, three = split3(value)
    return jnp.concatenate([one, two, one, three, two, one], axis=0)


def left3(value):
    one, two = split2(value)
    return jnp.concatenate([one, one, two], axis=1)


def right3(value):
    one, two = split2(value)
    return jnp.concatenate([one, two, one], axis=0)


def phi_pair(value):
    cdf = 0.5 + 0.5 * lax.erf(value * math.sqrt(0.5))
    pdf = jnp.exp(value * value * -0.5) * (1.0 / math.sqrt(2.0 * math.pi))
    return cdf, pdf


def pad_rows(value):
    return jnp.concatenate([value, jnp.zeros((LANES - SMAX, value.shape[1]), F32)], axis=0)


def fold_rows(value):
    return jnp.sum(value.reshape(-1, 8, value.shape[-1]), axis=0)


def spread8(rows):
    one, two, three = split3(rows)
    parts = [value.astype(F32) for value in (one, two, three)]
    left = jnp.concatenate(parts + [jnp.zeros_like(rows)], axis=0).astype(BF16)
    index = lax.broadcasted_iota(jnp.int32, (32, SLABS * LANES), 0)
    lane = lax.broadcasted_iota(jnp.int32, (32, SLABS * LANES), 1)
    pick = (index % SLABS == lane // LANES) & (index < 3 * SLABS)
    return mm(left, jnp.where(pick, 1.0, 0.0).astype(BF16), TN)


def slab_of(wide, slab):
    return wide[:SMAX, slab * LANES : (slab + 1) * LANES]


def us(time):
    return (int(time * 1e9), int(time * 3e6))


def call(body, out_shape, in_specs, out_specs, grid=(), scratch=(), aliases=None, cost=None):
    flops, moved = cost or (0, 0)
    return pl.pallas_call(
        body,
        out_shape=out_shape,
        grid=grid,
        in_specs=in_specs,
        out_specs=out_specs,
        scratch_shapes=list(scratch),
        input_output_aliases=aliases or {},
        compiler_params=pltpu.CompilerParams(vmem_limit_bytes=LIMIT),
        cost_estimate=pl.CostEstimate(flops=flops, bytes_accessed=moved, transcendentals=0),
    )


SMEM = pl.BlockSpec(memory_space=pltpu.SMEM)
VMEM = pl.BlockSpec(memory_space=pltpu.VMEM)
ANY = pl.BlockSpec(memory_space=pl.ANY)


def whole(shape):
    zeros = (0,) * len(shape)
    return pl.BlockSpec(shape, lambda *_: zeros)


def sds(shape, dtype=F32):
    return jax.ShapeDtypeStruct(shape, dtype)


def table(item_sides, item_modes):
    row = lax.broadcasted_iota(jnp.int32, (LANES, LANES), 0)
    cell = lax.broadcasted_iota(jnp.int32, (LANES, LANES), 1)
    index = row % FREQ
    frequency = index - (MODES - 1)
    extent = item_sides[0]
    phase = frequency * cell % extent
    keep = (jnp.abs(frequency) < item_modes[0]) & (cell < extent) & (index < 2 * MODES - 1)
    length = extent.astype(F32)
    angle = 2.0 * math.pi * phase.astype(F32) / length
    wave = jnp.where(row < FREQ, jnp.cos(angle), -jnp.sin(angle)) * lax.rsqrt(length)
    return jnp.where(keep, wave, jnp.zeros_like(wave))


def big_weight(weight, out):
    out[...] = jnp.zeros_like(out)
    for block in range(2):
        rows = pl.ds(block * 64, 64)
        later = pl.ds(128 + block * 64, 64)
        out[rows, rows] = weight[0, block]
        out[rows, later] = weight[1, block]
        out[later, rows] = -weight[1, block]
        out[later, later] = weight[0, block]


def prepare_body(f_ref, w1_ref, w2_ref, f6, g6, ft3, gt3, w1c, w2c, w1t, w2t, big):
    full = f_ref[...]
    cosine, sine = full[:FREQ], full[FREQ:]
    half = jnp.concatenate([cosine[HALF - 1 : FREQ - 1], sine[HALF - 1 : FREQ - 1]], axis=0)
    f6[...] = left6(half)
    ft3[...] = left3(half.T)
    lines = [(cosine, -sine), (sine, cosine), (cosine, sine), (sine, -cosine)]
    table_ = jnp.concatenate([jnp.concatenate(line, axis=1) for line in lines], axis=0)
    g6[...] = left6(table_)
    gt3[...] = left3(table_.T)
    for source, straight, across in ((w1_ref, w1c, w1t), (w2_ref, w2c, w2t)):
        big_weight(source, big)
        straight[...] = right6(big[...])
        across[...] = right3(big[...].T)


def prepare(forward, spec_w1, spec_w2):
    shapes = [
        sds((64, 768), BF16),
        sds((256, 1536), BF16),
        sds((128, 192), BF16),
        sds((256, 768), BF16),
        sds((1536, 256), BF16),
        sds((1536, 256), BF16),
        sds((768, 256), BF16),
        sds((768, 256), BF16),
    ]
    return call(
        prepare_body,
        shapes,
        [VMEM] * 3,
        [VMEM] * 8,
        scratch=[pltpu.VMEM((256, 256), F32)],
        cost=us(3),
    )(forward, spec_w1, spec_w2)


def slab_mask(first, side):
    cell = lax.broadcasted_iota(jnp.int32, (SMAX, LANES), 0)
    return (cell < side) & (first < side)


def moments_body(side_ref, x_ref, b1_ref, gain_ref, bias_ref, out_ref):
    step = pl.program_id(0)
    side = side_ref[0]

    @pl.when(step == 0)
    def _():
        vectors = [b1_ref[...], gain_ref[...], bias_ref[...], jnp.zeros((2, LANES), F32)]
        out_ref[2 * STEPS] = jnp.concatenate(vectors, axis=0)

    for slab in range(STAGE):
        inside = slab_mask(step * STAGE + slab, side)
        value = pad_rows(jnp.where(inside, x_ref[slab], 0.0)).T
        mean = jnp.sum(value, axis=0, keepdims=True) * (1.0 / LANES)
        centered = value - mean
        block, row = step * THIRDS + slab // SLABS, pl.ds(slab % SLABS, 1)
        out_ref[block, row, :] = mean
        out_ref[STEPS + block, row, :] = jnp.sum(centered * centered, axis=0, keepdims=True)


def moments(side, x, b1, gain, bias):
    return call(
        moments_body,
        sds((2 * STEPS + 1, SLABS, LANES)),
        [
            SMEM,
            pl.BlockSpec((STAGE, SMAX, LANES), lambda i: (i, 0, 0)),
            whole((4, LANES)),
            whole((1, LANES)),
            whole((1, LANES)),
        ],
        whole((2 * STEPS + 1, SLABS, LANES)),
        grid=(SMAX // STAGE,),
        cost=us(6),
    )(side, x, b1, gain, bias)


def cotangent_body(side_ref, g_ref, out_ref, total):
    chunk = pl.program_id(0)
    side = side_ref[0]

    @pl.when(chunk == 0)
    def _():
        total[...] = jnp.zeros_like(total)

    carry = jnp.zeros((8, LANES), F32)
    for part in range(PARTS):
        for slab in range(SLABS):
            first = part * SLABS + slab
            value = jnp.where(slab_mask(chunk * GROUP + first, side), g_ref[first], 0.0)
            out_ref[part, 0, slab] = value
            carry = carry + fold_rows(value)
    total[...] += carry


def cotangent_pieces(side, g):
    return call(
        cotangent_body,
        [sds((PARTS, CHUNKS, SLABS, SMAX, LANES)), sds((8, LANES))],
        [SMEM, pl.BlockSpec((GROUP, SMAX, LANES), lambda i: (i, 0, 0))],
        [
            pl.BlockSpec((PARTS, 1, SLABS, SMAX, LANES), lambda i: (0, i, 0, 0, 0)),
            whole((8, LANES)),
        ],
        grid=(CHUNKS,),
        cost=us(5),
    )(side, g)


def row_stats(means, totals):
    mean = (means[0] + means[1] + means[2] + means[3]) * (1.0 / PARTS)
    total = totals[0] + totals[1] + totals[2] + totals[3]
    for part in range(PARTS):
        gap = means[part] - mean
        total = total + LANES * (gap * gap)
    spread_ = total * (1.0 / C) + EPS
    inverse = lax.rsqrt(spread_)
    inverse = inverse * (1.5 - 0.5 * spread_ * inverse * inverse)
    return mean, inverse


def first_body(side_ref, x_ref, *refs):
    stats = refs[:PARTS]
    gain_ref, bias_ref, f6_ref, b_ref, xn_ref, xhat_ref, r_ref = refs[PARTS:]
    step = pl.program_id(0)
    side = side_ref[0]
    gain, bias = gain_ref[...], bias_ref[...]
    for third in range(THIRDS):
        block = step * THIRDS + third
        mean, inverse = row_stats([ref[block] for ref in stats], [ref[STEPS + block] for ref in stats])
        r_ref[pl.ds(third * SLABS, SLABS), :] = inverse
        means, scales = spread8(mean), spread8(inverse)
        for pair in range(SLABS // 2):
            columns = []
            for inner in (2 * pair, 2 * pair + 1):
                slab = third * SLABS + inner
                value = jnp.where(slab_mask(step * STAGE + slab, side), x_ref[slab], 0.0)
                centered = value - slab_of(means, inner)
                normal = centered * slab_of(scales, inner)
                normed = normal * gain + bias
                xhat_ref[slab] = normal
                xn_ref[slab] = value + normed
                columns.append(pad_rows(normed))
            out = mm(f6_ref[...], right6(jnp.concatenate(columns, axis=1)))
            b_ref[slab - 1] = out[:, :LANES]
            b_ref[slab] = out[:, LANES:]


def first_stage(side, x, stats, gain, bias, f6):
    field = pl.BlockSpec((STAGE, SMAX, LANES), lambda i: (i, 0, 0))
    return call(
        first_body,
        [sds((SMAX, FREQ, LANES)), sds((SMAX, SMAX, LANES)), sds((SMAX, SMAX, LANES)), sds((SMAX, LANES))],
        [SMEM, field]
        + [whole((2 * STEPS + 1, SLABS, LANES))] * PARTS
        + [whole((1, LANES)), whole((1, LANES)), whole((64, 768))],
        [
            pl.BlockSpec((STAGE, FREQ, LANES), lambda i: (i, 0, 0)),
            field,
            field,
            pl.BlockSpec((STAGE, LANES), lambda i: (i, 0)),
        ],
        grid=(SMAX // STAGE,),
        cost=us(3),
    )(side, x, *stats, gain, bias, f6)


def gather_columns(re_ref, im_ref, first):
    zeros = jnp.zeros((LANES - SMAX, LANES), F32)
    re, im = [ref.reshape(SMAX * WIDTH, LANES) for ref in (re_ref, im_ref)]
    columns = []
    for j in range(first, first + BATCH):
        rows = pl.ds(j, SMAX, stride=WIDTH)
        columns.append(jnp.concatenate([re[rows, :], zeros, im[rows, :], zeros], axis=0))
    return jnp.concatenate(columns, axis=1)


def to_rows(out):
    rows = []
    for j in range(BATCH):
        lanes = part_lanes(j)
        for base in (0, 2 * FREQ):
            parts = [out[base : base + FREQ, lanes], out[base + FREQ : base + 2 * FREQ, lanes]]
            rows.append(jnp.concatenate(parts, axis=1))
    return jnp.concatenate(rows, axis=0)


def to_columns(rows):
    columns = []
    for j in range(BATCH):
        parts = []
        for sign in range(2):
            first = (2 * j + sign) * FREQ
            part = rows[first : first + FREQ]
            parts += [part[:, :LANES], part[:, LANES:]]
        columns.append(jnp.concatenate(parts, axis=0))
    return jnp.concatenate(columns, axis=1)


def counted(step, half, shape):
    row = lax.broadcasted_iota(jnp.int32, shape, 0)
    twice = (step == 0) & (half == 0)
    return (row < FREQ) | (row >= 2 * FREQ) | jnp.logical_not(twice)


def scatter_columns(re_ref, im_ref, first, out):
    re, im = [ref.reshape(SMAX * WIDTH, LANES) for ref in (re_ref, im_ref)]
    for j in range(BATCH):
        lanes = slice(j * LANES, (j + 1) * LANES)
        rows = pl.ds(first + j, SMAX, stride=WIDTH)
        re[rows, :] = out[:SMAX, lanes]
        im[rows, :] = out[LANES : LANES + SMAX, lanes]


def shrink(value):
    return jnp.where(
        value > SHRINK,
        value - SHRINK,
        jnp.where(value < -SHRINK, value + SHRINK, jnp.zeros_like(value)),
    )


def mix_body(re_ref, im_ref, g6_ref, w1_ref, b1_ref, w2_ref, b2_ref, gt3_ref, bre, bim, a_out, p_out, o_out):
    for half in range(WIDTH // BATCH):
        rows = pl.ds(half * 2 * BATCH * FREQ, 2 * BATCH * FREQ)
        spectrum = to_rows(mm(g6_ref[...], right6(gather_columns(re_ref, im_ref, BATCH * half))))
        a_out[rows, :] = spectrum
        pre = mm(left6(spectrum), w1_ref[...]) + b1_ref[...]
        p_out[rows, :] = pre
        cdf = 0.5 + 0.5 * lax.erf(pre * math.sqrt(0.5))
        out = mm(left6(pre * cdf), w2_ref[...]) + b2_ref[...]
        o_out[rows, :] = out
        if half == 0:
            out = jnp.where(counted(pl.program_id(0), half, out.shape), out, 0.0)
        scatter_columns(bre, bim, BATCH * half, mm(gt3_ref[...], right3(to_columns(shrink(out)))))


def mix_forward(b, g6, w1c, bias1, w2c, bias2, gt3):
    count = HALF // WIDTH
    re = pl.BlockSpec((SMAX, WIDTH, LANES), lambda j: (0, j, 0))
    im = pl.BlockSpec((SMAX, WIDTH, LANES), lambda j: (0, count + j, 0))
    out = pl.BlockSpec((SMAX, WIDTH, LANES), lambda j: (0, j, 0))
    rows = pl.BlockSpec((2 * WIDTH * FREQ, 256), lambda j: (j, 0))
    half = sds((SMAX, HALF, LANES))
    return call(
        mix_body,
        [half, half] + [sds((4096, 256))] * 3,
        [
            re,
            im,
            whole((256, 1536)),
            whole((1536, 256)),
            whole((1, 256)),
            whole((1536, 256)),
            whole((1, 256)),
            whole((256, 768)),
        ],
        [out, out, rows, rows, rows],
        grid=(count,),
        cost=us(4),
    )(b, b, g6, w1c, bias1, w2c, bias2, gt3)


def last_body(own_ref, re_ref, im_ref, xn_ref, ft3_ref, *refs):
    full, outs = refs[-1], refs[-1 - PARTS : -1]
    own = own_ref[0]
    for part in range(PARTS):
        base = (own ^ part) * SLABS
        for pair in range(SLABS // 2):
            slabs = (base + 2 * pair, base + 2 * pair + 1)
            columns = [jnp.concatenate([re_ref[s], im_ref[s]], axis=0) for s in slabs]
            out = mm(ft3_ref[...], right3(jnp.concatenate(columns, axis=1)))[:SMAX]
            for index, s in enumerate(slabs):
                value = xn_ref[s] + out[:, index * LANES : (index + 1) * LANES]
                full[s] = value
                if len(outs[part].shape) == 3:
                    outs[part][2 * pair + index] = value
                else:
                    outs[part][0, 2 * pair + index] = value


def last_stage(own, bre, bim, xn, ft3, keep, chunk):
    half = pl.BlockSpec((GROUP, HALF, LANES), lambda i: (chunk + i, 0, 0))
    field = pl.BlockSpec((GROUP, SMAX, LANES), lambda i: (chunk + i, 0, 0))
    args = [own, bre, bim, xn, ft3]
    in_specs = [SMEM, half, half, field, whole((128, 192))]
    aliases = {}
    steps = 1 if chunk == 0 else CHUNKS - 1
    if keep is not None:
        aliases[len(args)] = PARTS
        args.append(keep)
        in_specs.append(ANY)
    piece = (SLABS, SMAX, LANES)
    shape = piece if chunk == 0 else (steps,) + piece
    spec = whole(piece)
    if chunk > 0:
        spec = pl.BlockSpec((1,) + piece, lambda i: (i, 0, 0, 0))
    *pieces, full = call(
        last_body,
        [sds(shape)] * PARTS + [sds((SMAX, SMAX, LANES))],
        in_specs,
        [spec] * PARTS + [field],
        grid=(steps,),
        aliases=aliases,
        cost=us(4 * steps),
    )(*args)
    return pieces, full


def weights_body(own_ref, *refs):
    step = pl.program_id(0)
    own = own_ref[0]
    one, two = refs[0:2], refs[2:4]
    far = refs[4:6]
    w1h, w1l, w2h, w2l = refs[6:]

    def emit(first, second):
        for part in range(PARTS):
            source = pl.ds(pl.multiple_of((own ^ part) * LANES, LANES), LANES)
            target = slice(part * LANES, (part + 1) * LANES)
            w1h[0, target, :], w1l[0, target, :] = split2(first(source))
            w2h[0, :, target], w2l[0, :, target] = split2(second(source))

    for index in range(2):

        @pl.when(step == index)
        def _(index=index):
            emit(lambda rows: one[index][rows, :], lambda lanes: two[index][:, lanes])

        @pl.when(step == 2 + index)
        def _(index=index):
            ref = far[index]
            depth = ref.shape[0] // PARTS

            def rows_of(rows):
                first = pl.multiple_of(rows.start // ref.shape[2], depth)
                return ref[pl.ds(first, depth), 0].reshape(LANES, 512)

            emit(rows_of, lambda lanes: ref[:, 1, :, lanes].reshape(512, LANES))


def split_weights(own, one, two, far):
    block = pl.BlockSpec((1, 512, 512), lambda i: (i, 0, 0))
    return call(
        weights_body,
        [sds((4, 512, 512), BF16)] * 4,
        [SMEM] + [whole((512, 512))] * 4 + [whole(far[0].shape)] * 2,
        [block] * 4,
        grid=(4,),
        cost=us(7),
    )(own, *one, *two, *far)


def row_mean(parts):
    total = parts[0] + parts[1] + parts[2] + parts[3]
    return jnp.sum(total, axis=1, keepdims=True) * (1.0 / C)


def part_lanes(part):
    return slice(part * LANES, (part + 1) * LANES)


def norm_tiles(load, vectors, n_h, n_l, nh, nl, xhat, scale):
    def norm(tile, carry):
        rows = pl.ds(tile * TILE, TILE)
        values = [load(part, rows) for part in range(PARTS)]
        mean = row_mean(values)
        centered = [value - mean for value in values]
        spread_ = row_mean([value * value for value in centered]) + EPS
        inverse = lax.rsqrt(spread_)
        inverse = inverse * (1.5 - 0.5 * spread_ * inverse * inverse)
        scale[rows, :] = jnp.broadcast_to(inverse, (TILE, LANES))
        for part in range(PARTS):
            lanes = part_lanes(part)
            normal = centered[part] * inverse
            xhat[rows, lanes] = normal
            gain, bias = vectors[part][0, 4:5, :], vectors[part][0, 5:6, :]
            high, low = split2(normal * gain + bias)
            n_h[rows, lanes] = high
            n_l[rows, lanes] = low
            nh[rows, lanes] = high
            nl[rows, lanes] = low
        return carry

    lax.fori_loop(0, PIECE // TILE, norm, 0)


def bias_of(vectors, step):
    row = jnp.zeros((4, LANES), F32)
    for part in range(PARTS):
        row = jnp.where(step == part, vectors[part][0, 0:4, :], row)
    return jnp.concatenate([row[i : i + 1] for i in range(4)], axis=1)


def grad_tiles(own, g_ref, vectors, dn, xhat, scale, store, small):
    small[...] = jnp.zeros_like(small)

    def back(tile, carry):
        rows = pl.ds(tile * TILE, TILE)
        inverse = scale[rows, :]
        scaled, normals = [], []
        for part in range(PARTS):
            lanes = part_lanes(part)
            grad = dn[rows, lanes]
            normal = xhat[rows, lanes]
            small[0, :, lanes] += fold_rows(grad * normal)
            small[1, :, lanes] += fold_rows(grad)
            scaled.append(grad * vectors[part][0, 4:5, :])
            normals.append(normal)
        first = row_mean(scaled)
        second = row_mean([s * n for s, n in zip(scaled, normals)])
        for part in range(PARTS):
            delta = inverse * (scaled[part] - first - normals[part] * second)
            store(part, rows, g_ref[own ^ part, rows, :] + delta)
        return carry

    lax.fori_loop(0, PIECE // TILE, back, 0)


def split_cotangent(own, g_ref, g_h, g_l):
    for part in range(PARTS):
        lanes = part_lanes(part)
        g_h[:, lanes], g_l[:, lanes] = split2(g_ref[own ^ part])


def product3(high, low, w_h, w_l, dims=NN):
    return mm(high, w_h[0], dims) + mm(low, w_h[0], dims) + mm(high, w_l[0], dims)


def add_to(ref, step, value):
    ref[...] = jnp.where(step == 0, 0.0, ref[...]) + value


def feed_body(*refs):
    own = refs[0][0]
    x_refs, g_ref = refs[1:5], refs[5]
    w1h, w1l, w2h, w2l = refs[6:10]
    vectors = refs[10:14]
    refs = refs[len(refs) - 21 :]
    hh, hl, nh, nl, out_ref, ph, plo = refs[0:7]
    dx_refs, db1, small = refs[7:11], refs[11], refs[12]
    n_h, n_l, g_h, g_l, xhat, scale, dn, acc = refs[13:21]
    step = pl.program_id(0)

    @pl.when(step == 0)
    def _():
        norm_tiles(lambda part, rows: x_refs[part][rows, :], vectors, n_h, n_l, nh, nl, xhat, scale)
        split_cotangent(own, g_ref, g_h, g_l)

    pre = product3(n_h[...], n_l[...], w1h, w1l) + bias_of(vectors, step)
    dh = product3(g_h[...], g_l[...], w2h, w2l, NT)
    cdf, pdf = phi_pair(pre)
    high, low = split2(pre * cdf)
    hh[...] = high
    hl[...] = low
    grad = dh * (cdf + pre * pdf)
    add_to(acc, step, product3(high, low, w2h, w2l))
    high, low = split2(grad)
    ph[...] = high
    plo[...] = low
    db1[0] = fold_rows(grad)
    add_to(dn, step, product3(high, low, w1h, w1l, NT))

    @pl.when(step == pl.num_programs(0) - 1)
    def _():
        for part in range(PARTS):
            out_ref[own ^ part, 0] = acc[:, part_lanes(part)]

        def store(part, rows, value):
            dx_refs[part][rows, :] = value

        grad_tiles(own, g_ref, vectors, dn, xhat, scale, store, small)


def forward_body(*refs):
    own = refs[0][0]
    x_refs = refs[1:5]
    w1h, w1l, w2h, w2l = refs[5:9]
    vectors = refs[9:13]
    hh, hl, nh, nl, out_ref, slope, xhat, scale, n_h, n_l, acc = refs[len(refs) - 11 :]
    step = pl.program_id(0)

    @pl.when(step == 0)
    def _():
        norm_tiles(lambda part, rows: x_refs[part][rows, :], vectors, n_h, n_l, nh, nl, xhat, scale)

    pre = product3(n_h[...], n_l[...], w1h, w1l) + bias_of(vectors, step)
    cdf, pdf = phi_pair(pre)
    slope[...] = cdf + pre * pdf
    high, low = split2(pre * cdf)
    hh[...] = high
    hl[...] = low
    add_to(acc, step, product3(high, low, w2h, w2l))

    @pl.when(step == pl.num_programs(0) - 1)
    def _():
        for part in range(PARTS):
            out_ref[own ^ part, 0] = acc[:, part_lanes(part)]


def backward_body(*refs):
    own = refs[0][0]
    g_ref, w1h, w1l, w2h, w2l, slope, xhat, scale = refs[1:9]
    vectors = refs[9:13]
    refs = refs[len(refs) - 11 :]
    ph, plo, dx_refs, db1, small = refs[0], refs[1], refs[2:6], refs[6], refs[7]
    g_h, g_l, dn = refs[8:]
    step = pl.program_id(0)

    @pl.when(step == 0)
    def _():
        split_cotangent(own, g_ref, g_h, g_l)

    grad = product3(g_h[...], g_l[...], w2h, w2l, NT) * slope[...]
    high, low = split2(grad)
    ph[...] = high
    plo[...] = low
    db1[0] = fold_rows(grad)
    add_to(dn, step, product3(high, low, w1h, w1l, NT))

    @pl.when(step == pl.num_programs(0) - 1)
    def _():

        def store(part, rows, value):
            dx_refs[part][rows, :] = value

        grad_tiles(own, g_ref, vectors, dn, xhat, scale, store, small)


def feed_call(body, head, heads, weights, stats, local, keep, kinds, chunk, cost):
    rows = PIECE * CHUNKS
    specs = {
        "x": (sds((PIECE, LANES)), whole((PIECE, LANES))),
        "later": (None, pl.BlockSpec((PIECE, LANES), lambda i: (chunk - 1, 0))),
        "g": (None, pl.BlockSpec((PARTS, PIECE, LANES), lambda i: (0, chunk, 0))),
        "out": (
            sds((PARTS, CHUNKS - 1, PIECE, LANES)),
            pl.BlockSpec((PARTS, 1, PIECE, LANES), lambda i: (0, chunk, 0, 0)),
        ),
        "wide": (sds((rows, 2048), BF16), pl.BlockSpec((PIECE, HID), lambda i: (chunk, i))),
        "narrow": (sds((rows, C), BF16), pl.BlockSpec((PIECE, C), lambda i: (chunk, 0))),
        "slope": (sds((PIECE, 2048)), pl.BlockSpec((PIECE, HID), lambda i: (0, i))),
        "tip": (sds((PARTS, 1, PIECE, LANES)), whole((PARTS, 1, PIECE, LANES))),
        "full": (sds((PIECE, C)), whole((PIECE, C))),
        "db1": (sds((4, 8, HID)), pl.BlockSpec((1, 8, HID), lambda i: (i, 0, 0))),
        "small": (sds((2, 8, C)), whole((2, 8, C))),
    }
    weight = pl.BlockSpec((1, 512, 512), lambda i: (i, 0, 0))
    vector = pl.BlockSpec((1, SLABS, LANES), lambda i: (2 * STEPS, 0, 0))
    args = [*head, *weights, *(value for _, value in local), *stats]
    in_specs = [SMEM] + [specs[kind][1] for kind in heads] + [weight] * 4
    in_specs += [specs[kind][1] for kind, _ in local] + [vector] * 4
    aliases = {}
    for index, array in enumerate(keep or ()):
        aliases[len(args)] = index
        args.append(array)
        in_specs.append(ANY)
    bf, big = pltpu.VMEM((PIECE, C), BF16), pltpu.VMEM((PIECE, C), F32)
    scratch = {
        "feed": [bf] * 4 + [big, pltpu.VMEM((PIECE, LANES), F32), big, big],
        "fore": [bf, bf, big],
        "back": [bf, bf, big],
    }[kinds]
    outs = {
        "feed": ["wide"] * 2 + ["narrow"] * 2 + ["out", "wide", "wide"] + ["x"] * 4 + ["db1", "small"],
        "fore": ["wide"] * 2 + ["narrow"] * 2 + ["tip", "slope", "full", "x"],
        "back": ["wide", "wide"] + ["x"] * 4 + ["db1", "small"],
    }[kinds]
    return call(
        body,
        [specs[kind][0] for kind in outs],
        in_specs,
        [specs[kind][1] for kind in outs],
        grid=(4,),
        scratch=scratch,
        aliases=aliases,
        cost=us(cost),
    )(*args)


def feed(own, xs, g, weights, stats, keep, chunk):
    head, heads = [own, *xs, g], ["x" if chunk == 0 else "later"] * 4 + ["g"]
    return feed_call(feed_body, head, heads, weights, stats, [], keep, "feed", chunk, 28)


def feed_forward(own, xs, weights, stats, keep, chunk):
    return feed_call(forward_body, [own, *xs], ["later"] * 4, weights, stats, [], keep, "fore", chunk, 18)


def feed_backward(own, g, weights, local, stats, keep, chunk):
    local = list(zip(("slope", "full", "x"), local))
    return feed_call(backward_body, [own, g], ["g"], weights, stats, local, keep, "back", chunk, 16)


def weight_body(own_ref, place_ref, th, tl, *refs):
    send, held, t_h, t_l = refs[-4:]
    step = pl.program_id(0)
    own, place = own_ref[0], place_ref[0]

    @pl.when(step == 0)
    def _():
        if len(refs) == 6:
            t_h[...] = refs[0][...].T
            t_l[...] = refs[1][...].T
        else:
            for part in range(PARTS):
                high, low = split2(refs[0][own ^ part])
                t_h[part_lanes(part), :] = high.T
                t_l[part_lanes(part), :] = low.T

    out = mm(t_h[...], th[...]) + mm(t_l[...], th[...]) + mm(t_h[...], tl[...])
    count, depth = send.shape[1], send.shape[2]

    def store(ref):
        for index in range(count):
            part, inner = divmod(index, count // PARTS)
            apart = ((own ^ part) * (count // PARTS) + inner) ^ place
            where = (apart & 1) * (count // 2) + (apart >> 1)
            ref[0, where] = out[index * depth : (index + 1) * depth]

    @pl.when(step < 2)
    def _():
        store(send)

    @pl.when(step >= 2)
    def _():
        store(held)


def weight_grads(own, place, dp_size, left, th, tl, cost):
    rows = PIECE * CHUNKS
    wide = pl.BlockSpec((rows, HID), lambda i: (0, (i % 2) * 2 + 1 - i // 2))
    block = (1, dp_size, C // dp_size, HID)
    shape = sds((2,) + block[1:])
    return call(
        weight_body,
        [shape, shape],
        [SMEM, SMEM]
        + [wide] * 2
        + [pl.BlockSpec(v.shape, lambda i, n=v.ndim: (0,) * n, pipeline_mode=pl.Buffered(1)) for v in left],
        [
            pl.BlockSpec(block, lambda i: (jnp.minimum(i, 1), 0, 0, 0)),
            pl.BlockSpec(block, lambda i: (jnp.maximum(i - 2, 0), 0, 0, 0)),
        ],
        grid=(4,),
        scratch=[pltpu.VMEM((C, rows), BF16)] * 2,
        cost=us(cost),
    )(own, place, th, tl, *left)


def assemble_body(turn, place_ref, near, far, out_ref, held):
    place = place_ref[0]
    half, depth = near.shape[0], near.shape[1]
    target = held if turn else out_ref
    for side, source in enumerate((near, far)):
        for index in range(half):
            rows = pl.ds(pl.multiple_of((place ^ (2 * index + side)) * depth, depth), depth)
            target[rows, :] = source[index]
    if turn:
        out_ref[...] = held[...].T


def assemble(place, near, far, turn):
    return call(
        functools.partial(assemble_body, turn),
        sds((C, HID)),
        [SMEM] + [VMEM] * 2,
        VMEM,
        scratch=[pltpu.VMEM((C, HID), F32)],
        cost=us(2),
    )(place, near, far)


def first_back_body(own_ref, f6_ref, *refs):
    d_ref, dx_ref = refs[-2:]
    own = own_ref[0]
    for chunk in range(CHUNKS):

        @pl.when(pl.program_id(0) == chunk)
        def _(pieces=refs[PARTS * chunk : PARTS * (chunk + 1)]):
            for part in range(PARTS):
                base = (own ^ part) * SLABS
                for pair in range(SLABS // 2):
                    slabs = (2 * pair, 2 * pair + 1)
                    values = [pieces[part][s] for s in slabs]
                    columns = jnp.concatenate([pad_rows(v) for v in values], axis=1)
                    out = mm(f6_ref[...], right3(columns))
                    for index, s in enumerate(slabs):
                        d_ref[base + s] = out[:, index * LANES : (index + 1) * LANES]
                        dx_ref[base + s] = values[index]


def first_back(own, pieces, f6):
    return call(
        first_back_body,
        [sds((SMAX, FREQ, LANES)), sds((SMAX, SMAX, LANES))],
        [SMEM, whole((64, 384))] + [whole(piece.shape) for piece in pieces],
        [
            pl.BlockSpec((GROUP, FREQ, LANES), lambda i: (i, 0, 0)),
            pl.BlockSpec((GROUP, SMAX, LANES), lambda i: (i, 0, 0)),
        ],
        grid=(CHUNKS,),
        cost=us(8),
    )(own, f6, *pieces)


def rows3(value):
    one, two = split2(value)
    return jnp.concatenate([one, one, two], axis=0)


def mix_back_body(*refs):
    re_ref, im_ref, a_ref, p_ref, o_ref, g3_ref, w1t, w2t, gt3_ref = refs[:9]
    sums = refs[-4:]
    dw1, dw2, db1, db2 = sums
    if len(refs) == 15:
        dre, dim = refs[9:11]
    else:
        gb_ref = refs[13]
        dre, dim, pack = refs[14:17]

    @pl.when(pl.program_id(0) == 0)
    def _():
        for index, ref in enumerate(sums):
            ref[...] = jnp.zeros_like(ref) if len(refs) == 15 else refs[9 + index][...]

    for half in range(WIDTH // BATCH):
        rows = pl.ds(half * 2 * BATCH * FREQ, 2 * BATCH * FREQ)
        dz = to_rows(mm(g3_ref[...], right3(gather_columns(re_ref, im_ref, BATCH * half))))
        do = jnp.where(jnp.abs(o_ref[rows, :]) > SHRINK, dz, 0.0)
        if half == 0 and len(refs) == 15:
            do = jnp.where(counted(pl.program_id(0), half, do.shape), do, 0.0)
        pre = p_ref[rows, :]
        cdf, pdf = phi_pair(pre)
        dw2[...] += mm(rows3(pre * cdf), right3(do), TN)
        db2[...] += fold_rows(do)
        dp = mm(left3(do), w2t[...]) * (cdf + pre * pdf)
        dw1[...] += mm(rows3(a_ref[rows, :]), right3(dp), TN)
        db1[...] += fold_rows(dp)
        dx = mm(left3(dp), w1t[...])
        if half == 0 and len(refs) == 15:
            dx = jnp.where(counted(pl.program_id(0), half, dx.shape), dx, 0.0)
        scatter_columns(dre, dim, BATCH * half, mm(gt3_ref[...], right3(to_columns(dx))))

    if len(refs) == 15:
        return

    @pl.when(pl.program_id(0) == pl.num_programs(0) - 1)
    def _():
        low = lax.broadcasted_iota(jnp.int32, (FREQ, LANES), 1) < FREQ
        for index, ref in enumerate((dw1, dw2)):
            full = ref[...]
            same = full[:LANES, :LANES] + full[LANES:, LANES:]
            cross = full[:LANES, LANES:] - full[LANES:, :LANES]
            for inner, value in enumerate((same, cross)):
                rows = pl.ds((2 * index + inner) * FREQ, FREQ)
                pack[rows, :] = jnp.where(low, value[:FREQ], value[FREQ:])
        sums = [jnp.sum(ref[...], axis=0, keepdims=True) for ref in (db1, db2)]
        lines = [sums[0][:, :LANES], sums[0][:, LANES:], sums[1][:, :LANES], sums[1][:, LANES:]]
        lines.append(jnp.sum(gb_ref[...], axis=0, keepdims=True))
        pack[4 * FREQ : 4 * FREQ + 8] = jnp.concatenate(lines + [jnp.zeros((3, LANES), F32)], axis=0)


def mix_backward(d, a, p, o, g6, w1t, w2t, gt3, carry, grad_b2):
    count = HALF // WIDTH
    skip = 0 if carry is None else count // 2
    re = pl.BlockSpec((SMAX, WIDTH, LANES), lambda j: (0, skip + j, 0))
    im = pl.BlockSpec((SMAX, WIDTH, LANES), lambda j: (0, count + skip + j, 0))
    out = pl.BlockSpec((SMAX, WIDTH, LANES), lambda j: (0, j, 0))
    rows = pl.BlockSpec((2 * WIDTH * FREQ, 256), lambda j: (skip + j, 0))
    half = sds((SMAX, HALF // 2, LANES))
    args = [d, d, a, p, o, g6, w1t, w2t, gt3]
    in_specs = [re, im, rows, rows, rows, whole((256, 768))]
    in_specs += [whole((768, 256)), whole((768, 256)), whole((256, 768))]
    sums = [(256, 256), (256, 256), (8, 256), (8, 256)]
    shapes, out_specs, scratch = [half, half], [out, out], []
    if carry is None:
        shapes += [sds(shape) for shape in sums]
        out_specs += [whole(shape) for shape in sums]
    else:
        args += [*carry, grad_b2]
        in_specs += [whole(shape) for shape in sums] + [whole((8, LANES))]
        shapes.append(sds((PACK, LANES)))
        out_specs.append(whole((PACK, LANES)))
        scratch = [pltpu.VMEM(shape, F32) for shape in sums]
    return call(
        mix_back_body, shapes, in_specs, out_specs, grid=(count // 2,), scratch=scratch, cost=us(13)
    )(*args)


def last_back_body(re0, re1, im0, im1, dx_ref, xhat_ref, gain_ref, ft3_ref, pack_ref, *refs):
    b1_refs, norm_refs = refs[:CHUNKS], refs[CHUNKS : 2 * CHUNKS]
    dn_ref, pack = refs[2 * CHUNKS : 2 * CHUNKS + 2]
    sums, small = refs[-1 - PARTS : -1], refs[-1]
    step = pl.program_id(0)

    @pl.when(step == 0)
    def _():
        small[...] = jnp.zeros_like(small)
        norms = norm_refs[0][...]
        for ref in norm_refs[1:]:
            norms = norms + ref[...]
        norms = [jnp.sum(norms[i], axis=0, keepdims=True) for i in range(2)]
        for part in range(PARTS):
            total = b1_refs[0][part]
            for ref in b1_refs[1:]:
                total = total + ref[part]
            total = jnp.sum(total, axis=0, keepdims=True)
            lines = [total[:, part_lanes(i)] for i in range(4)]
            lines += [value[:, part_lanes(part)] for value in norms]
            lines.append(jnp.zeros((2, LANES), F32))
            sums[part][2 * STEPS] = jnp.concatenate(lines, axis=0)

    gain = gain_ref[...]
    for pair in range(STAGE // 2):
        slabs = (2 * pair, 2 * pair + 1)
        columns = [jnp.concatenate([re0[s], re1[s], im0[s], im1[s]], axis=0) for s in slabs]
        out = mm(ft3_ref[...], right3(jnp.concatenate(columns, axis=1)))[:SMAX]
        for index, s in enumerate(slabs):
            grad = dx_ref[s] + out[:, index * LANES : (index + 1) * LANES]
            dn_ref[s] = grad
            product = grad * xhat_ref[s]
            small[0] += fold_rows(product)
            small[1] += fold_rows(grad)
            for which, value in enumerate((grad, product)):
                row = jnp.sum(pad_rows(value * gain).T, axis=0, keepdims=True)
                for ref in sums:
                    block = which * STEPS + step * THIRDS + s // SLABS
                    ref[block, pl.ds(s % SLABS, 1), :] = row

    @pl.when(step == pl.num_programs(0) - 1)
    def _():
        pack[...] = pack_ref[...]
        for index in range(2):
            where = pl.ds(4 * FREQ + 5 + index, 1)
            pack[where, :] = jnp.sum(small[index], axis=0, keepdims=True)


def last_back(quarters, dx, xhat, gain, ft3, pack, b1s, norms):
    half = pl.BlockSpec((STAGE, HALF // 2, LANES), lambda i: (i, 0, 0))
    field = pl.BlockSpec((STAGE, SMAX, LANES), lambda i: (i, 0, 0))
    shape = (2 * STEPS + 1, SLABS, LANES)
    return call(
        last_back_body,
        [sds((SMAX, SMAX, LANES)), sds((PACK, LANES))] + [sds(shape)] * PARTS,
        [half] * 4
        + [field, field, whole((1, LANES)), whole((128, 192)), whole((PACK, LANES))]
        + [whole((4, 8, HID))] * CHUNKS
        + [whole((2, 8, C))] * CHUNKS,
        [field, whole((PACK, LANES))] + [whole(shape)] * PARTS,
        grid=(SMAX // STAGE,),
        scratch=[pltpu.VMEM((2, 8, LANES), F32)],
        cost=us(13),
    )(*quarters, dx, xhat, gain, ft3, pack, *b1s, *norms)


def final_body(side_ref, dx_ref, dn_ref, xhat_ref, r_ref, gain_ref, *refs):
    sums, out_ref = refs[:PARTS], refs[PARTS]
    step = pl.program_id(0)
    side = side_ref[0]
    for third in range(THIRDS):
        block = step * THIRDS + third
        inverse = r_ref[pl.ds(third * SLABS, SLABS), :]
        total = [sum(ref[which * STEPS + block] for ref in sums) for which in range(2)]
        first = total[0] * (inverse * (1.0 / C))
        second = total[1] * (inverse * (1.0 / C))
        wide = [spread8(value) for value in (inverse, first, second)]
        for inner in range(SLABS):
            slab = third * SLABS + inner
            scaled = dn_ref[slab] * gain_ref[...]
            scale, shift, slope = [slab_of(value, inner) for value in wide]
            value = dx_ref[slab] + (scale * scaled - shift - xhat_ref[slab] * slope)
            out_ref[slab] = jnp.where(slab_mask(step * STAGE + slab, side), value, 0.0)


def final_stage(side, dx, dn, xhat, sums, r, gain):
    field = pl.BlockSpec((STAGE, SMAX, LANES), lambda i: (i, 0, 0))
    return call(
        final_body,
        sds((SMAX, SMAX, LANES)),
        [SMEM, field, field, field, pl.BlockSpec((STAGE, LANES), lambda i: (i, 0)), whole((1, LANES))]
        + [whole((2 * STEPS + 1, SLABS, LANES))] * PARTS,
        field,
        grid=(SMAX // STAGE,),
        cost=us(13),
    )(side, dx, dn, xhat, r, gain, *sums)


def output_body(side_ref, x_ref, y_ref, tip_ref, b2_ref, out_ref):
    step = pl.program_id(0)
    side = side_ref[0]
    for part in range(PARTS):
        for inner in range(SLABS):
            slab = part * SLABS + inner
            branch = jnp.where(step < CHUNKS - 1, y_ref[part, 0, inner], tip_ref[part, inner])
            value = x_ref[slab] + branch + b2_ref[...]
            out_ref[slab] = jnp.where(slab_mask(step * GROUP + slab, side), value, 0.0)


def output_stage(side, x1, y, tip, b2):
    field = pl.BlockSpec((GROUP, SMAX, LANES), lambda i: (i, 0, 0))
    return call(
        output_body,
        sds((SMAX, SMAX, LANES)),
        [
            SMEM,
            field,
            pl.BlockSpec(
                (PARTS, 1, SLABS, SMAX, LANES), lambda i: (0, jnp.minimum(i, CHUNKS - 2), 0, 0, 0)
            ),
            whole((PARTS, SLABS, SMAX, LANES)),
            whole((1, LANES)),
        ],
        field,
        grid=(CHUNKS,),
        cost=us(5),
    )(side, x1, y, tip, b2)


def swap(value, axis, size, distance):
    return lax.ppermute(value, axis, [(i, i ^ distance) for i in range(size)])


def exchange(pieces):
    return [pieces[0]] + [swap(pieces[part], "blk", PARTS, part) for part in range(1, PARTS)]


def after(value, *others):
    return lax.optimization_barrier((value, *others))[0]


def halve(value, size, distance, gate):
    cut = value.shape[0] // 2
    return after(value[:cut], gate) + swap(value[cut:], "dp", size, distance)


def scatter_last(mine, size, gate):
    total = after(mine[0], gate)
    for index in range(1, size // 2):
        total = total + swap(mine[index], "dp", size, 2 * index)
    return total


def gather_near(piece, size, gate):
    return jnp.stack([after(piece, gate)] + [swap(piece, "dp", size, 2 * index) for index in range(1, size // 2)])


def per_device(
    dp_size,
    block_input,
    cotangent,
    item_sides,
    item_modes,
    ln1_gain,
    ln1_bias,
    spec_w1,
    spec_b1,
    spec_w2,
    spec_b2,
    ln2_gain,
    ln2_bias,
    mlp_w1,
    mlp_b1,
    mlp_w2,
    mlp_b2,
):
    own = lax.axis_index("blk").astype(jnp.int32).reshape(1)
    place = lax.axis_index("dp").astype(jnp.int32).reshape(1)
    cube = (SMAX, SMAX, LANES)
    x = block_input.reshape(cube)
    gain1, bias1 = ln1_gain.reshape(1, LANES), ln1_bias.reshape(1, LANES)

    depth = C // dp_size
    share = jnp.stack([lax.dynamic_slice_in_dim(w, place[0] * depth, depth) for w in (mlp_w1, mlp_w2)])
    share = swap(share, "blk", PARTS, 2)
    moment = moments(
        item_sides, x, mlp_b1.reshape(4, LANES), ln2_gain.reshape(1, LANES), ln2_bias.reshape(1, LANES)
    )
    stats = exchange([moment] * PARTS)
    g_parts, grad_b2 = cotangent_pieces(item_sides, after(cotangent.reshape(cube), moment))
    g = lax.all_to_all(after(g_parts, *stats[1:]), "blk", 0, 0).reshape(PARTS, CHUNKS * PIECE, LANES)
    sides = after(item_sides, g_parts)
    f6, g6, ft3, gt3, w1c, w2c, w1t, w2t = prepare(table(sides, item_modes), spec_w1, spec_w2)
    far = lax.all_gather(after(share, moment), "dp", axis=0)
    mlp_w1, mlp_w2, _ = lax.optimization_barrier((mlp_w1, mlp_w2, stats[3]))
    one = [mlp_w1, swap(mlp_w1, "blk", PARTS, 1)]
    two = [mlp_w2, swap(mlp_w2, "blk", PARTS, 1)]

    b, xn, xhat, r = first_stage(item_sides, after(x, g_parts), stats, gain1, bias1, f6)
    bre, bim, a, p, o = mix_forward(
        b, g6, w1c, spec_b1.reshape(1, 256), w2c, spec_b2.reshape(1, 256), gt3
    )
    far = after(far, bre)
    far = [far, swap(far, "blk", PARTS, 1)]
    first_pieces, x1 = last_stage(own, bre, bim, xn, ft3, None, 0)
    x1_first = [piece.reshape(PIECE, LANES) for piece in exchange(first_pieces)]
    weights = split_weights(own, one, two, far)
    field = after(xn, g, *weights)
    pieces, x1 = last_stage(own, bre, bim, field, ft3, x1, 1)
    x1_later = [piece.reshape((CHUNKS - 1) * PIECE, LANES) for piece in exchange(pieces)]

    x1_first[0] = after(x1_first[0], x1)
    keep, b1s, norms, dx_early = None, [], [], []
    for chunk in range(CHUNKS - 1):
        results = feed(own, x1_later if chunk else x1_first, g, weights, stats, keep, chunk)
        keep = results[:7]
        dx_early.append(exchange(results[7:11]))
        b1s.append(results[11])
        norms.append(results[12])
    results = feed_forward(own, x1_later, weights, stats, keep[:4], CHUNKS - 1)
    hh, hl, nh, nl, tip = results[:5]
    branch = lax.all_to_all(after(keep[4], hh), "blk", 0, 0)
    send2, held2 = weight_grads(own, place, dp_size, [after(g, *dx_early[0][1:], *dx_early[1][1:])], hh, hl, 20)
    local = list(results[5:])
    local[1] = after(local[1], held2)
    results = feed_backward(own, g, weights, local, stats, keep[5:7], CHUNKS - 1)
    ph, plo = results[:2]
    b1s.append(results[6])
    norms.append(results[7])
    got2 = after(held2, ph) + swap(send2, "blk", PARTS, 1)
    dx_all = dx_early + [exchange(results[2:6])]
    dx_all = [v.reshape(SLABS, SMAX, LANES) for group in dx_all for v in group]
    tip = lax.all_to_all(after(tip, ph), "blk", 0, 0)
    ph = after(ph, got2, branch)
    send1, held1 = weight_grads(own, place, dp_size, [nh, nl], ph, plo, 20)

    half, cut = dp_size // 2, send1.shape[2] // 2
    mine2 = got2[:, :half] + swap(got2[:, half:], "dp", dp_size, 1)
    got1 = after(held1, *dx_all[-3:]) + swap(send1, "blk", PARTS, 1)
    dx_all[0] = after(dx_all[0], mine2, tip)
    d, dx = first_back(own, dx_all, f6)
    mine2 = after(mine2[0], d) + swap(mine2[1], "blk", PARTS, 2)
    block_output = output_stage(
        item_sides,
        after(x1, d),
        branch.reshape(PARTS, CHUNKS - 1, SLABS, SMAX, LANES),
        tip.reshape(PARTS, SLABS, SMAX, LANES),
        mlp_b2.reshape(1, LANES),
    )
    early = mix_backward(after(d, got1, mine2, block_output), a, p, o, g6, w1t, w2t, gt3, None, None)
    kept = after(got1, early[0])
    one = kept[:, :half, :cut] + swap(got1[:, half:, :cut], "dp", dp_size, 1)
    two = kept[0, :, cut:] + swap(got1[1, :, cut:], "blk", PARTS, 2)
    second = scatter_last(after(mine2, d), dp_size, early[0])
    d_late = after(d, early[0], second, one, two)
    late = mix_backward(d_late, a, p, o, g6, w1t, w2t, gt3, early[2:], grad_b2)
    near2 = gather_near(after(second, early[0]), dp_size, late[0])
    one = after(one[0], late[0]) + swap(one[1], "blk", PARTS, 2)
    two = after(two[:half], late[0]) + swap(two[half:], "dp", dp_size, 1)
    quarters = [early[0], late[0], early[1], late[1]]
    dx_gated = after(dx, near2, one, two)
    dn, pack, *sums = last_back(quarters, dx_gated, xhat, gain1, ft3, late[2], b1s, norms)
    first = scatter_last(jnp.concatenate([one, two], axis=1), dp_size, dn)
    far2 = swap(after(near2, late[0]), "dp", dp_size, 1)
    sums = exchange([after(value, first) for value in sums])
    input_grad = final_stage(item_sides, after(dx, far2), dn, xhat, sums, r, gain1)
    tail = sums[0][-1] + sums[1][-1] + sums[2][-1] + sums[3][-1]
    pack = jnp.concatenate([pack, tail], axis=0)
    near1 = gather_near(first, dp_size, input_grad)
    pack = after(pack, input_grad) + swap(pack, "dp", dp_size, 1)
    distance = 2
    while distance < dp_size:
        pack = pack + swap(pack, "dp", dp_size, distance)
        distance *= 2
    far1 = swap(near1, "dp", dp_size, 1)
    w1_grad = assemble(place, near1, far1, False)
    w2_grad = assemble(place, near2, far2, True)

    spec = pack[: 4 * FREQ].reshape(2, 2, FREQ, 2, FREQ).transpose(0, 1, 3, 2, 4)
    rest = pack[4 * FREQ :]
    return (
        block_output.reshape(SMAX * SMAX, LANES),
        input_grad.reshape(SMAX * SMAX, LANES),
        rest[5],
        rest[6],
        spec[0],
        rest[0:2].reshape(2, 2, 64),
        spec[1],
        rest[2:4].reshape(2, 2, 64),
        rest[12],
        rest[13],
        w1_grad,
        rest[8:12].reshape(HID),
        w2_grad,
        rest[4],
    )


def solution(mesh):
    in_specs = (
        P("dp", "blk"),
        P("dp", "blk"),
        P("dp"),
        P("dp"),
        P("blk"),
        P("blk"),
        P(None, "blk", None, None),
        P(None, "blk", None),
        P(None, "blk", None, None),
        P(None, "blk", None),
        P("blk"),
        P("blk"),
        P(None, "blk"),
        P("blk"),
        P("blk", None),
        P("blk"),
    )
    out_specs = (
        P("dp", "blk"),
        P("dp", "blk"),
        P("blk"),
        P("blk"),
        P(None, "blk", None, None),
        P(None, "blk", None),
        P(None, "blk", None, None),
        P(None, "blk", None),
        P("blk"),
        P("blk"),
        P(None, "blk"),
        P("blk"),
        P("blk", None),
        P("blk"),
    )
    return jax.shard_map(
        functools.partial(per_device, mesh.shape["dp"]),
        mesh=mesh,
        in_specs=in_specs,
        out_specs=out_specs,
        check_vma=False,
    )
```

```python
import functools
import math

import jax
import jax.numpy as jnp
from jax import lax
from jax.experimental import pallas as pl
from jax.experimental.pallas import tpu as pltpu
from jax.sharding import PartitionSpec as P

C = 512
MODES = 32
SMAX = 96
LANES = 128
FREQ = 64
HALF = 32
PARTS = 4
CHUNKS = 3
SLABS = SMAX // (PARTS * CHUNKS)
PIECE = SLABS * SMAX
GROUP = PARTS * SLABS
STEPS = SMAX // SLABS
STAGE = 24
THIRDS = STAGE // SLABS
WIDTH = 8
BATCH = 8
TILE = 256
SUB = 768
HID = 512
PACK = 4 * FREQ + 8

EPS = 1e-05
SHRINK = 0.01
F32 = jnp.float32
BF16 = jnp.bfloat16
NN = (((1,), (0,)), ((), ()))
NT = (((1,), (1,)), ((), ()))
TN = (((0,), (0,)), ((), ()))
LIMIT = 56 * 1024 * 1024


def mm(left, right, dims=NN):
    return lax.dot_general(left, right, dims, preferred_element_type=F32)


def split2(value):
    high = value.astype(BF16)
    return high, (value - high.astype(F32)).astype(BF16)


def split3(value):
    high = value.astype(BF16)
    rest = value - high.astype(F32)
    mid = rest.astype(BF16)
    return high, mid, (rest - mid.astype(F32)).astype(BF16)


def left6(value):
    one, two, three = split3(value)
    return jnp.concatenate([one, one, two, one, two, three], axis=1)


def right6(value):
    one, two, three = split3(value)
    return jnp.concatenate([one, two, one, three, two, one], axis=0)


def left3(value):
    one, two = split2(value)
    return jnp.concatenate([one, one, two], axis=1)


def right3(value):
    one, two = split2(value)
    return jnp.concatenate([one, two, one], axis=0)


def phi_pair(value):
    cdf = 0.5 + 0.5 * lax.erf(value * math.sqrt(0.5))
    pdf = jnp.exp(value * value * -0.5) * (1.0 / math.sqrt(2.0 * math.pi))
    return cdf, pdf


def pad_rows(value):
    return jnp.concatenate([value, jnp.zeros((LANES - SMAX, value.shape[1]), F32)], axis=0)


def fold_rows(value):
    return jnp.sum(value.reshape(-1, 8, value.shape[-1]), axis=0)


def spread8(rows):
    one, two, three = split3(rows)
    parts = [value.astype(F32) for value in (one, two, three)]
    left = jnp.concatenate(parts + [jnp.zeros_like(rows)], axis=0).astype(BF16)
    index = lax.broadcasted_iota(jnp.int32, (32, SLABS * LANES), 0)
    lane = lax.broadcasted_iota(jnp.int32, (32, SLABS * LANES), 1)
    pick = (index % SLABS == lane // LANES) & (index < 3 * SLABS)
    return mm(left, jnp.where(pick, 1.0, 0.0).astype(BF16), TN)


def slab_of(wide, slab):
    return wide[:SMAX, slab * LANES : (slab + 1) * LANES]


def us(time):
    return (int(time * 1e9), int(time * 3e6))


def call(body, out_shape, in_specs, out_specs, grid=(), scratch=(), aliases=None, cost=None):
    flops, moved = cost or (0, 0)
    return pl.pallas_call(
        body,
        out_shape=out_shape,
        grid=grid,
        in_specs=in_specs,
        out_specs=out_specs,
        scratch_shapes=list(scratch),
        input_output_aliases=aliases or {},
        compiler_params=pltpu.CompilerParams(vmem_limit_bytes=LIMIT),
        cost_estimate=pl.CostEstimate(flops=flops, bytes_accessed=moved, transcendentals=0),
    )


SMEM = pl.BlockSpec(memory_space=pltpu.SMEM)
VMEM = pl.BlockSpec(memory_space=pltpu.VMEM)
ANY = pl.BlockSpec(memory_space=pl.ANY)


def whole(shape):
    zeros = (0,) * len(shape)
    return pl.BlockSpec(shape, lambda *_: zeros)


def sds(shape, dtype=F32):
    return jax.ShapeDtypeStruct(shape, dtype)


def table(item_sides, item_modes):
    row = lax.broadcasted_iota(jnp.int32, (LANES, LANES), 0)
    cell = lax.broadcasted_iota(jnp.int32, (LANES, LANES), 1)
    index = row % FREQ
    frequency = index - (MODES - 1)
    extent = item_sides[0]
    phase = frequency * cell % extent
    keep = (jnp.abs(frequency) < item_modes[0]) & (cell < extent) & (index < 2 * MODES - 1)
    length = extent.astype(F32)
    angle = 2.0 * math.pi * phase.astype(F32) / length
    wave = jnp.where(row < FREQ, jnp.cos(angle), -jnp.sin(angle)) * lax.rsqrt(length)
    return jnp.where(keep, wave, jnp.zeros_like(wave))


def big_weight(weight, out):
    out[...] = jnp.zeros_like(out)
    for block in range(2):
        rows = pl.ds(block * 64, 64)
        later = pl.ds(128 + block * 64, 64)
        out[rows, rows] = weight[0, block]
        out[rows, later] = weight[1, block]
        out[later, rows] = -weight[1, block]
        out[later, later] = weight[0, block]


def prepare_body(f_ref, w1_ref, w2_ref, f6, g6, ft3, gt3, w1c, w2c, w1t, w2t, big):
    full = f_ref[...]
    cosine, sine = full[:FREQ], full[FREQ:]
    half = jnp.concatenate([cosine[HALF - 1 : FREQ - 1], sine[HALF - 1 : FREQ - 1]], axis=0)
    f6[...] = left6(half)
    ft3[...] = left3(half.T)
    lines = [(cosine, -sine), (sine, cosine), (cosine, sine), (sine, -cosine)]
    table_ = jnp.concatenate([jnp.concatenate(line, axis=1) for line in lines], axis=0)
    g6[...] = left6(table_)
    gt3[...] = left3(table_.T)
    for source, straight, across in ((w1_ref, w1c, w1t), (w2_ref, w2c, w2t)):
        big_weight(source, big)
        straight[...] = right6(big[...])
        across[...] = right3(big[...].T)


def prepare(forward, spec_w1, spec_w2):
    shapes = [
        sds((64, 768), BF16),
        sds((256, 1536), BF16),
        sds((128, 192), BF16),
        sds((256, 768), BF16),
        sds((1536, 256), BF16),
        sds((1536, 256), BF16),
        sds((768, 256), BF16),
        sds((768, 256), BF16),
    ]
    return call(
        prepare_body,
        shapes,
        [VMEM] * 3,
        [VMEM] * 8,
        scratch=[pltpu.VMEM((256, 256), F32)],
        cost=us(3),
    )(forward, spec_w1, spec_w2)


def slab_mask(first, side):
    cell = lax.broadcasted_iota(jnp.int32, (SMAX, LANES), 0)
    return (cell < side) & (first < side)


def moments_body(side_ref, x_ref, b1_ref, gain_ref, bias_ref, out_ref):
    step = pl.program_id(0)
    side = side_ref[0]

    @pl.when(step == 0)
    def _():
        vectors = [b1_ref[...], gain_ref[...], bias_ref[...], jnp.zeros((2, LANES), F32)]
        out_ref[2 * STEPS] = jnp.concatenate(vectors, axis=0)

    for slab in range(STAGE):
        inside = slab_mask(step * STAGE + slab, side)
        value = pad_rows(jnp.where(inside, x_ref[slab], 0.0)).T
        mean = jnp.sum(value, axis=0, keepdims=True) * (1.0 / LANES)
        centered = value - mean
        block, row = step * THIRDS + slab // SLABS, pl.ds(slab % SLABS, 1)
        out_ref[block, row, :] = mean
        out_ref[STEPS + block, row, :] = jnp.sum(centered * centered, axis=0, keepdims=True)


def moments(side, x, b1, gain, bias):
    return call(
        moments_body,
        sds((2 * STEPS + 1, SLABS, LANES)),
        [
            SMEM,
            pl.BlockSpec((STAGE, SMAX, LANES), lambda i: (i, 0, 0)),
            whole((4, LANES)),
            whole((1, LANES)),
            whole((1, LANES)),
        ],
        whole((2 * STEPS + 1, SLABS, LANES)),
        grid=(SMAX // STAGE,),
        cost=us(6),
    )(side, x, b1, gain, bias)


def cotangent_body(side_ref, g_ref, early, late, total):
    chunk = pl.program_id(0)
    side = side_ref[0]

    @pl.when(chunk == 0)
    def _():
        total[...] = jnp.zeros_like(total)

    def emit(out_ref):
        carry = jnp.zeros((8, LANES), F32)
        for part in range(PARTS):
            for slab in range(SLABS):
                first = part * SLABS + slab
                value = jnp.where(slab_mask(chunk * GROUP + first, side), g_ref[first], 0.0)
                out_ref[part, 0, slab] = value
                carry = carry + fold_rows(value)
        total[...] += carry

    @pl.when(chunk < CHUNKS - 1)
    def _():
        emit(early)

    @pl.when(chunk == CHUNKS - 1)
    def _():
        emit(late)


def cotangent_pieces(side, g):
    block = (PARTS, 1, SLABS, SMAX, LANES)
    return call(
        cotangent_body,
        [sds((PARTS, CHUNKS - 1, SLABS, SMAX, LANES)), sds(block), sds((8, LANES))],
        [SMEM, pl.BlockSpec((GROUP, SMAX, LANES), lambda i: (i, 0, 0))],
        [
            pl.BlockSpec(block, lambda i: (0, jnp.minimum(i, CHUNKS - 2), 0, 0, 0)),
            whole(block),
            whole((8, LANES)),
        ],
        grid=(CHUNKS,),
        cost=us(5),
    )(side, g)


def row_stats(means, totals):
    mean = (means[0] + means[1] + means[2] + means[3]) * (1.0 / PARTS)
    total = totals[0] + totals[1] + totals[2] + totals[3]
    for part in range(PARTS):
        gap = means[part] - mean
        total = total + LANES * (gap * gap)
    spread_ = total * (1.0 / C) + EPS
    inverse = lax.rsqrt(spread_)
    inverse = inverse * (1.5 - 0.5 * spread_ * inverse * inverse)
    return mean, inverse


def first_body(side_ref, x_ref, *refs):
    stats = refs[:PARTS]
    gain_ref, bias_ref, f6_ref, b_ref, xn_ref, xhat_ref, r_ref = refs[PARTS:]
    step = pl.program_id(0)
    side = side_ref[0]
    gain, bias = gain_ref[...], bias_ref[...]
    for third in range(THIRDS):
        block = step * THIRDS + third
        mean, inverse = row_stats([ref[block] for ref in stats], [ref[STEPS + block] for ref in stats])
        r_ref[pl.ds(third * SLABS, SLABS), :] = inverse
        means, scales = spread8(mean), spread8(inverse)
        columns = []
        for inner in range(SLABS):
            slab = third * SLABS + inner
            value = jnp.where(slab_mask(step * STAGE + slab, side), x_ref[slab], 0.0)
            centered = value - slab_of(means, inner)
            normal = centered * slab_of(scales, inner)
            normed = normal * gain + bias
            xhat_ref[slab] = normal
            xn_ref[slab] = value + normed
            columns.append(pad_rows(normed))
        out = mm(f6_ref[...], right6(jnp.concatenate(columns, axis=1)))
        for inner in range(SLABS):
            b_ref[third * SLABS + inner] = out[:, part_lanes(inner)]


def first_stage(side, x, stats, gain, bias, f6):
    field = pl.BlockSpec((STAGE, SMAX, LANES), lambda i: (i, 0, 0))
    return call(
        first_body,
        [sds((SMAX, FREQ, LANES)), sds((SMAX, SMAX, LANES)), sds((SMAX, SMAX, LANES)), sds((SMAX, LANES))],
        [SMEM, field]
        + [whole((2 * STEPS + 1, SLABS, LANES))] * PARTS
        + [whole((1, LANES)), whole((1, LANES)), whole((64, 768))],
        [
            pl.BlockSpec((STAGE, FREQ, LANES), lambda i: (i, 0, 0)),
            field,
            field,
            pl.BlockSpec((STAGE, LANES), lambda i: (i, 0)),
        ],
        grid=(SMAX // STAGE,),
        cost=us(3),
    )(side, x, *stats, gain, bias, f6)


def gather_columns(re_ref, im_ref, first):
    zeros = jnp.zeros((LANES - SMAX, LANES), F32)
    re, im = [ref.reshape(SMAX * WIDTH, LANES) for ref in (re_ref, im_ref)]
    columns = []
    for j in range(first, first + BATCH):
        rows = pl.ds(j, SMAX, stride=WIDTH)
        columns.append(jnp.concatenate([re[rows, :], zeros, im[rows, :], zeros], axis=0))
    return jnp.concatenate(columns, axis=1)


def to_rows(out):
    rows = []
    for j in range(BATCH):
        lanes = part_lanes(j)
        for base in (0, 2 * FREQ):
            parts = [out[base : base + FREQ, lanes], out[base + FREQ : base + 2 * FREQ, lanes]]
            rows.append(jnp.concatenate(parts, axis=1))
    return jnp.concatenate(rows, axis=0)


def to_columns(rows):
    columns = []
    for j in range(BATCH):
        parts = []
        for sign in range(2):
            first = (2 * j + sign) * FREQ
            part = rows[first : first + FREQ]
            parts += [part[:, :LANES], part[:, LANES:]]
        columns.append(jnp.concatenate(parts, axis=0))
    return jnp.concatenate(columns, axis=1)


def counted(step, half, shape):
    row = lax.broadcasted_iota(jnp.int32, shape, 0)
    twice = (step == 0) & (half == 0)
    return (row < FREQ) | (row >= 2 * FREQ) | jnp.logical_not(twice)


def scatter_columns(re_ref, im_ref, first, out):
    re, im = [ref.reshape(SMAX * WIDTH, LANES) for ref in (re_ref, im_ref)]
    for j in range(BATCH):
        lanes = slice(j * LANES, (j + 1) * LANES)
        rows = pl.ds(first + j, SMAX, stride=WIDTH)
        re[rows, :] = out[:SMAX, lanes]
        im[rows, :] = out[LANES : LANES + SMAX, lanes]


def shrink(value):
    return jnp.where(
        value > SHRINK,
        value - SHRINK,
        jnp.where(value < -SHRINK, value + SHRINK, jnp.zeros_like(value)),
    )


def mix_body(re_ref, im_ref, g6_ref, w1_ref, b1_ref, w2_ref, b2_ref, gt3_ref, bre, bim, a_out, p_out, o_out):
    for half in range(WIDTH // BATCH):
        rows = pl.ds(half * 2 * BATCH * FREQ, 2 * BATCH * FREQ)
        spectrum = to_rows(mm(g6_ref[...], right6(gather_columns(re_ref, im_ref, BATCH * half))))
        a_out[rows, :] = spectrum
        pre = mm(left6(spectrum), w1_ref[...]) + b1_ref[...]
        p_out[rows, :] = pre
        cdf = 0.5 + 0.5 * lax.erf(pre * math.sqrt(0.5))
        out = mm(left6(pre * cdf), w2_ref[...]) + b2_ref[...]
        o_out[rows, :] = out
        if half == 0:
            out = jnp.where(counted(pl.program_id(0), half, out.shape), out, 0.0)
        scatter_columns(bre, bim, BATCH * half, mm(gt3_ref[...], right3(to_columns(shrink(out)))))


def mix_forward(b, g6, w1c, bias1, w2c, bias2, gt3):
    count = HALF // WIDTH
    re = pl.BlockSpec((SMAX, WIDTH, LANES), lambda j: (0, j, 0))
    im = pl.BlockSpec((SMAX, WIDTH, LANES), lambda j: (0, count + j, 0))
    out = pl.BlockSpec((SMAX, WIDTH, LANES), lambda j: (0, j, 0))
    rows = pl.BlockSpec((2 * WIDTH * FREQ, 256), lambda j: (j, 0))
    half = sds((SMAX, HALF, LANES))
    return call(
        mix_body,
        [half, half] + [sds((4096, 256))] * 3,
        [
            re,
            im,
            whole((256, 1536)),
            whole((1536, 256)),
            whole((1, 256)),
            whole((1536, 256)),
            whole((1, 256)),
            whole((256, 768)),
        ],
        [out, out, rows, rows, rows],
        grid=(count,),
        cost=us(0.1),
    )(b, b, g6, w1c, bias1, w2c, bias2, gt3)


def last_body(own_ref, re_ref, im_ref, xn_ref, ft3_ref, *refs):
    full, outs = refs[-1], refs[-1 - PARTS : -1]
    own = own_ref[0]
    for part in range(PARTS):
        base = (own ^ part) * SLABS
        columns = [jnp.concatenate([re_ref[base + s], im_ref[base + s]], axis=0) for s in range(SLABS)]
        out = mm(ft3_ref[...], right3(jnp.concatenate(columns, axis=1)))[:SMAX]
        for s in range(SLABS):
            value = xn_ref[base + s] + out[:, part_lanes(s)]
            full[base + s] = value
            if len(outs[part].shape) == 3:
                outs[part][s] = value
            else:
                outs[part][0, s] = value


def last_stage(own, bre, bim, xn, ft3, keep, chunk):
    half = pl.BlockSpec((GROUP, HALF, LANES), lambda i: (chunk + i, 0, 0))
    field = pl.BlockSpec((GROUP, SMAX, LANES), lambda i: (chunk + i, 0, 0))
    args = [own, bre, bim, xn, ft3]
    in_specs = [SMEM, half, half, field, whole((128, 192))]
    aliases = {}
    steps = 1 if chunk == 0 else CHUNKS - 1
    if keep is not None:
        aliases[len(args)] = PARTS
        args.append(keep)
        in_specs.append(ANY)
    piece = (SLABS, SMAX, LANES)
    shape = piece if chunk == 0 else (steps,) + piece
    spec = whole(piece)
    if chunk > 0:
        spec = pl.BlockSpec((1,) + piece, lambda i: (i, 0, 0, 0))
    *pieces, full = call(
        last_body,
        [sds(shape)] * PARTS + [sds((SMAX, SMAX, LANES))],
        in_specs,
        [spec] * PARTS + [field],
        grid=(steps,),
        aliases=aliases,
        cost=us(0.1 * steps),
    )(*args)
    return pieces, full


def weights_body(own_ref, *refs):
    step = pl.program_id(0)
    own = own_ref[0]
    one, two = refs[0:2], refs[2:4]
    far = refs[4:6]
    w1h, w1l, w2h, w2l = refs[6:]

    def emit(first, second):
        for part in range(PARTS):
            source = pl.ds(pl.multiple_of((own ^ part) * LANES, LANES), LANES)
            target = slice(part * LANES, (part + 1) * LANES)
            w1h[0, target, :], w1l[0, target, :] = split2(first(source))
            w2h[0, :, target], w2l[0, :, target] = split2(second(source))

    for index in range(2):

        @pl.when(step == index)
        def _(index=index):
            emit(lambda rows: one[index][rows, :], lambda lanes: two[index][:, lanes])

        @pl.when(step == 2 + index)
        def _(index=index):
            ref = far[index]
            depth = ref.shape[0] // PARTS

            def rows_of(rows):
                first = pl.multiple_of(rows.start // ref.shape[2], depth)
                return ref[pl.ds(first, depth), 0].reshape(LANES, 512)

            emit(rows_of, lambda lanes: ref[:, 1, :, lanes].reshape(512, LANES))


def split_weights(own, one, two, far):
    block = pl.BlockSpec((1, 512, 512), lambda i: (i, 0, 0))
    return call(
        weights_body,
        [sds((4, 512, 512), BF16)] * 4,
        [SMEM] + [whole((512, 512))] * 4 + [whole(far[0].shape)] * 2,
        [block] * 4,
        grid=(4,),
        cost=us(0.1),
    )(own, *one, *two, *far)


def row_mean(parts):
    total = parts[0] + parts[1] + parts[2] + parts[3]
    return jnp.sum(total, axis=1, keepdims=True) * (1.0 / C)


def part_lanes(part):
    return slice(part * LANES, (part + 1) * LANES)


def norm_tiles(load, vectors, n_h, n_l, nh, nl, xhat, scale):
    def norm(tile, carry):
        rows = pl.ds(tile * TILE, TILE)
        values = [load(part, rows) for part in range(PARTS)]
        mean = row_mean(values)
        centered = [value - mean for value in values]
        spread_ = row_mean([value * value for value in centered]) + EPS
        inverse = lax.rsqrt(spread_)
        inverse = inverse * (1.5 - 0.5 * spread_ * inverse * inverse)
        scale[rows, :] = jnp.broadcast_to(inverse, (TILE, LANES))
        for part in range(PARTS):
            lanes = part_lanes(part)
            normal = centered[part] * inverse
            xhat[rows, lanes] = normal
            gain, bias = vectors[part][0, 4:5, :], vectors[part][0, 5:6, :]
            high, low = split2(normal * gain + bias)
            n_h[rows, lanes] = high
            n_l[rows, lanes] = low
            nh[rows, lanes] = high
            nl[rows, lanes] = low
        return carry

    lax.fori_loop(0, PIECE // TILE, norm, 0)


def bias_of(vectors, step):
    row = jnp.zeros((4, LANES), F32)
    for part in range(PARTS):
        row = jnp.where(step == part, vectors[part][0, 0:4, :], row)
    return jnp.concatenate([row[i : i + 1] for i in range(4)], axis=1)


def grad_tiles(own, g_ref, vectors, dn, xhat, scale, store, small):
    small[...] = jnp.zeros_like(small)

    def back(tile, carry):
        rows = pl.ds(tile * TILE, TILE)
        inverse = scale[rows, :]
        scaled, normals = [], []
        for part in range(PARTS):
            lanes = part_lanes(part)
            grad = dn[rows, lanes]
            normal = xhat[rows, lanes]
            small[0, :, lanes] += fold_rows(grad * normal)
            small[1, :, lanes] += fold_rows(grad)
            scaled.append(grad * vectors[part][0, 4:5, :])
            normals.append(normal)
        first = row_mean(scaled)
        second = row_mean([s * n for s, n in zip(scaled, normals)])
        for part in range(PARTS):
            delta = inverse * (scaled[part] - first - normals[part] * second)
            store(part, rows, g_ref[own ^ part, rows, :] + delta)
        return carry

    lax.fori_loop(0, PIECE // TILE, back, 0)


def split_cotangent(own, g_ref, g_h, g_l):
    for part in range(PARTS):
        lanes = part_lanes(part)
        g_h[:, lanes], g_l[:, lanes] = split2(g_ref[own ^ part])


def product3(high, low, w_h, w_l, dims=NN):
    return mm(high, w_h[0], dims) + mm(low, w_h[0], dims) + mm(high, w_l[0], dims)


def add_to(ref, step, value):
    ref[...] = jnp.where(step == 0, 0.0, ref[...]) + value


def feed_body(*refs):
    own = refs[0][0]
    x_refs, g_ref = refs[1:5], refs[5]
    w1h, w1l, w2h, w2l = refs[6:10]
    vectors = refs[10:14]
    refs = refs[len(refs) - 21 :]
    hh, hl, nh, nl, out_ref, ph, plo = refs[0:7]
    dx_refs, db1, small = refs[7:11], refs[11], refs[12]
    n_h, n_l, g_h, g_l, xhat, scale, dn, acc = refs[13:21]
    step = pl.program_id(0)

    @pl.when(step == 0)
    def _():
        norm_tiles(lambda part, rows: x_refs[part][rows, :], vectors, n_h, n_l, nh, nl, xhat, scale)
        split_cotangent(own, g_ref, g_h, g_l)

    pre = product3(n_h[...], n_l[...], w1h, w1l) + bias_of(vectors, step)
    dh = product3(g_h[...], g_l[...], w2h, w2l, NT)
    cdf, pdf = phi_pair(pre)
    high, low = split2(pre * cdf)
    hh[...] = high
    hl[...] = low
    grad = dh * (cdf + pre * pdf)
    add_to(acc, step, product3(high, low, w2h, w2l))
    high, low = split2(grad)
    ph[...] = high
    plo[...] = low
    db1[0] = fold_rows(grad)
    add_to(dn, step, product3(high, low, w1h, w1l, NT))

    @pl.when(step == pl.num_programs(0) - 1)
    def _():
        for part in range(PARTS):
            out_ref[own ^ part, 0] = acc[:, part_lanes(part)]

        def store(part, rows, value):
            dx_refs[part][rows, :] = value

        grad_tiles(own, g_ref, vectors, dn, xhat, scale, store, small)


def forward_body(*refs):
    own = refs[0][0]
    x_refs = refs[1:5]
    w1h, w1l, w2h, w2l = refs[5:9]
    vectors = refs[9:13]
    hh, hl, nh, nl, out_ref, slope, xhat, scale, n_h, n_l, acc = refs[len(refs) - 11 :]
    step = pl.program_id(0)

    @pl.when(step == 0)
    def _():
        norm_tiles(lambda part, rows: x_refs[part][rows, :], vectors, n_h, n_l, nh, nl, xhat, scale)

    pre = product3(n_h[...], n_l[...], w1h, w1l) + bias_of(vectors, step)
    cdf, pdf = phi_pair(pre)
    slope[...] = cdf + pre * pdf
    high, low = split2(pre * cdf)
    hh[...] = high
    hl[...] = low
    add_to(acc, step, product3(high, low, w2h, w2l))

    @pl.when(step == pl.num_programs(0) - 1)
    def _():
        for part in range(PARTS):
            out_ref[own ^ part, 0] = acc[:, part_lanes(part)]


def backward_body(*refs):
    own = refs[0][0]
    g_ref, w1h, w1l, w2h, w2l, slope, xhat, scale = refs[1:9]
    vectors = refs[9:13]
    refs = refs[len(refs) - 11 :]
    ph, plo, dx_refs, db1, small = refs[0], refs[1], refs[2:6], refs[6], refs[7]
    g_h, g_l, dn = refs[8:]
    step = pl.program_id(0)

    @pl.when(step == 0)
    def _():
        split_cotangent(own, g_ref, g_h, g_l)

    grad = product3(g_h[...], g_l[...], w2h, w2l, NT) * slope[...]
    high, low = split2(grad)
    ph[...] = high
    plo[...] = low
    db1[0] = fold_rows(grad)
    add_to(dn, step, product3(high, low, w1h, w1l, NT))

    @pl.when(step == pl.num_programs(0) - 1)
    def _():

        def store(part, rows, value):
            dx_refs[part][rows, :] = value

        grad_tiles(own, g_ref, vectors, dn, xhat, scale, store, small)


def feed_call(body, head, heads, weights, stats, local, keep, kinds, chunk, cost):
    rows = PIECE * CHUNKS
    specs = {
        "x": (sds((PIECE, LANES)), whole((PIECE, LANES))),
        "later": (None, pl.BlockSpec((PIECE, LANES), lambda i: (chunk - 1, 0))),
        "g": (None, pl.BlockSpec((PARTS, PIECE, LANES), lambda i: (0, chunk, 0))),
        "g2": (None, whole((PARTS, PIECE, LANES))),
        "out": (
            sds((PARTS, CHUNKS - 1, PIECE, LANES)),
            pl.BlockSpec((PARTS, 1, PIECE, LANES), lambda i: (0, chunk, 0, 0)),
        ),
        "wide": (sds((rows, 2048), BF16), pl.BlockSpec((PIECE, HID), lambda i: (chunk, i))),
        "narrow": (sds((rows, C), BF16), pl.BlockSpec((PIECE, C), lambda i: (chunk, 0))),
        "slope": (sds((PIECE, 2048)), pl.BlockSpec((PIECE, HID), lambda i: (0, i))),
        "tip": (sds((PARTS, 1, PIECE, LANES)), whole((PARTS, 1, PIECE, LANES))),
        "full": (sds((PIECE, C)), whole((PIECE, C))),
        "db1": (sds((4, 8, HID)), pl.BlockSpec((1, 8, HID), lambda i: (i, 0, 0))),
        "small": (sds((2, 8, C)), whole((2, 8, C))),
    }
    weight = pl.BlockSpec((1, 512, 512), lambda i: (i, 0, 0))
    vector = pl.BlockSpec((1, SLABS, LANES), lambda i: (2 * STEPS, 0, 0))
    args = [*head, *weights, *(value for _, value in local), *stats]
    in_specs = [SMEM] + [specs[kind][1] for kind in heads] + [weight] * 4
    in_specs += [specs[kind][1] for kind, _ in local] + [vector] * 4
    aliases = {}
    for index, array in enumerate(keep or ()):
        aliases[len(args)] = index
        args.append(array)
        in_specs.append(ANY)
    bf, big = pltpu.VMEM((PIECE, C), BF16), pltpu.VMEM((PIECE, C), F32)
    scratch = {
        "feed": [bf] * 4 + [big, pltpu.VMEM((PIECE, LANES), F32), big, big],
        "fore": [bf, bf, big],
        "back": [bf, bf, big],
    }[kinds]
    outs = {
        "feed": ["wide"] * 2 + ["narrow"] * 2 + ["out", "wide", "wide"] + ["x"] * 4 + ["db1", "small"],
        "fore": ["wide"] * 2 + ["narrow"] * 2 + ["tip", "slope", "full", "x"],
        "back": ["wide", "wide"] + ["x"] * 4 + ["db1", "small"],
    }[kinds]
    return call(
        body,
        [specs[kind][0] for kind in outs],
        in_specs,
        [specs[kind][1] for kind in outs],
        grid=(4,),
        scratch=scratch,
        aliases=aliases,
        cost=us(cost),
    )(*args)


def feed(own, xs, g, weights, stats, keep, chunk):
    head, heads = [own, *xs, g], ["x" if chunk == 0 else "later"] * 4 + ["g"]
    return feed_call(feed_body, head, heads, weights, stats, [], keep, "feed", chunk, 28)


def feed_forward(own, xs, weights, stats, keep, chunk):
    return feed_call(forward_body, [own, *xs], ["later"] * 4, weights, stats, [], keep, "fore", chunk, 18)


def feed_backward(own, g, weights, local, stats, keep, chunk):
    local = list(zip(("slope", "full", "x"), local))
    return feed_call(backward_body, [own, g], ["g2"], weights, stats, local, keep, "back", chunk, 16)


def weight_body(own_ref, place_ref, th, tl, *refs):
    send, held, t_h, t_l = refs[-4:]
    step = pl.program_id(0)
    own, place = own_ref[0], place_ref[0]

    @pl.when(step == 0)
    def _():
        if len(refs[0].shape) == 2:
            t_h[...] = refs[0][...].T
            t_l[...] = refs[1][...].T
        else:
            for part in range(PARTS):
                pieces = [ref[own ^ part] for ref in refs[:2]]
                high, low = split2(jnp.concatenate(pieces, axis=0))
                t_h[part_lanes(part), :] = high.T
                t_l[part_lanes(part), :] = low.T

    out = mm(t_h[...], th[...]) + mm(t_l[...], th[...]) + mm(t_h[...], tl[...])
    count, depth = send.shape[1], send.shape[2]

    def store(ref):
        for index in range(count):
            part, inner = divmod(index, count // PARTS)
            apart = ((own ^ part) * (count // PARTS) + inner) ^ place
            where = (apart & 1) * (count // 2) + (apart >> 1)
            ref[0, where] = out[index * depth : (index + 1) * depth]

    @pl.when(step < 2)
    def _():
        store(send)

    @pl.when(step >= 2)
    def _():
        store(held)


def weight_grads(own, place, dp_size, left, th, tl, cost):
    rows = PIECE * CHUNKS
    wide = pl.BlockSpec((rows, HID), lambda i: (0, (i % 2) * 2 + 1 - i // 2))
    block = (1, dp_size, C // dp_size, HID)
    shape = sds((2,) + block[1:])
    return call(
        weight_body,
        [shape, shape],
        [SMEM, SMEM]
        + [wide] * 2
        + [pl.BlockSpec(v.shape, lambda i, n=v.ndim: (0,) * n, pipeline_mode=pl.Buffered(1)) for v in left],
        [
            pl.BlockSpec(block, lambda i: (jnp.minimum(i, 1), 0, 0, 0)),
            pl.BlockSpec(block, lambda i: (jnp.maximum(i - 2, 0), 0, 0, 0)),
        ],
        grid=(4,),
        scratch=[pltpu.VMEM((C, rows), BF16)] * 2,
        cost=us(cost),
    )(own, place, th, tl, *left)


def assemble_body(turn, place_ref, near, far, out_ref, held):
    place = place_ref[0]
    half, depth = near.shape[0], near.shape[1]
    target = held if turn else out_ref
    for side, source in enumerate((near, far)):
        for index in range(half):
            rows = pl.ds(pl.multiple_of((place ^ (2 * index + side)) * depth, depth), depth)
            target[rows, :] = source[index]
    if turn:
        out_ref[...] = held[...].T


def assemble(place, near, far, turn):
    return call(
        functools.partial(assemble_body, turn),
        sds((C, HID)),
        [SMEM] + [VMEM] * 2,
        VMEM,
        scratch=[pltpu.VMEM((C, HID), F32)],
        cost=us(2),
    )(place, near, far)


def first_back_body(own_ref, f6_ref, *refs):
    d_ref, dx_ref = refs[-2:]
    own = own_ref[0]
    for chunk in range(CHUNKS):

        @pl.when(pl.program_id(0) == chunk)
        def _(pieces=refs[PARTS * chunk : PARTS * (chunk + 1)]):
            for part in range(PARTS):
                base = (own ^ part) * SLABS
                columns = [pad_rows(pieces[part][s]) for s in range(SLABS)]
                out = mm(f6_ref[...], right3(jnp.concatenate(columns, axis=1)))
                for s in range(SLABS):
                    d_ref[base + s] = out[:, part_lanes(s)]
                    dx_ref[base + s] = pieces[part][s]


def first_back(own, pieces, f6):
    return call(
        first_back_body,
        [sds((SMAX, FREQ, LANES)), sds((SMAX, SMAX, LANES))],
        [SMEM, whole((64, 384))] + [whole(piece.shape) for piece in pieces],
        [
            pl.BlockSpec((GROUP, FREQ, LANES), lambda i: (i, 0, 0)),
            pl.BlockSpec((GROUP, SMAX, LANES), lambda i: (i, 0, 0)),
        ],
        grid=(CHUNKS,),
        cost=us(8),
    )(own, f6, *pieces)


def rows3(value):
    one, two = split2(value)
    return jnp.concatenate([one, one, two], axis=0)


def mix_back_body(*refs):
    re_ref, im_ref, a_ref, p_ref, o_ref, g3_ref, w1t, w2t, gt3_ref = refs[:9]
    sums = refs[-4:]
    dw1, dw2, db1, db2 = sums
    if len(refs) == 15:
        dre, dim = refs[9:11]
    else:
        gb_ref = refs[13]
        dre, dim, pack = refs[14:17]

    @pl.when(pl.program_id(0) == 0)
    def _():
        for index, ref in enumerate(sums):
            ref[...] = jnp.zeros_like(ref) if len(refs) == 15 else refs[9 + index][...]

    for half in range(WIDTH // BATCH):
        rows = pl.ds(half * 2 * BATCH * FREQ, 2 * BATCH * FREQ)
        dz = to_rows(mm(g3_ref[...], right3(gather_columns(re_ref, im_ref, BATCH * half))))
        do = jnp.where(jnp.abs(o_ref[rows, :]) > SHRINK, dz, 0.0)
        if half == 0 and len(refs) == 15:
            do = jnp.where(counted(pl.program_id(0), half, do.shape), do, 0.0)
        pre = p_ref[rows, :]
        cdf, pdf = phi_pair(pre)
        dw2[...] += mm(rows3(pre * cdf), right3(do), TN)
        db2[...] += fold_rows(do)
        dp = mm(left3(do), w2t[...]) * (cdf + pre * pdf)
        dw1[...] += mm(rows3(a_ref[rows, :]), right3(dp), TN)
        db1[...] += fold_rows(dp)
        dx = mm(left3(dp), w1t[...])
        if half == 0 and len(refs) == 15:
            dx = jnp.where(counted(pl.program_id(0), half, dx.shape), dx, 0.0)
        scatter_columns(dre, dim, BATCH * half, mm(gt3_ref[...], right3(to_columns(dx))))

    if len(refs) == 15:
        return

    @pl.when(pl.program_id(0) == pl.num_programs(0) - 1)
    def _():
        low = lax.broadcasted_iota(jnp.int32, (FREQ, LANES), 1) < FREQ
        for index, ref in enumerate((dw1, dw2)):
            full = ref[...]
            same = full[:LANES, :LANES] + full[LANES:, LANES:]
            cross = full[:LANES, LANES:] - full[LANES:, :LANES]
            for inner, value in enumerate((same, cross)):
                rows = pl.ds((2 * index + inner) * FREQ, FREQ)
                pack[rows, :] = jnp.where(low, value[:FREQ], value[FREQ:])
        sums = [jnp.sum(ref[...], axis=0, keepdims=True) for ref in (db1, db2)]
        lines = [sums[0][:, :LANES], sums[0][:, LANES:], sums[1][:, :LANES], sums[1][:, LANES:]]
        lines.append(jnp.sum(gb_ref[...], axis=0, keepdims=True))
        pack[4 * FREQ : 4 * FREQ + 8] = jnp.concatenate(lines + [jnp.zeros((3, LANES), F32)], axis=0)


def mix_backward(d, a, p, o, g6, w1t, w2t, gt3, carry, grad_b2):
    count = HALF // WIDTH
    skip = 0 if carry is None else count // 2
    re = pl.BlockSpec((SMAX, WIDTH, LANES), lambda j: (0, skip + j, 0))
    im = pl.BlockSpec((SMAX, WIDTH, LANES), lambda j: (0, count + skip + j, 0))
    out = pl.BlockSpec((SMAX, WIDTH, LANES), lambda j: (0, j, 0))
    rows = pl.BlockSpec((2 * WIDTH * FREQ, 256), lambda j: (skip + j, 0))
    half = sds((SMAX, HALF // 2, LANES))
    args = [d, d, a, p, o, g6, w1t, w2t, gt3]
    in_specs = [re, im, rows, rows, rows, whole((256, 768))]
    in_specs += [whole((768, 256)), whole((768, 256)), whole((256, 768))]
    sums = [(256, 256), (256, 256), (8, 256), (8, 256)]
    shapes, out_specs, scratch = [half, half], [out, out], []
    if carry is None:
        shapes += [sds(shape) for shape in sums]
        out_specs += [whole(shape) for shape in sums]
    else:
        args += [*carry, grad_b2]
        in_specs += [whole(shape) for shape in sums] + [whole((8, LANES))]
        shapes.append(sds((PACK, LANES)))
        out_specs.append(whole((PACK, LANES)))
        scratch = [pltpu.VMEM(shape, F32) for shape in sums]
    return call(
        mix_back_body, shapes, in_specs, out_specs, grid=(count // 2,), scratch=scratch, cost=us(13)
    )(*args)


def last_back_body(re0, re1, im0, im1, dx_ref, xhat_ref, gain_ref, ft3_ref, pack_ref, *refs):
    b1_refs, norm_refs = refs[:CHUNKS], refs[CHUNKS : 2 * CHUNKS]
    dn_ref, pack = refs[2 * CHUNKS : 2 * CHUNKS + 2]
    sums, small = refs[-1 - PARTS : -1], refs[-1]
    step = pl.program_id(0)

    @pl.when(step == 0)
    def _():
        small[...] = jnp.zeros_like(small)
        norms = norm_refs[0][...]
        for ref in norm_refs[1:]:
            norms = norms + ref[...]
        norms = [jnp.sum(norms[i], axis=0, keepdims=True) for i in range(2)]
        for part in range(PARTS):
            total = b1_refs[0][part]
            for ref in b1_refs[1:]:
                total = total + ref[part]
            total = jnp.sum(total, axis=0, keepdims=True)
            lines = [total[:, part_lanes(i)] for i in range(4)]
            lines += [value[:, part_lanes(part)] for value in norms]
            lines.append(jnp.zeros((2, LANES), F32))
            sums[part][2 * STEPS] = jnp.concatenate(lines, axis=0)

    gain = gain_ref[...]
    for third in range(THIRDS):
        slabs = [third * SLABS + inner for inner in range(SLABS)]
        columns = [jnp.concatenate([re0[s], re1[s], im0[s], im1[s]], axis=0) for s in slabs]
        out = mm(ft3_ref[...], right3(jnp.concatenate(columns, axis=1)))[:SMAX]
        for index, s in enumerate(slabs):
            grad = dx_ref[s] + out[:, part_lanes(index)]
            dn_ref[s] = grad
            product = grad * xhat_ref[s]
            small[0] += fold_rows(product)
            small[1] += fold_rows(grad)
            for which, value in enumerate((grad, product)):
                row = jnp.sum(pad_rows(value * gain).T, axis=0, keepdims=True)
                for ref in sums:
                    block = which * STEPS + step * THIRDS + s // SLABS
                    ref[block, pl.ds(s % SLABS, 1), :] = row

    @pl.when(step == pl.num_programs(0) - 1)
    def _():
        pack[...] = pack_ref[...]
        for index in range(2):
            where = pl.ds(4 * FREQ + 5 + index, 1)
            pack[where, :] = jnp.sum(small[index], axis=0, keepdims=True)


def last_back(quarters, dx, xhat, gain, ft3, pack, b1s, norms):
    half = pl.BlockSpec((STAGE, HALF // 2, LANES), lambda i: (i, 0, 0))
    field = pl.BlockSpec((STAGE, SMAX, LANES), lambda i: (i, 0, 0))
    shape = (2 * STEPS + 1, SLABS, LANES)
    return call(
        last_back_body,
        [sds((SMAX, SMAX, LANES)), sds((PACK, LANES))] + [sds(shape)] * PARTS,
        [half] * 4
        + [field, field, whole((1, LANES)), whole((128, 192)), whole((PACK, LANES))]
        + [whole((4, 8, HID))] * CHUNKS
        + [whole((2, 8, C))] * CHUNKS,
        [field, whole((PACK, LANES))] + [whole(shape)] * PARTS,
        grid=(SMAX // STAGE,),
        scratch=[pltpu.VMEM((2, 8, LANES), F32)],
        cost=us(13),
    )(*quarters, dx, xhat, gain, ft3, pack, *b1s, *norms)


def final_body(side_ref, dx_ref, dn_ref, xhat_ref, r_ref, gain_ref, *refs):
    sums, out_ref = refs[:PARTS], refs[PARTS]
    step = pl.program_id(0)
    side = side_ref[0]
    for third in range(THIRDS):
        block = step * THIRDS + third
        inverse = r_ref[pl.ds(third * SLABS, SLABS), :]
        total = [sum(ref[which * STEPS + block] for ref in sums) for which in range(2)]
        first = total[0] * (inverse * (1.0 / C))
        second = total[1] * (inverse * (1.0 / C))
        wide = [spread8(value) for value in (inverse, first, second)]
        for inner in range(SLABS):
            slab = third * SLABS + inner
            scaled = dn_ref[slab] * gain_ref[...]
            scale, shift, slope = [slab_of(value, inner) for value in wide]
            value = dx_ref[slab] + (scale * scaled - shift - xhat_ref[slab] * slope)
            out_ref[slab] = jnp.where(slab_mask(step * STAGE + slab, side), value, 0.0)


def final_stage(side, dx, dn, xhat, sums, r, gain):
    field = pl.BlockSpec((STAGE, SMAX, LANES), lambda i: (i, 0, 0))
    return call(
        final_body,
        sds((SMAX, SMAX, LANES)),
        [SMEM, field, field, field, pl.BlockSpec((STAGE, LANES), lambda i: (i, 0)), whole((1, LANES))]
        + [whole((2 * STEPS + 1, SLABS, LANES))] * PARTS,
        field,
        grid=(SMAX // STAGE,),
        cost=us(13),
    )(side, dx, dn, xhat, r, gain, *sums)


def output_body(side_ref, x_ref, y_ref, tip_ref, b2_ref, out_ref):
    step = pl.program_id(0)
    side = side_ref[0]
    for part in range(PARTS):
        for inner in range(SLABS):
            slab = part * SLABS + inner
            branch = jnp.where(step < CHUNKS - 1, y_ref[part, 0, inner], tip_ref[part, inner])
            value = x_ref[slab] + branch + b2_ref[...]
            out_ref[slab] = jnp.where(slab_mask(step * GROUP + slab, side), value, 0.0)


def output_stage(side, x1, y, tip, b2):
    field = pl.BlockSpec((GROUP, SMAX, LANES), lambda i: (i, 0, 0))
    return call(
        output_body,
        sds((SMAX, SMAX, LANES)),
        [
            SMEM,
            field,
            pl.BlockSpec(
                (PARTS, 1, SLABS, SMAX, LANES), lambda i: (0, jnp.minimum(i, CHUNKS - 2), 0, 0, 0)
            ),
            whole((PARTS, SLABS, SMAX, LANES)),
            whole((1, LANES)),
        ],
        field,
        grid=(CHUNKS,),
        cost=us(5),
    )(side, x1, y, tip, b2)


def swap(value, axis, size, distance):
    return lax.ppermute(value, axis, [(i, i ^ distance) for i in range(size)])


def exchange(pieces):
    return [pieces[0]] + [swap(pieces[part], "blk", PARTS, part) for part in range(1, PARTS)]


def after(value, *others):
    return lax.optimization_barrier((value, *others))[0]


def halve(value, size, distance, gate):
    cut = value.shape[0] // 2
    return after(value[:cut], gate) + swap(value[cut:], "dp", size, distance)


def scatter_last(mine, size, gate):
    total = after(mine[0], gate)
    for index in range(1, size // 2):
        total = total + swap(mine[index], "dp", size, 2 * index)
    return total


def gather_near(piece, size, gate):
    return jnp.stack([after(piece, gate)] + [swap(piece, "dp", size, 2 * index) for index in range(1, size // 2)])


def per_device(
    dp_size,
    block_input,
    cotangent,
    item_sides,
    item_modes,
    ln1_gain,
    ln1_bias,
    spec_w1,
    spec_b1,
    spec_w2,
    spec_b2,
    ln2_gain,
    ln2_bias,
    mlp_w1,
    mlp_b1,
    mlp_w2,
    mlp_b2,
):
    own = lax.axis_index("blk").astype(jnp.int32).reshape(1)
    place = lax.axis_index("dp").astype(jnp.int32).reshape(1)
    cube = (SMAX, SMAX, LANES)
    x = block_input.reshape(cube)
    gain1, bias1 = ln1_gain.reshape(1, LANES), ln1_bias.reshape(1, LANES)

    depth = C // dp_size
    share = jnp.stack([lax.dynamic_slice_in_dim(w, place[0] * depth, depth) for w in (mlp_w1, mlp_w2)])
    share = swap(share, "blk", PARTS, 2)
    moment = moments(
        item_sides, x, mlp_b1.reshape(4, LANES), ln2_gain.reshape(1, LANES), ln2_bias.reshape(1, LANES)
    )
    stats = exchange([moment] * PARTS)
    g_parts, g_late, grad_b2 = cotangent_pieces(item_sides, after(cotangent.reshape(cube), moment))
    g = lax.all_to_all(after(g_parts, *stats[1:]), "blk", 0, 0).reshape(PARTS, (CHUNKS - 1) * PIECE, LANES)
    sides = after(item_sides, g_parts)
    f6, g6, ft3, gt3, w1c, w2c, w1t, w2t = prepare(table(sides, item_modes), spec_w1, spec_w2)
    far = lax.all_gather(after(share, moment), "dp", axis=0)
    mlp_w1, mlp_w2, _ = lax.optimization_barrier((mlp_w1, mlp_w2, stats[3]))
    one = [mlp_w1, swap(mlp_w1, "blk", PARTS, 1)]
    two = [mlp_w2, swap(mlp_w2, "blk", PARTS, 1)]

    b, xn, xhat, r = first_stage(item_sides, after(x, g_parts), stats, gain1, bias1, f6)
    bre, bim, a, p, o = mix_forward(
        b, g6, w1c, spec_b1.reshape(1, 256), w2c, spec_b2.reshape(1, 256), gt3
    )
    far = after(far, bre)
    far = [far, swap(far, "blk", PARTS, 1)]
    first_pieces, x1 = last_stage(own, bre, bim, xn, ft3, None, 0)
    x1_first = [piece.reshape(PIECE, LANES) for piece in exchange(first_pieces)]
    weights = split_weights(own, one, two, far)
    field = after(xn, g, *weights)
    pieces, x1 = last_stage(own, bre, bim, field, ft3, x1, 1)
    x1_later = [piece.reshape((CHUNKS - 1) * PIECE, LANES) for piece in exchange(pieces)]

    x1_first[0] = after(x1_first[0], x1)
    keep, b1s, norms, dx_early = None, [], [], []
    for chunk in range(CHUNKS - 1):
        results = feed(own, x1_later if chunk else x1_first, g, weights, stats, keep, chunk)
        keep = results[:7]
        dx_early.append(exchange(results[7:11]))
        if chunk == 0:
            g_late = lax.all_to_all(after(g_late, results[7]), "blk", 0, 0).reshape(PARTS, PIECE, LANES)
        b1s.append(results[11])
        norms.append(results[12])
    x1_now = [after(x1_later[0], g_late), *x1_later[1:]]
    results = feed_forward(own, x1_now, weights, stats, keep[:4], CHUNKS - 1)
    hh, hl, nh, nl, tip = results[:5]
    branch = lax.all_to_all(after(keep[4], hh), "blk", 0, 0)
    send2, held2 = weight_grads(own, place, dp_size, [after(g, *dx_early[0][1:], *dx_early[1][1:]), g_late], hh, hl, 20)
    local = list(results[5:])
    local[1] = after(local[1], held2)
    results = feed_backward(own, g_late, weights, local, stats, keep[5:7], CHUNKS - 1)
    ph, plo = results[:2]
    b1s.append(results[6])
    norms.append(results[7])
    got2 = after(held2, ph) + swap(send2, "blk", PARTS, 1)
    dx_all = dx_early + [exchange(results[2:6])]
    dx_all = [v.reshape(SLABS, SMAX, LANES) for group in dx_all for v in group]
    tip = lax.all_to_all(after(tip, ph), "blk", 0, 0)
    ph = after(ph, got2, branch)
    send1, held1 = weight_grads(own, place, dp_size, [nh, nl], ph, plo, 20)

    half, cut = dp_size // 2, send1.shape[2] // 2
    mine2 = got2[:, :half] + swap(got2[:, half:], "dp", dp_size, 1)
    got1 = after(held1, *dx_all[-3:]) + swap(send1, "blk", PARTS, 1)
    dx_all[0] = after(dx_all[0], mine2, tip)
    d, dx = first_back(own, dx_all, f6)
    mine2 = after(mine2[0], d) + swap(mine2[1], "blk", PARTS, 2)
    block_output = output_stage(
        item_sides,
        after(x1, d),
        branch.reshape(PARTS, CHUNKS - 1, SLABS, SMAX, LANES),
        tip.reshape(PARTS, SLABS, SMAX, LANES),
        mlp_b2.reshape(1, LANES),
    )
    early = mix_backward(after(d, got1, mine2, block_output), a, p, o, g6, w1t, w2t, gt3, None, None)
    kept = after(got1, early[0])
    one = kept[:, :half, :cut] + swap(got1[:, half:, :cut], "dp", dp_size, 1)
    two = kept[0, :, cut:] + swap(got1[1, :, cut:], "blk", PARTS, 2)
    second = scatter_last(after(mine2, d), dp_size, early[0])
    d_late = after(d, early[0], second, one, two)
    late = mix_backward(d_late, a, p, o, g6, w1t, w2t, gt3, early[2:], grad_b2)
    near2 = gather_near(after(second, early[0]), dp_size, late[0])
    one = after(one[0], late[0]) + swap(one[1], "blk", PARTS, 2)
    two = after(two[:half], late[0]) + swap(two[half:], "dp", dp_size, 1)
    quarters = [early[0], late[0], early[1], late[1]]
    dx_gated = after(dx, near2, one, two)
    dn, pack, *sums = last_back(quarters, dx_gated, xhat, gain1, ft3, late[2], b1s, norms)
    first = scatter_last(jnp.concatenate([one, two], axis=1), dp_size, dn)
    far2 = swap(after(near2, late[0]), "dp", dp_size, 1)
    sums = exchange([after(value, first) for value in sums])
    input_grad = final_stage(item_sides, after(dx, far2), dn, xhat, sums, r, gain1)
    tail = sums[0][-1] + sums[1][-1] + sums[2][-1] + sums[3][-1]
    pack = jnp.concatenate([pack, tail], axis=0)
    near1 = gather_near(first, dp_size, input_grad)
    pack = after(pack, input_grad) + swap(pack, "dp", dp_size, 1)
    distance = 2
    while distance < dp_size:
        pack = pack + swap(pack, "dp", dp_size, distance)
        distance *= 2
    far1 = swap(near1, "dp", dp_size, 1)
    w1_grad = assemble(place, near1, far1, False)
    w2_grad = assemble(place, near2, far2, True)

    spec = pack[: 4 * FREQ].reshape(2, 2, FREQ, 2, FREQ).transpose(0, 1, 3, 2, 4)
    rest = pack[4 * FREQ :]
    return (
        block_output.reshape(SMAX * SMAX, LANES),
        input_grad.reshape(SMAX * SMAX, LANES),
        rest[5],
        rest[6],
        spec[0],
        rest[0:2].reshape(2, 2, 64),
        spec[1],
        rest[2:4].reshape(2, 2, 64),
        rest[12],
        rest[13],
        w1_grad,
        rest[8:12].reshape(HID),
        w2_grad,
        rest[4],
    )


def solution(mesh):
    in_specs = (
        P("dp", "blk"),
        P("dp", "blk"),
        P("dp"),
        P("dp"),
        P("blk"),
        P("blk"),
        P(None, "blk", None, None),
        P(None, "blk", None),
        P(None, "blk", None, None),
        P(None, "blk", None),
        P("blk"),
        P("blk"),
        P(None, "blk"),
        P("blk"),
        P("blk", None),
        P("blk"),
    )
    out_specs = (
        P("dp", "blk"),
        P("dp", "blk"),
        P("blk"),
        P("blk"),
        P(None, "blk", None, None),
        P(None, "blk", None),
        P(None, "blk", None, None),
        P(None, "blk", None),
        P("blk"),
        P("blk"),
        P(None, "blk"),
        P("blk"),
        P("blk", None),
        P("blk"),
    )
    return jax.shard_map(
        functools.partial(per_device, mesh.shape["dp"]),
        mesh=mesh,
        in_specs=in_specs,
        out_specs=out_specs,
        check_vma=False,
    )
```

```python
import functools
import math

import jax
import jax.numpy as jnp
from jax import lax
from jax.experimental import pallas as pl
from jax.experimental.pallas import tpu as pltpu
from jax.sharding import PartitionSpec as P

C = 512
MODES = 32
SMAX = 96
LANES = 128
FREQ = 64
HALF = 32
PARTS = 4
CHUNKS = 3
SLABS = SMAX // (PARTS * CHUNKS)
PIECE = SLABS * SMAX
GROUP = PARTS * SLABS
STEPS = SMAX // SLABS
STAGE = 24
THIRDS = STAGE // SLABS
WIDTH = 8
BATCH = 8
TILE = 256
SUB = 768
HID = 512
PACK = 4 * FREQ + 8

EPS = 1e-05
SHRINK = 0.01
F32 = jnp.float32
BF16 = jnp.bfloat16
NN = (((1,), (0,)), ((), ()))
NT = (((1,), (1,)), ((), ()))
TN = (((0,), (0,)), ((), ()))
LIMIT = 56 * 1024 * 1024


def mm(left, right, dims=NN):
    return lax.dot_general(left, right, dims, preferred_element_type=F32)


def split2(value):
    high = value.astype(BF16)
    return high, (value - high.astype(F32)).astype(BF16)


def split3(value):
    high = value.astype(BF16)
    rest = value - high.astype(F32)
    mid = rest.astype(BF16)
    return high, mid, (rest - mid.astype(F32)).astype(BF16)


def left6(value):
    one, two, three = split3(value)
    return jnp.concatenate([one, one, two, one, two, three], axis=1)


def right6(value):
    one, two, three = split3(value)
    return jnp.concatenate([one, two, one, three, two, one], axis=0)


def left3(value):
    one, two = split2(value)
    return jnp.concatenate([one, one, two], axis=1)


def right3(value):
    one, two = split2(value)
    return jnp.concatenate([one, two, one], axis=0)


def phi_pair(value):
    cdf = 0.5 + 0.5 * lax.erf(value * math.sqrt(0.5))
    pdf = jnp.exp(value * value * -0.5) * (1.0 / math.sqrt(2.0 * math.pi))
    return cdf, pdf


def pad_rows(value):
    return jnp.concatenate([value, jnp.zeros((LANES - SMAX, value.shape[1]), F32)], axis=0)


def fold_rows(value):
    return jnp.sum(value.reshape(-1, 8, value.shape[-1]), axis=0)


def spread8(rows):
    one, two, three = split3(rows)
    parts = [value.astype(F32) for value in (one, two, three)]
    left = jnp.concatenate(parts + [jnp.zeros_like(rows)], axis=0).astype(BF16)
    index = lax.broadcasted_iota(jnp.int32, (32, SLABS * LANES), 0)
    lane = lax.broadcasted_iota(jnp.int32, (32, SLABS * LANES), 1)
    pick = (index % SLABS == lane // LANES) & (index < 3 * SLABS)
    return mm(left, jnp.where(pick, 1.0, 0.0).astype(BF16), TN)


def slab_of(wide, slab):
    return wide[:SMAX, slab * LANES : (slab + 1) * LANES]


def us(time):
    return (int(time * 1e9), int(time * 3e6))


def call(body, out_shape, in_specs, out_specs, grid=(), scratch=(), aliases=None, cost=None):
    flops, moved = cost or (0, 0)
    return pl.pallas_call(
        body,
        out_shape=out_shape,
        grid=grid,
        in_specs=in_specs,
        out_specs=out_specs,
        scratch_shapes=list(scratch),
        input_output_aliases=aliases or {},
        compiler_params=pltpu.CompilerParams(vmem_limit_bytes=LIMIT),
        cost_estimate=pl.CostEstimate(flops=flops, bytes_accessed=moved, transcendentals=0),
    )


SMEM = pl.BlockSpec(memory_space=pltpu.SMEM)
VMEM = pl.BlockSpec(memory_space=pltpu.VMEM)
ANY = pl.BlockSpec(memory_space=pl.ANY)


def whole(shape):
    zeros = (0,) * len(shape)
    return pl.BlockSpec(shape, lambda *_: zeros)


def sds(shape, dtype=F32):
    return jax.ShapeDtypeStruct(shape, dtype)


def table(item_sides, item_modes):
    row = lax.broadcasted_iota(jnp.int32, (LANES, LANES), 0)
    cell = lax.broadcasted_iota(jnp.int32, (LANES, LANES), 1)
    index = row % FREQ
    frequency = index - (MODES - 1)
    extent = item_sides[0]
    phase = frequency * cell % extent
    keep = (jnp.abs(frequency) < item_modes[0]) & (cell < extent) & (index < 2 * MODES - 1)
    length = extent.astype(F32)
    angle = 2.0 * math.pi * phase.astype(F32) / length
    wave = jnp.where(row < FREQ, jnp.cos(angle), -jnp.sin(angle)) * lax.rsqrt(length)
    return jnp.where(keep, wave, jnp.zeros_like(wave))


def big_weight(weight, out):
    out[...] = jnp.zeros_like(out)
    for block in range(2):
        rows = pl.ds(block * 64, 64)
        later = pl.ds(128 + block * 64, 64)
        out[rows, rows] = weight[0, block]
        out[rows, later] = weight[1, block]
        out[later, rows] = -weight[1, block]
        out[later, later] = weight[0, block]


def prepare_body(f_ref, w1_ref, w2_ref, f6, g6, ft3, gt3, w1c, w2c, w1t, w2t, big):
    full = f_ref[...]
    cosine, sine = full[:FREQ], full[FREQ:]
    half = jnp.concatenate([cosine[HALF - 1 : FREQ - 1], sine[HALF - 1 : FREQ - 1]], axis=0)
    f6[...] = left6(half)
    ft3[...] = left3(half.T)
    lines = [(cosine, -sine), (sine, cosine), (cosine, sine), (sine, -cosine)]
    table_ = jnp.concatenate([jnp.concatenate(line, axis=1) for line in lines], axis=0)
    g6[...] = left6(table_)
    gt3[...] = left3(table_.T)
    for source, straight, across in ((w1_ref, w1c, w1t), (w2_ref, w2c, w2t)):
        big_weight(source, big)
        straight[...] = right6(big[...])
        across[...] = right3(big[...].T)


def prepare(forward, spec_w1, spec_w2):
    shapes = [
        sds((64, 768), BF16),
        sds((256, 1536), BF16),
        sds((128, 192), BF16),
        sds((256, 768), BF16),
        sds((1536, 256), BF16),
        sds((1536, 256), BF16),
        sds((768, 256), BF16),
        sds((768, 256), BF16),
    ]
    return call(
        prepare_body,
        shapes,
        [VMEM] * 3,
        [VMEM] * 8,
        scratch=[pltpu.VMEM((256, 256), F32)],
        cost=us(3),
    )(forward, spec_w1, spec_w2)


def slab_mask(first, side):
    cell = lax.broadcasted_iota(jnp.int32, (SMAX, LANES), 0)
    return (cell < side) & (first < side)


def moments_body(side_ref, x_ref, b1_ref, gain_ref, bias_ref, out_ref):
    step = pl.program_id(0)
    side = side_ref[0]

    @pl.when(step == 0)
    def _():
        vectors = [b1_ref[...], gain_ref[...], bias_ref[...], jnp.zeros((2, LANES), F32)]
        out_ref[2 * STEPS] = jnp.concatenate(vectors, axis=0)

    for slab in range(STAGE):
        inside = slab_mask(step * STAGE + slab, side)
        value = pad_rows(jnp.where(inside, x_ref[slab], 0.0)).T
        mean = jnp.sum(value, axis=0, keepdims=True) * (1.0 / LANES)
        centered = value - mean
        block, row = step * THIRDS + slab // SLABS, pl.ds(slab % SLABS, 1)
        out_ref[block, row, :] = mean
        out_ref[STEPS + block, row, :] = jnp.sum(centered * centered, axis=0, keepdims=True)


def moments(side, x, b1, gain, bias):
    return call(
        moments_body,
        sds((2 * STEPS + 1, SLABS, LANES)),
        [
            SMEM,
            pl.BlockSpec((STAGE, SMAX, LANES), lambda i: (i, 0, 0)),
            whole((4, LANES)),
            whole((1, LANES)),
            whole((1, LANES)),
        ],
        whole((2 * STEPS + 1, SLABS, LANES)),
        grid=(SMAX // STAGE,),
        cost=us(6),
    )(side, x, b1, gain, bias)


def cotangent_body(side_ref, g_ref, early, late, total):
    chunk = pl.program_id(0)
    side = side_ref[0]

    @pl.when(chunk == 0)
    def _():
        total[...] = jnp.zeros_like(total)

    def emit(out_ref):
        carry = jnp.zeros((8, LANES), F32)
        for part in range(PARTS):
            for slab in range(SLABS):
                first = part * SLABS + slab
                value = jnp.where(slab_mask(chunk * GROUP + first, side), g_ref[first], 0.0)
                out_ref[part, 0, slab] = value
                carry = carry + fold_rows(value)
        total[...] += carry

    @pl.when(chunk < CHUNKS - 1)
    def _():
        emit(early)

    @pl.when(chunk == CHUNKS - 1)
    def _():
        emit(late)


def cotangent_pieces(side, g):
    block = (PARTS, 1, SLABS, SMAX, LANES)
    return call(
        cotangent_body,
        [sds((PARTS, CHUNKS - 1, SLABS, SMAX, LANES)), sds(block), sds((8, LANES))],
        [SMEM, pl.BlockSpec((GROUP, SMAX, LANES), lambda i: (i, 0, 0))],
        [
            pl.BlockSpec(block, lambda i: (0, jnp.minimum(i, CHUNKS - 2), 0, 0, 0)),
            whole(block),
            whole((8, LANES)),
        ],
        grid=(CHUNKS,),
        cost=us(5),
    )(side, g)


def row_stats(means, totals):
    mean = (means[0] + means[1] + means[2] + means[3]) * (1.0 / PARTS)
    total = totals[0] + totals[1] + totals[2] + totals[3]
    for part in range(PARTS):
        gap = means[part] - mean
        total = total + LANES * (gap * gap)
    spread_ = total * (1.0 / C) + EPS
    inverse = lax.rsqrt(spread_)
    inverse = inverse * (1.5 - 0.5 * spread_ * inverse * inverse)
    return mean, inverse


def first_body(side_ref, x_ref, *refs):
    stats = refs[:PARTS]
    gain_ref, bias_ref, f6_ref, b_ref, xn_ref, xhat_ref, r_ref = refs[PARTS:]
    step = pl.program_id(0)
    side = side_ref[0]
    gain, bias = gain_ref[...], bias_ref[...]
    for third in range(THIRDS):
        block = step * THIRDS + third
        mean, inverse = row_stats([ref[block] for ref in stats], [ref[STEPS + block] for ref in stats])
        r_ref[pl.ds(third * SLABS, SLABS), :] = inverse
        means, scales = spread8(mean), spread8(inverse)
        columns = []
        for inner in range(SLABS):
            slab = third * SLABS + inner
            value = jnp.where(slab_mask(step * STAGE + slab, side), x_ref[slab], 0.0)
            centered = value - slab_of(means, inner)
            normal = centered * slab_of(scales, inner)
            normed = normal * gain + bias
            xhat_ref[slab] = normal
            xn_ref[slab] = value + normed
            columns.append(pad_rows(normed))
        out = mm(f6_ref[...], right6(jnp.concatenate(columns, axis=1)))
        for inner in range(SLABS):
            b_ref[third * SLABS + inner] = out[:, part_lanes(inner)]


def first_stage(side, x, stats, gain, bias, f6):
    field = pl.BlockSpec((STAGE, SMAX, LANES), lambda i: (i, 0, 0))
    return call(
        first_body,
        [sds((SMAX, FREQ, LANES)), sds((SMAX, SMAX, LANES)), sds((SMAX, SMAX, LANES)), sds((SMAX, LANES))],
        [SMEM, field]
        + [whole((2 * STEPS + 1, SLABS, LANES))] * PARTS
        + [whole((1, LANES)), whole((1, LANES)), whole((64, 768))],
        [
            pl.BlockSpec((STAGE, FREQ, LANES), lambda i: (i, 0, 0)),
            field,
            field,
            pl.BlockSpec((STAGE, LANES), lambda i: (i, 0)),
        ],
        grid=(SMAX // STAGE,),
        cost=us(3),
    )(side, x, *stats, gain, bias, f6)


def gather_columns(re_ref, im_ref, first):
    zeros = jnp.zeros((LANES - SMAX, LANES), F32)
    re, im = [ref.reshape(SMAX * WIDTH, LANES) for ref in (re_ref, im_ref)]
    columns = []
    for j in range(first, first + BATCH):
        rows = pl.ds(j, SMAX, stride=WIDTH)
        columns.append(jnp.concatenate([re[rows, :], zeros, im[rows, :], zeros], axis=0))
    return jnp.concatenate(columns, axis=1)


def to_rows(out):
    rows = []
    for j in range(BATCH):
        lanes = part_lanes(j)
        for base in (0, 2 * FREQ):
            parts = [out[base : base + FREQ, lanes], out[base + FREQ : base + 2 * FREQ, lanes]]
            rows.append(jnp.concatenate(parts, axis=1))
    return jnp.concatenate(rows, axis=0)


def to_columns(rows):
    columns = []
    for j in range(BATCH):
        parts = []
        for sign in range(2):
            first = (2 * j + sign) * FREQ
            part = rows[first : first + FREQ]
            parts += [part[:, :LANES], part[:, LANES:]]
        columns.append(jnp.concatenate(parts, axis=0))
    return jnp.concatenate(columns, axis=1)


def counted(step, half, shape):
    row = lax.broadcasted_iota(jnp.int32, shape, 0)
    twice = (step == 0) & (half == 0)
    return (row < FREQ) | (row >= 2 * FREQ) | jnp.logical_not(twice)


def scatter_columns(re_ref, im_ref, first, out):
    re, im = [ref.reshape(SMAX * WIDTH, LANES) for ref in (re_ref, im_ref)]
    for j in range(BATCH):
        lanes = slice(j * LANES, (j + 1) * LANES)
        rows = pl.ds(first + j, SMAX, stride=WIDTH)
        re[rows, :] = out[:SMAX, lanes]
        im[rows, :] = out[LANES : LANES + SMAX, lanes]


def shrink(value):
    return jnp.where(
        value > SHRINK,
        value - SHRINK,
        jnp.where(value < -SHRINK, value + SHRINK, jnp.zeros_like(value)),
    )


def mix_body(re_ref, im_ref, g6_ref, w1_ref, b1_ref, w2_ref, b2_ref, gt3_ref, bre, bim, a_out, p_out, o_out):
    for half in range(WIDTH // BATCH):
        rows = pl.ds(half * 2 * BATCH * FREQ, 2 * BATCH * FREQ)
        spectrum = to_rows(mm(g6_ref[...], right6(gather_columns(re_ref, im_ref, BATCH * half))))
        a_out[rows, :] = spectrum
        pre = mm(left6(spectrum), w1_ref[...]) + b1_ref[...]
        p_out[rows, :] = pre
        cdf = 0.5 + 0.5 * lax.erf(pre * math.sqrt(0.5))
        out = mm(left6(pre * cdf), w2_ref[...]) + b2_ref[...]
        o_out[rows, :] = out
        if half == 0:
            out = jnp.where(counted(pl.program_id(0), half, out.shape), out, 0.0)
        scatter_columns(bre, bim, BATCH * half, mm(gt3_ref[...], right3(to_columns(shrink(out)))))


def mix_forward(b, g6, w1c, bias1, w2c, bias2, gt3):
    count = HALF // WIDTH
    re = pl.BlockSpec((SMAX, WIDTH, LANES), lambda j: (0, j, 0))
    im = pl.BlockSpec((SMAX, WIDTH, LANES), lambda j: (0, count + j, 0))
    out = pl.BlockSpec((SMAX, WIDTH, LANES), lambda j: (0, j, 0))
    rows = pl.BlockSpec((2 * WIDTH * FREQ, 256), lambda j: (j, 0))
    half = sds((SMAX, HALF, LANES))
    return call(
        mix_body,
        [half, half] + [sds((4096, 256))] * 3,
        [
            re,
            im,
            whole((256, 1536)),
            whole((1536, 256)),
            whole((1, 256)),
            whole((1536, 256)),
            whole((1, 256)),
            whole((256, 768)),
        ],
        [out, out, rows, rows, rows],
        grid=(count,),
        cost=us(0.1),
    )(b, b, g6, w1c, bias1, w2c, bias2, gt3)


def last_body(own_ref, re_ref, im_ref, xn_ref, ft3_ref, *refs):
    full, outs = refs[-1], refs[-1 - PARTS : -1]
    own = own_ref[0]
    for part in range(PARTS):
        base = (own ^ part) * SLABS
        columns = [jnp.concatenate([re_ref[base + s], im_ref[base + s]], axis=0) for s in range(SLABS)]
        out = mm(ft3_ref[...], right3(jnp.concatenate(columns, axis=1)))[:SMAX]
        for s in range(SLABS):
            value = xn_ref[base + s] + out[:, part_lanes(s)]
            full[base + s] = value
            if len(outs[part].shape) == 3:
                outs[part][s] = value
            else:
                outs[part][0, s] = value


def last_stage(own, bre, bim, xn, ft3, keep, chunk):
    half = pl.BlockSpec((GROUP, HALF, LANES), lambda i: (chunk + i, 0, 0))
    field = pl.BlockSpec((GROUP, SMAX, LANES), lambda i: (chunk + i, 0, 0))
    args = [own, bre, bim, xn, ft3]
    in_specs = [SMEM, half, half, field, whole((128, 192))]
    aliases = {}
    steps = 1 if chunk == 0 else CHUNKS - 1
    if keep is not None:
        aliases[len(args)] = PARTS
        args.append(keep)
        in_specs.append(ANY)
    piece = (SLABS, SMAX, LANES)
    shape = piece if chunk == 0 else (steps,) + piece
    spec = whole(piece)
    if chunk > 0:
        spec = pl.BlockSpec((1,) + piece, lambda i: (i, 0, 0, 0))
    *pieces, full = call(
        last_body,
        [sds(shape)] * PARTS + [sds((SMAX, SMAX, LANES))],
        in_specs,
        [spec] * PARTS + [field],
        grid=(steps,),
        aliases=aliases,
        cost=us(0.1 * steps),
    )(*args)
    return pieces, full


def weights_body(own_ref, *refs):
    own = own_ref[0]
    firsts, seconds, outs = refs[:PARTS], refs[PARTS : 2 * PARTS], refs[2 * PARTS :]
    w1h, w1l, w2h, w2l = outs
    for block in range(PARTS):
        w1h[block], w1l[block] = split2(firsts[block][...].reshape(LANES, HID))
        for part in range(PARTS):
            source = pl.ds(pl.multiple_of((own ^ part) * LANES, LANES), LANES)
            ref = seconds[block]
            value = ref[:, source] if len(ref.shape) == 2 else ref[:, 0, :, source].reshape(LANES, LANES)
            high, low = split2(value)
            w2h[block, :, part_lanes(part)] = high
            w2l[block, :, part_lanes(part)] = low


def split_weights(own, one, two, far):
    depth, height = far[0].shape[0] // PARTS, far[0].shape[2]
    far_block = (depth, 1, height, HID)
    turned = pl.BlockSpec((LANES, HID), lambda i, own_ref: (i ^ own_ref[0], 0))
    straight = pl.BlockSpec((LANES, HID), lambda i, own_ref: (i, 0))
    far_turned = pl.BlockSpec(far_block, lambda i, own_ref: (i ^ own_ref[0], 0, 0, 0))
    far_straight = pl.BlockSpec(far_block, lambda i, own_ref: (i, 1, 0, 0))
    flops, moved = us(0.1)
    return pl.pallas_call(
        weights_body,
        out_shape=[sds((4, 512, 512), BF16)] * 4,
        grid_spec=pltpu.PrefetchScalarGridSpec(
            num_scalar_prefetch=1,
            grid=(PARTS,),
            in_specs=[turned] * 2 + [far_turned] * 2 + [straight] * 2 + [far_straight] * 2,
            out_specs=[pl.BlockSpec((PARTS, LANES, HID), lambda i, own_ref: (0, i, 0))] * 4,
        ),
        compiler_params=pltpu.CompilerParams(vmem_limit_bytes=LIMIT),
        cost_estimate=pl.CostEstimate(flops=flops, bytes_accessed=moved, transcendentals=0),
    )(own, *one, *far, *two, *far)


def row_mean(parts):
    total = parts[0] + parts[1] + parts[2] + parts[3]
    return jnp.sum(total, axis=1, keepdims=True) * (1.0 / C)


def part_lanes(part):
    return slice(part * LANES, (part + 1) * LANES)


def norm_tiles(load, vectors, n_h, n_l, nh, nl, xhat, scale):
    def norm(tile, carry):
        rows = pl.ds(tile * TILE, TILE)
        values = [load(part, rows) for part in range(PARTS)]
        mean = row_mean(values)
        centered = [value - mean for value in values]
        spread_ = row_mean([value * value for value in centered]) + EPS
        inverse = lax.rsqrt(spread_)
        inverse = inverse * (1.5 - 0.5 * spread_ * inverse * inverse)
        scale[rows, :] = jnp.broadcast_to(inverse, (TILE, LANES))
        for part in range(PARTS):
            lanes = part_lanes(part)
            normal = centered[part] * inverse
            xhat[rows, lanes] = normal
            gain, bias = vectors[part][0, 4:5, :], vectors[part][0, 5:6, :]
            high, low = split2(normal * gain + bias)
            n_h[rows, lanes] = high
            n_l[rows, lanes] = low
            nh[rows, lanes] = high
            nl[rows, lanes] = low
        return carry

    lax.fori_loop(0, PIECE // TILE, norm, 0)


def bias_of(vectors, step):
    row = jnp.zeros((4, LANES), F32)
    for part in range(PARTS):
        row = jnp.where(step == part, vectors[part][0, 0:4, :], row)
    return jnp.concatenate([row[i : i + 1] for i in range(4)], axis=1)


def grad_tiles(own, g_ref, vectors, dn, xhat, scale, store, small):
    small[...] = jnp.zeros_like(small)

    def back(tile, carry):
        rows = pl.ds(tile * TILE, TILE)
        inverse = scale[rows, :]
        scaled, normals = [], []
        for part in range(PARTS):
            lanes = part_lanes(part)
            grad = dn[rows, lanes]
            normal = xhat[rows, lanes]
            small[0, :, lanes] += fold_rows(grad * normal)
            small[1, :, lanes] += fold_rows(grad)
            scaled.append(grad * vectors[part][0, 4:5, :])
            normals.append(normal)
        first = row_mean(scaled)
        second = row_mean([s * n for s, n in zip(scaled, normals)])
        for part in range(PARTS):
            delta = inverse * (scaled[part] - first - normals[part] * second)
            store(part, rows, g_ref[own ^ part, rows, :] + delta)
        return carry

    lax.fori_loop(0, PIECE // TILE, back, 0)


def split_cotangent(own, g_ref, g_h, g_l):
    for part in range(PARTS):
        lanes = part_lanes(part)
        g_h[:, lanes], g_l[:, lanes] = split2(g_ref[own ^ part])


def product3(high, low, w_h, w_l, dims=NN):
    return mm(high, w_h[0], dims) + mm(low, w_h[0], dims) + mm(high, w_l[0], dims)


def add_to(ref, step, value):
    ref[...] = jnp.where(step == 0, 0.0, ref[...]) + value


def feed_body(*refs):
    own = refs[0][0]
    x_refs, g_ref = refs[1:5], refs[5]
    w1h, w1l, w2h, w2l = refs[6:10]
    vectors = refs[10:14]
    refs = refs[len(refs) - 21 :]
    hh, hl, nh, nl, out_ref, ph, plo = refs[0:7]
    dx_refs, db1, small = refs[7:11], refs[11], refs[12]
    n_h, n_l, g_h, g_l, xhat, scale, dn, acc = refs[13:21]
    step = pl.program_id(0)

    @pl.when(step == 0)
    def _():
        norm_tiles(lambda part, rows: x_refs[part][rows, :], vectors, n_h, n_l, nh, nl, xhat, scale)
        split_cotangent(own, g_ref, g_h, g_l)

    pre = product3(n_h[...], n_l[...], w1h, w1l) + bias_of(vectors, step)
    dh = product3(g_h[...], g_l[...], w2h, w2l, NT)
    cdf, pdf = phi_pair(pre)
    high, low = split2(pre * cdf)
    hh[...] = high
    hl[...] = low
    grad = dh * (cdf + pre * pdf)
    add_to(acc, step, product3(high, low, w2h, w2l))
    high, low = split2(grad)
    ph[...] = high
    plo[...] = low
    db1[0] = fold_rows(grad)
    add_to(dn, step, product3(high, low, w1h, w1l, NT))

    @pl.when(step == pl.num_programs(0) - 1)
    def _():
        for part in range(PARTS):
            out_ref[own ^ part, 0] = acc[:, part_lanes(part)]

        def store(part, rows, value):
            dx_refs[part][rows, :] = value

        grad_tiles(own, g_ref, vectors, dn, xhat, scale, store, small)


def forward_body(*refs):
    own = refs[0][0]
    x_refs = refs[1:5]
    w1h, w1l, w2h, w2l = refs[5:9]
    vectors = refs[9:13]
    hh, hl, nh, nl, out_ref, slope, xhat, scale, n_h, n_l, acc = refs[len(refs) - 11 :]
    step = pl.program_id(0)

    @pl.when(step == 0)
    def _():
        norm_tiles(lambda part, rows: x_refs[part][rows, :], vectors, n_h, n_l, nh, nl, xhat, scale)

    pre = product3(n_h[...], n_l[...], w1h, w1l) + bias_of(vectors, step)
    cdf, pdf = phi_pair(pre)
    slope[...] = cdf + pre * pdf
    high, low = split2(pre * cdf)
    hh[...] = high
    hl[...] = low
    add_to(acc, step, product3(high, low, w2h, w2l))

    @pl.when(step == pl.num_programs(0) - 1)
    def _():
        for part in range(PARTS):
            out_ref[own ^ part, 0] = acc[:, part_lanes(part)]


def backward_body(*refs):
    own = refs[0][0]
    g_ref, w1h, w1l, w2h, w2l, slope, xhat, scale = refs[1:9]
    vectors = refs[9:13]
    refs = refs[len(refs) - 11 :]
    ph, plo, dx_refs, db1, small = refs[0], refs[1], refs[2:6], refs[6], refs[7]
    g_h, g_l, dn = refs[8:]
    step = pl.program_id(0)

    @pl.when(step == 0)
    def _():
        split_cotangent(own, g_ref, g_h, g_l)

    grad = product3(g_h[...], g_l[...], w2h, w2l, NT) * slope[...]
    high, low = split2(grad)
    ph[...] = high
    plo[...] = low
    db1[0] = fold_rows(grad)
    add_to(dn, step, product3(high, low, w1h, w1l, NT))

    @pl.when(step == pl.num_programs(0) - 1)
    def _():

        def store(part, rows, value):
            dx_refs[part][rows, :] = value

        grad_tiles(own, g_ref, vectors, dn, xhat, scale, store, small)


def feed_call(body, head, heads, weights, stats, local, keep, kinds, chunk, cost):
    rows = PIECE * CHUNKS
    specs = {
        "x": (sds((PIECE, LANES)), whole((PIECE, LANES))),
        "later": (None, pl.BlockSpec((PIECE, LANES), lambda i: (chunk - 1, 0))),
        "g": (None, pl.BlockSpec((PARTS, PIECE, LANES), lambda i: (0, chunk, 0))),
        "g2": (None, whole((PARTS, PIECE, LANES))),
        "out": (
            sds((PARTS, CHUNKS - 1, PIECE, LANES)),
            pl.BlockSpec((PARTS, 1, PIECE, LANES), lambda i: (0, chunk, 0, 0)),
        ),
        "wide": (sds((rows, 2048), BF16), pl.BlockSpec((PIECE, HID), lambda i: (chunk, i))),
        "narrow": (sds((rows, C), BF16), pl.BlockSpec((PIECE, C), lambda i: (chunk, 0))),
        "slope": (sds((PIECE, 2048)), pl.BlockSpec((PIECE, HID), lambda i: (0, i))),
        "tip": (sds((PARTS, 1, PIECE, LANES)), whole((PARTS, 1, PIECE, LANES))),
        "full": (sds((PIECE, C)), whole((PIECE, C))),
        "db1": (sds((4, 8, HID)), pl.BlockSpec((1, 8, HID), lambda i: (i, 0, 0))),
        "small": (sds((2, 8, C)), whole((2, 8, C))),
    }
    weight = pl.BlockSpec((1, 512, 512), lambda i: (i, 0, 0))
    vector = pl.BlockSpec((1, SLABS, LANES), lambda i: (2 * STEPS, 0, 0))
    args = [*head, *weights, *(value for _, value in local), *stats]
    in_specs = [SMEM] + [specs[kind][1] for kind in heads] + [weight] * 4
    in_specs += [specs[kind][1] for kind, _ in local] + [vector] * 4
    aliases = {}
    for index, array in enumerate(keep or ()):
        aliases[len(args)] = index
        args.append(array)
        in_specs.append(ANY)
    bf, big = pltpu.VMEM((PIECE, C), BF16), pltpu.VMEM((PIECE, C), F32)
    scratch = {
        "feed": [bf] * 4 + [big, pltpu.VMEM((PIECE, LANES), F32), big, big],
        "fore": [bf, bf, big],
        "back": [bf, bf, big],
    }[kinds]
    outs = {
        "feed": ["wide"] * 2 + ["narrow"] * 2 + ["out", "wide", "wide"] + ["x"] * 4 + ["db1", "small"],
        "fore": ["wide"] * 2 + ["narrow"] * 2 + ["tip", "slope", "full", "x"],
        "back": ["wide", "wide"] + ["x"] * 4 + ["db1", "small"],
    }[kinds]
    return call(
        body,
        [specs[kind][0] for kind in outs],
        in_specs,
        [specs[kind][1] for kind in outs],
        grid=(4,),
        scratch=scratch,
        aliases=aliases,
        cost=us(cost),
    )(*args)


def feed(own, xs, g, weights, stats, keep, chunk):
    head, heads = [own, *xs, g], ["x" if chunk == 0 else "later"] * 4 + ["g"]
    return feed_call(feed_body, head, heads, weights, stats, [], keep, "feed", chunk, 28)


def feed_forward(own, xs, weights, stats, keep, chunk):
    return feed_call(forward_body, [own, *xs], ["later"] * 4, weights, stats, [], keep, "fore", chunk, 18)


def feed_backward(own, g, weights, local, stats, keep, chunk):
    local = list(zip(("slope", "full", "x"), local))
    return feed_call(backward_body, [own, g], ["g2"], weights, stats, local, keep, "back", chunk, 16)


def weight_body(own_ref, place_ref, th, tl, *refs):
    send, held, t_h, t_l = refs[-4:]
    step = pl.program_id(0)
    own, place = own_ref[0], place_ref[0]

    @pl.when(step == 0)
    def _():
        if len(refs[0].shape) == 2:
            t_h[...] = refs[0][...].T
            t_l[...] = refs[1][...].T
        else:
            for part in range(PARTS):
                pieces = [ref[own ^ part] for ref in refs[:2]]
                high, low = split2(jnp.concatenate(pieces, axis=0))
                t_h[part_lanes(part), :] = high.T
                t_l[part_lanes(part), :] = low.T

    out = mm(t_h[...], th[...]) + mm(t_l[...], th[...]) + mm(t_h[...], tl[...])
    count, depth = send.shape[1], send.shape[2]

    def store(ref):
        for index in range(count):
            part, inner = divmod(index, count // PARTS)
            apart = ((own ^ part) * (count // PARTS) + inner) ^ place
            where = (apart & 1) * (count // 2) + (apart >> 1)
            ref[0, where] = out[index * depth : (index + 1) * depth]

    @pl.when(step < 2)
    def _():
        store(send)

    @pl.when(step >= 2)
    def _():
        store(held)


def weight_grads(own, place, dp_size, left, th, tl, cost):
    rows = PIECE * CHUNKS
    wide = pl.BlockSpec((rows, HID), lambda i: (0, (i % 2) * 2 + 1 - i // 2))
    block = (1, dp_size, C // dp_size, HID)
    shape = sds((2,) + block[1:])
    return call(
        weight_body,
        [shape, shape],
        [SMEM, SMEM]
        + [wide] * 2
        + [pl.BlockSpec(v.shape, lambda i, n=v.ndim: (0,) * n, pipeline_mode=pl.Buffered(1)) for v in left],
        [
            pl.BlockSpec(block, lambda i: (jnp.minimum(i, 1), 0, 0, 0)),
            pl.BlockSpec(block, lambda i: (jnp.maximum(i - 2, 0), 0, 0, 0)),
        ],
        grid=(4,),
        scratch=[pltpu.VMEM((C, rows), BF16)] * 2,
        cost=us(cost),
    )(own, place, th, tl, *left)


def assemble_body(turn, place_ref, near, far, out_ref, held):
    place = place_ref[0]
    half, depth = near.shape[0], near.shape[1]
    target = held if turn else out_ref
    for side, source in enumerate((near, far)):
        for index in range(half):
            rows = pl.ds(pl.multiple_of((place ^ (2 * index + side)) * depth, depth), depth)
            target[rows, :] = source[index]
    if turn:
        out_ref[...] = held[...].T


def assemble(place, near, far, turn):
    return call(
        functools.partial(assemble_body, turn),
        sds((C, HID)),
        [SMEM] + [VMEM] * 2,
        VMEM,
        scratch=[pltpu.VMEM((C, HID), F32)],
        cost=us(2),
    )(place, near, far)


def first_back_body(own_ref, f6_ref, *refs):
    d_ref, dx_ref = refs[-2:]
    own = own_ref[0]
    for chunk in range(CHUNKS):

        @pl.when(pl.program_id(0) == chunk)
        def _(pieces=refs[PARTS * chunk : PARTS * (chunk + 1)]):
            for part in range(PARTS):
                base = (own ^ part) * SLABS
                columns = [pad_rows(pieces[part][s]) for s in range(SLABS)]
                out = mm(f6_ref[...], right3(jnp.concatenate(columns, axis=1)))
                for s in range(SLABS):
                    d_ref[base + s] = out[:, part_lanes(s)]
                    dx_ref[base + s] = pieces[part][s]


def first_back(own, pieces, f6):
    return call(
        first_back_body,
        [sds((SMAX, FREQ, LANES)), sds((SMAX, SMAX, LANES))],
        [SMEM, whole((64, 384))] + [whole(piece.shape) for piece in pieces],
        [
            pl.BlockSpec((GROUP, FREQ, LANES), lambda i: (i, 0, 0)),
            pl.BlockSpec((GROUP, SMAX, LANES), lambda i: (i, 0, 0)),
        ],
        grid=(CHUNKS,),
        cost=us(8),
    )(own, f6, *pieces)


def rows3(value):
    one, two = split2(value)
    return jnp.concatenate([one, one, two], axis=0)


def mix_back_body(*refs):
    re_ref, im_ref, a_ref, p_ref, o_ref, g3_ref, w1t, w2t, gt3_ref = refs[:9]
    sums = refs[-4:]
    dw1, dw2, db1, db2 = sums
    if len(refs) == 15:
        dre, dim = refs[9:11]
    else:
        gb_ref = refs[13]
        dre, dim, pack = refs[14:17]

    @pl.when(pl.program_id(0) == 0)
    def _():
        for index, ref in enumerate(sums):
            ref[...] = jnp.zeros_like(ref) if len(refs) == 15 else refs[9 + index][...]

    for half in range(WIDTH // BATCH):
        rows = pl.ds(half * 2 * BATCH * FREQ, 2 * BATCH * FREQ)
        dz = to_rows(mm(g3_ref[...], right3(gather_columns(re_ref, im_ref, BATCH * half))))
        do = jnp.where(jnp.abs(o_ref[rows, :]) > SHRINK, dz, 0.0)
        if half == 0 and len(refs) == 15:
            do = jnp.where(counted(pl.program_id(0), half, do.shape), do, 0.0)
        pre = p_ref[rows, :]
        cdf, pdf = phi_pair(pre)
        dw2[...] += mm(rows3(pre * cdf), right3(do), TN)
        db2[...] += fold_rows(do)
        dp = mm(left3(do), w2t[...]) * (cdf + pre * pdf)
        dw1[...] += mm(rows3(a_ref[rows, :]), right3(dp), TN)
        db1[...] += fold_rows(dp)
        dx = mm(left3(dp), w1t[...])
        if half == 0 and len(refs) == 15:
            dx = jnp.where(counted(pl.program_id(0), half, dx.shape), dx, 0.0)
        scatter_columns(dre, dim, BATCH * half, mm(gt3_ref[...], right3(to_columns(dx))))

    if len(refs) == 15:
        return

    @pl.when(pl.program_id(0) == pl.num_programs(0) - 1)
    def _():
        low = lax.broadcasted_iota(jnp.int32, (FREQ, LANES), 1) < FREQ
        for index, ref in enumerate((dw1, dw2)):
            full = ref[...]
            same = full[:LANES, :LANES] + full[LANES:, LANES:]
            cross = full[:LANES, LANES:] - full[LANES:, :LANES]
            for inner, value in enumerate((same, cross)):
                rows = pl.ds((2 * index + inner) * FREQ, FREQ)
                pack[rows, :] = jnp.where(low, value[:FREQ], value[FREQ:])
        sums = [jnp.sum(ref[...], axis=0, keepdims=True) for ref in (db1, db2)]
        lines = [sums[0][:, :LANES], sums[0][:, LANES:], sums[1][:, :LANES], sums[1][:, LANES:]]
        lines.append(jnp.sum(gb_ref[...], axis=0, keepdims=True))
        pack[4 * FREQ : 4 * FREQ + 8] = jnp.concatenate(lines + [jnp.zeros((3, LANES), F32)], axis=0)


def mix_backward(d, a, p, o, g6, w1t, w2t, gt3, carry, grad_b2):
    count = HALF // WIDTH
    skip = 0 if carry is None else count // 2
    re = pl.BlockSpec((SMAX, WIDTH, LANES), lambda j: (0, skip + j, 0))
    im = pl.BlockSpec((SMAX, WIDTH, LANES), lambda j: (0, count + skip + j, 0))
    out = pl.BlockSpec((SMAX, WIDTH, LANES), lambda j: (0, j, 0))
    rows = pl.BlockSpec((2 * WIDTH * FREQ, 256), lambda j: (skip + j, 0))
    half = sds((SMAX, HALF // 2, LANES))
    args = [d, d, a, p, o, g6, w1t, w2t, gt3]
    in_specs = [re, im, rows, rows, rows, whole((256, 768))]
    in_specs += [whole((768, 256)), whole((768, 256)), whole((256, 768))]
    sums = [(256, 256), (256, 256), (8, 256), (8, 256)]
    shapes, out_specs, scratch = [half, half], [out, out], []
    if carry is None:
        shapes += [sds(shape) for shape in sums]
        out_specs += [whole(shape) for shape in sums]
    else:
        args += [*carry, grad_b2]
        in_specs += [whole(shape) for shape in sums] + [whole((8, LANES))]
        shapes.append(sds((PACK, LANES)))
        out_specs.append(whole((PACK, LANES)))
        scratch = [pltpu.VMEM(shape, F32) for shape in sums]
    return call(
        mix_back_body, shapes, in_specs, out_specs, grid=(count // 2,), scratch=scratch, cost=us(13)
    )(*args)


def last_back_body(re0, re1, im0, im1, dx_ref, xhat_ref, gain_ref, ft3_ref, pack_ref, *refs):
    b1_refs, norm_refs = refs[:CHUNKS], refs[CHUNKS : 2 * CHUNKS]
    dn_ref, pack = refs[2 * CHUNKS : 2 * CHUNKS + 2]
    sums, small = refs[-1 - PARTS : -1], refs[-1]
    step = pl.program_id(0)

    @pl.when(step == 0)
    def _():
        small[...] = jnp.zeros_like(small)
        norms = norm_refs[0][...]
        for ref in norm_refs[1:]:
            norms = norms + ref[...]
        norms = [jnp.sum(norms[i], axis=0, keepdims=True) for i in range(2)]
        for part in range(PARTS):
            total = b1_refs[0][part]
            for ref in b1_refs[1:]:
                total = total + ref[part]
            total = jnp.sum(total, axis=0, keepdims=True)
            lines = [total[:, part_lanes(i)] for i in range(4)]
            lines += [value[:, part_lanes(part)] for value in norms]
            lines.append(jnp.zeros((2, LANES), F32))
            sums[part][2 * STEPS] = jnp.concatenate(lines, axis=0)

    gain = gain_ref[...]
    for third in range(THIRDS):
        slabs = [third * SLABS + inner for inner in range(SLABS)]
        columns = [jnp.concatenate([re0[s], re1[s], im0[s], im1[s]], axis=0) for s in slabs]
        out = mm(ft3_ref[...], right3(jnp.concatenate(columns, axis=1)))[:SMAX]
        for index, s in enumerate(slabs):
            grad = dx_ref[s] + out[:, part_lanes(index)]
            dn_ref[s] = grad
            product = grad * xhat_ref[s]
            small[0] += fold_rows(product)
            small[1] += fold_rows(grad)
            for which, value in enumerate((grad, product)):
                row = jnp.sum(pad_rows(value * gain).T, axis=0, keepdims=True)
                for ref in sums:
                    block = which * STEPS + step * THIRDS + s // SLABS
                    ref[block, pl.ds(s % SLABS, 1), :] = row

    @pl.when(step == pl.num_programs(0) - 1)
    def _():
        pack[...] = pack_ref[...]
        for index in range(2):
            where = pl.ds(4 * FREQ + 5 + index, 1)
            pack[where, :] = jnp.sum(small[index], axis=0, keepdims=True)


def last_back(quarters, dx, xhat, gain, ft3, pack, b1s, norms):
    half = pl.BlockSpec((STAGE, HALF // 2, LANES), lambda i: (i, 0, 0))
    field = pl.BlockSpec((STAGE, SMAX, LANES), lambda i: (i, 0, 0))
    shape = (2 * STEPS + 1, SLABS, LANES)
    return call(
        last_back_body,
        [sds((SMAX, SMAX, LANES)), sds((PACK, LANES))] + [sds(shape)] * PARTS,
        [half] * 4
        + [field, field, whole((1, LANES)), whole((128, 192)), whole((PACK, LANES))]
        + [whole((4, 8, HID))] * CHUNKS
        + [whole((2, 8, C))] * CHUNKS,
        [field, whole((PACK, LANES))] + [whole(shape)] * PARTS,
        grid=(SMAX // STAGE,),
        scratch=[pltpu.VMEM((2, 8, LANES), F32)],
        cost=us(13),
    )(*quarters, dx, xhat, gain, ft3, pack, *b1s, *norms)


def final_body(side_ref, dx_ref, dn_ref, xhat_ref, r_ref, gain_ref, *refs):
    sums, out_ref = refs[:PARTS], refs[PARTS]
    step = pl.program_id(0)
    side = side_ref[0]
    for third in range(THIRDS):
        block = step * THIRDS + third
        inverse = r_ref[pl.ds(third * SLABS, SLABS), :]
        total = [sum(ref[which * STEPS + block] for ref in sums) for which in range(2)]
        first = total[0] * (inverse * (1.0 / C))
        second = total[1] * (inverse * (1.0 / C))
        wide = [spread8(value) for value in (inverse, first, second)]
        for inner in range(SLABS):
            slab = third * SLABS + inner
            scaled = dn_ref[slab] * gain_ref[...]
            scale, shift, slope = [slab_of(value, inner) for value in wide]
            value = dx_ref[slab] + (scale * scaled - shift - xhat_ref[slab] * slope)
            out_ref[slab] = jnp.where(slab_mask(step * STAGE + slab, side), value, 0.0)


def final_stage(side, dx, dn, xhat, sums, r, gain):
    field = pl.BlockSpec((STAGE, SMAX, LANES), lambda i: (i, 0, 0))
    return call(
        final_body,
        sds((SMAX, SMAX, LANES)),
        [SMEM, field, field, field, pl.BlockSpec((STAGE, LANES), lambda i: (i, 0)), whole((1, LANES))]
        + [whole((2 * STEPS + 1, SLABS, LANES))] * PARTS,
        field,
        grid=(SMAX // STAGE,),
        cost=us(13),
    )(side, dx, dn, xhat, r, gain, *sums)


def output_body(side_ref, x_ref, y_ref, tip_ref, b2_ref, out_ref):
    step = pl.program_id(0)
    side = side_ref[0]
    for part in range(PARTS):
        for inner in range(SLABS):
            slab = part * SLABS + inner
            branch = jnp.where(step < CHUNKS - 1, y_ref[part, 0, inner], tip_ref[part, inner])
            value = x_ref[slab] + branch + b2_ref[...]
            out_ref[slab] = jnp.where(slab_mask(step * GROUP + slab, side), value, 0.0)


def output_stage(side, x1, y, tip, b2):
    field = pl.BlockSpec((GROUP, SMAX, LANES), lambda i: (i, 0, 0))
    return call(
        output_body,
        sds((SMAX, SMAX, LANES)),
        [
            SMEM,
            field,
            pl.BlockSpec(
                (PARTS, 1, SLABS, SMAX, LANES), lambda i: (0, jnp.minimum(i, CHUNKS - 2), 0, 0, 0)
            ),
            whole((PARTS, SLABS, SMAX, LANES)),
            whole((1, LANES)),
        ],
        field,
        grid=(CHUNKS,),
        cost=us(5),
    )(side, x1, y, tip, b2)


def swap(value, axis, size, distance):
    return lax.ppermute(value, axis, [(i, i ^ distance) for i in range(size)])


def exchange(pieces):
    return [pieces[0]] + [swap(pieces[part], "blk", PARTS, part) for part in range(1, PARTS)]


def after(value, *others):
    return lax.optimization_barrier((value, *others))[0]


def halve(value, size, distance, gate):
    cut = value.shape[0] // 2
    return after(value[:cut], gate) + swap(value[cut:], "dp", size, distance)


def scatter_last(mine, size, gate):
    total = after(mine[0], gate)
    for index in range(1, size // 2):
        total = total + swap(mine[index], "dp", size, 2 * index)
    return total


def gather_near(piece, size, gate):
    return jnp.stack([after(piece, gate)] + [swap(piece, "dp", size, 2 * index) for index in range(1, size // 2)])


def per_device(
    dp_size,
    block_input,
    cotangent,
    item_sides,
    item_modes,
    ln1_gain,
    ln1_bias,
    spec_w1,
    spec_b1,
    spec_w2,
    spec_b2,
    ln2_gain,
    ln2_bias,
    mlp_w1,
    mlp_b1,
    mlp_w2,
    mlp_b2,
):
    own = lax.axis_index("blk").astype(jnp.int32).reshape(1)
    place = lax.axis_index("dp").astype(jnp.int32).reshape(1)
    cube = (SMAX, SMAX, LANES)
    x = block_input.reshape(cube)
    gain1, bias1 = ln1_gain.reshape(1, LANES), ln1_bias.reshape(1, LANES)

    depth = C // dp_size
    share = jnp.stack([lax.dynamic_slice_in_dim(w, place[0] * depth, depth) for w in (mlp_w1, mlp_w2)])
    share = swap(share, "blk", PARTS, 2)
    moment = moments(
        item_sides, x, mlp_b1.reshape(4, LANES), ln2_gain.reshape(1, LANES), ln2_bias.reshape(1, LANES)
    )
    stats = exchange([moment] * PARTS)
    g_parts, g_late, grad_b2 = cotangent_pieces(item_sides, after(cotangent.reshape(cube), moment))
    g = lax.all_to_all(after(g_parts, *stats[1:]), "blk", 0, 0).reshape(PARTS, (CHUNKS - 1) * PIECE, LANES)
    sides = after(item_sides, g_parts)
    f6, g6, ft3, gt3, w1c, w2c, w1t, w2t = prepare(table(sides, item_modes), spec_w1, spec_w2)
    far = lax.all_gather(after(share, moment), "dp", axis=0)
    mlp_w1, mlp_w2, _ = lax.optimization_barrier((mlp_w1, mlp_w2, stats[3]))
    one = [mlp_w1, swap(mlp_w1, "blk", PARTS, 1)]
    two = [mlp_w2, swap(mlp_w2, "blk", PARTS, 1)]

    b, xn, xhat, r = first_stage(item_sides, after(x, g_parts), stats, gain1, bias1, f6)
    bre, bim, a, p, o = mix_forward(
        b, g6, w1c, spec_b1.reshape(1, 256), w2c, spec_b2.reshape(1, 256), gt3
    )
    far = after(far, bre)
    far = [far, swap(far, "blk", PARTS, 1)]
    first_pieces, x1 = last_stage(own, bre, bim, xn, ft3, None, 0)
    x1_first = [piece.reshape(PIECE, LANES) for piece in exchange(first_pieces)]
    weights = split_weights(own, one, two, far)
    field = after(xn, g, *weights)
    pieces, x1 = last_stage(own, bre, bim, field, ft3, x1, 1)
    x1_later = [piece.reshape((CHUNKS - 1) * PIECE, LANES) for piece in exchange(pieces)]

    x1_first[0] = after(x1_first[0], x1)
    keep, b1s, norms, dx_early = None, [], [], []
    for chunk in range(CHUNKS - 1):
        results = feed(own, x1_later if chunk else x1_first, g, weights, stats, keep, chunk)
        keep = results[:7]
        dx_early.append(exchange(results[7:11]))
        if chunk == 0:
            g_late = lax.all_to_all(after(g_late, results[7]), "blk", 0, 0).reshape(PARTS, PIECE, LANES)
        b1s.append(results[11])
        norms.append(results[12])
    x1_now = [after(x1_later[0], g_late), *x1_later[1:]]
    results = feed_forward(own, x1_now, weights, stats, keep[:4], CHUNKS - 1)
    hh, hl, nh, nl, tip = results[:5]
    branch = lax.all_to_all(after(keep[4], hh), "blk", 0, 0)
    send2, held2 = weight_grads(own, place, dp_size, [after(g, *dx_early[0][1:], *dx_early[1][1:]), g_late], hh, hl, 20)
    local = list(results[5:])
    local[1] = after(local[1], held2)
    results = feed_backward(own, g_late, weights, local, stats, keep[5:7], CHUNKS - 1)
    ph, plo = results[:2]
    b1s.append(results[6])
    norms.append(results[7])
    got2 = after(held2, ph) + swap(send2, "blk", PARTS, 1)
    dx_all = dx_early + [exchange(results[2:6])]
    dx_all = [v.reshape(SLABS, SMAX, LANES) for group in dx_all for v in group]
    tip = lax.all_to_all(after(tip, ph), "blk", 0, 0)
    ph = after(ph, got2, branch)
    send1, held1 = weight_grads(own, place, dp_size, [nh, nl], ph, plo, 20)

    half, cut = dp_size // 2, send1.shape[2] // 2
    mine2 = got2[:, :half] + swap(got2[:, half:], "dp", dp_size, 1)
    got1 = after(held1, *dx_all[-3:]) + swap(send1, "blk", PARTS, 1)
    dx_all[0] = after(dx_all[0], mine2, tip)
    d, dx = first_back(own, dx_all, f6)
    mine2 = after(mine2[0], d) + swap(mine2[1], "blk", PARTS, 2)
    block_output = output_stage(
        item_sides,
        after(x1, d),
        branch.reshape(PARTS, CHUNKS - 1, SLABS, SMAX, LANES),
        tip.reshape(PARTS, SLABS, SMAX, LANES),
        mlp_b2.reshape(1, LANES),
    )
    early = mix_backward(after(d, got1, mine2, block_output), a, p, o, g6, w1t, w2t, gt3, None, None)
    kept = after(got1, early[0])
    one = kept[:, :half, :cut] + swap(got1[:, half:, :cut], "dp", dp_size, 1)
    two = kept[0, :, cut:] + swap(got1[1, :, cut:], "blk", PARTS, 2)
    second = scatter_last(after(mine2, d), dp_size, early[0])
    d_late = after(d, early[0], second, one, two)
    late = mix_backward(d_late, a, p, o, g6, w1t, w2t, gt3, early[2:], grad_b2)
    near2 = gather_near(after(second, early[0]), dp_size, late[0])
    one = after(one[0], late[0]) + swap(one[1], "blk", PARTS, 2)
    two = after(two[:half], late[0]) + swap(two[half:], "dp", dp_size, 1)
    quarters = [early[0], late[0], early[1], late[1]]
    dx_gated = after(dx, near2, one, two)
    dn, pack, *sums = last_back(quarters, dx_gated, xhat, gain1, ft3, late[2], b1s, norms)
    first = scatter_last(jnp.concatenate([one, two], axis=1), dp_size, dn)
    far2 = swap(after(near2, late[0]), "dp", dp_size, 1)
    sums = exchange([after(value, first) for value in sums])
    input_grad = final_stage(item_sides, after(dx, far2), dn, xhat, sums, r, gain1)
    tail = sums[0][-1] + sums[1][-1] + sums[2][-1] + sums[3][-1]
    pack = jnp.concatenate([pack, tail], axis=0)
    near1 = gather_near(first, dp_size, input_grad)
    pack = after(pack, input_grad) + swap(pack, "dp", dp_size, 1)
    distance = 2
    while distance < dp_size:
        pack = pack + swap(pack, "dp", dp_size, distance)
        distance *= 2
    far1 = swap(near1, "dp", dp_size, 1)
    w1_grad = assemble(place, near1, far1, False)
    w2_grad = assemble(place, near2, far2, True)

    spec = pack[: 4 * FREQ].reshape(2, 2, FREQ, 2, FREQ).transpose(0, 1, 3, 2, 4)
    rest = pack[4 * FREQ :]
    return (
        block_output.reshape(SMAX * SMAX, LANES),
        input_grad.reshape(SMAX * SMAX, LANES),
        rest[5],
        rest[6],
        spec[0],
        rest[0:2].reshape(2, 2, 64),
        spec[1],
        rest[2:4].reshape(2, 2, 64),
        rest[12],
        rest[13],
        w1_grad,
        rest[8:12].reshape(HID),
        w2_grad,
        rest[4],
    )


def solution(mesh):
    in_specs = (
        P("dp", "blk"),
        P("dp", "blk"),
        P("dp"),
        P("dp"),
        P("blk"),
        P("blk"),
        P(None, "blk", None, None),
        P(None, "blk", None),
        P(None, "blk", None, None),
        P(None, "blk", None),
        P("blk"),
        P("blk"),
        P(None, "blk"),
        P("blk"),
        P("blk", None),
        P("blk"),
    )
    out_specs = (
        P("dp", "blk"),
        P("dp", "blk"),
        P("blk"),
        P("blk"),
        P(None, "blk", None, None),
        P(None, "blk", None),
        P(None, "blk", None, None),
        P(None, "blk", None),
        P("blk"),
        P("blk"),
        P(None, "blk"),
        P("blk"),
        P("blk", None),
        P("blk"),
    )
    return jax.shard_map(
        functools.partial(per_device, mesh.shape["dp"]),
        mesh=mesh,
        in_specs=in_specs,
        out_specs=out_specs,
        check_vma=False,
    )
```

```python
import functools
import math

import jax
import jax.numpy as jnp
from jax import lax
from jax.experimental import pallas as pl
from jax.experimental.pallas import tpu as pltpu
from jax.sharding import PartitionSpec as P

C = 512
MODES = 32
SMAX = 96
LANES = 128
FREQ = 64
HALF = 32
PARTS = 4
CHUNKS = 3
SLABS = SMAX // (PARTS * CHUNKS)
PIECE = SLABS * SMAX
GROUP = PARTS * SLABS
STEPS = SMAX // SLABS
STAGE = 24
THIRDS = STAGE // SLABS
WIDTH = 8
BATCH = 8
TILE = 256
SUB = 768
HID = 512
PACK = 4 * FREQ + 8

EPS = 1e-05
SHRINK = 0.01
F32 = jnp.float32
BF16 = jnp.bfloat16
NN = (((1,), (0,)), ((), ()))
NT = (((1,), (1,)), ((), ()))
TN = (((0,), (0,)), ((), ()))
LIMIT = 56 * 1024 * 1024
LESS = 32 * 1024 * 1024


def mm(left, right, dims=NN):
    return lax.dot_general(left, right, dims, preferred_element_type=F32)


def split2(value):
    high = value.astype(BF16)
    return high, (value - high.astype(F32)).astype(BF16)


def split3(value):
    high = value.astype(BF16)
    rest = value - high.astype(F32)
    mid = rest.astype(BF16)
    return high, mid, (rest - mid.astype(F32)).astype(BF16)


def left6(value):
    one, two, three = split3(value)
    return jnp.concatenate([one, one, two, one, two, three], axis=1)


def right6(value):
    one, two, three = split3(value)
    return jnp.concatenate([one, two, one, three, two, one], axis=0)


def left3(value):
    one, two = split2(value)
    return jnp.concatenate([one, one, two], axis=1)


def right3(value):
    one, two = split2(value)
    return jnp.concatenate([one, two, one], axis=0)


def phi_pair(value):
    cdf = 0.5 + 0.5 * lax.erf(value * math.sqrt(0.5))
    pdf = jnp.exp(value * value * -0.5) * (1.0 / math.sqrt(2.0 * math.pi))
    return cdf, pdf


def pad_rows(value):
    return jnp.concatenate([value, jnp.zeros((LANES - SMAX, value.shape[1]), F32)], axis=0)


def fold_rows(value):
    return jnp.sum(value.reshape(-1, 8, value.shape[-1]), axis=0)


def spread8(rows):
    one, two, three = split3(rows)
    parts = [value.astype(F32) for value in (one, two, three)]
    left = jnp.concatenate(parts + [jnp.zeros_like(rows)], axis=0).astype(BF16)
    index = lax.broadcasted_iota(jnp.int32, (32, SLABS * LANES), 0)
    lane = lax.broadcasted_iota(jnp.int32, (32, SLABS * LANES), 1)
    pick = (index % SLABS == lane // LANES) & (index < 3 * SLABS)
    return mm(left, jnp.where(pick, 1.0, 0.0).astype(BF16), TN)


def slab_of(wide, slab):
    return wide[:SMAX, slab * LANES : (slab + 1) * LANES]


def us(time):
    return (int(time * 1e9), int(time * 3e6))


def call(body, out_shape, in_specs, out_specs, grid=(), scratch=(), aliases=None, cost=None, limit=LESS):
    flops, moved = cost or (0, 0)
    return pl.pallas_call(
        body,
        out_shape=out_shape,
        grid=grid,
        in_specs=in_specs,
        out_specs=out_specs,
        scratch_shapes=list(scratch),
        input_output_aliases=aliases or {},
        compiler_params=pltpu.CompilerParams(vmem_limit_bytes=limit),
        cost_estimate=pl.CostEstimate(flops=flops, bytes_accessed=moved, transcendentals=0),
    )


SMEM = pl.BlockSpec(memory_space=pltpu.SMEM)
VMEM = pl.BlockSpec(memory_space=pltpu.VMEM)
ANY = pl.BlockSpec(memory_space=pl.ANY)


def whole(shape):
    zeros = (0,) * len(shape)
    return pl.BlockSpec(shape, lambda *_: zeros)


def sds(shape, dtype=F32):
    return jax.ShapeDtypeStruct(shape, dtype)


def table(item_sides, item_modes):
    row = lax.broadcasted_iota(jnp.int32, (LANES, LANES), 0)
    cell = lax.broadcasted_iota(jnp.int32, (LANES, LANES), 1)
    index = row % FREQ
    frequency = index - (MODES - 1)
    extent = item_sides[0]
    phase = frequency * cell % extent
    keep = (jnp.abs(frequency) < item_modes[0]) & (cell < extent) & (index < 2 * MODES - 1)
    length = extent.astype(F32)
    angle = 2.0 * math.pi * phase.astype(F32) / length
    wave = jnp.where(row < FREQ, jnp.cos(angle), -jnp.sin(angle)) * lax.rsqrt(length)
    return jnp.where(keep, wave, jnp.zeros_like(wave))


def big_weight(weight, out):
    out[...] = jnp.zeros_like(out)
    for block in range(2):
        rows = pl.ds(block * 64, 64)
        later = pl.ds(128 + block * 64, 64)
        out[rows, rows] = weight[0, block]
        out[rows, later] = weight[1, block]
        out[later, rows] = -weight[1, block]
        out[later, later] = weight[0, block]


def prepare_body(f_ref, w1_ref, w2_ref, f6, g6, ft3, gt3, w1c, w2c, w1t, w2t, big):
    full = f_ref[...]
    cosine, sine = full[:FREQ], full[FREQ:]
    half = jnp.concatenate([cosine[HALF - 1 : FREQ - 1], sine[HALF - 1 : FREQ - 1]], axis=0)
    f6[...] = left6(half)
    ft3[...] = left3(half.T)
    lines = [(cosine, -sine), (sine, cosine), (cosine, sine), (sine, -cosine)]
    table_ = jnp.concatenate([jnp.concatenate(line, axis=1) for line in lines], axis=0)
    g6[...] = left6(table_)
    gt3[...] = left3(table_.T)
    for source, straight, across in ((w1_ref, w1c, w1t), (w2_ref, w2c, w2t)):
        big_weight(source, big)
        straight[...] = right6(big[...])
        across[...] = right3(big[...].T)


def prepare(forward, spec_w1, spec_w2):
    shapes = [
        sds((64, 768), BF16),
        sds((256, 1536), BF16),
        sds((128, 192), BF16),
        sds((256, 768), BF16),
        sds((1536, 256), BF16),
        sds((1536, 256), BF16),
        sds((768, 256), BF16),
        sds((768, 256), BF16),
    ]
    return call(
        prepare_body,
        shapes,
        [VMEM] * 3,
        [VMEM] * 8,
        scratch=[pltpu.VMEM((256, 256), F32)],
        cost=us(3),
    )(forward, spec_w1, spec_w2)


def slab_mask(first, side):
    cell = lax.broadcasted_iota(jnp.int32, (SMAX, LANES), 0)
    return (cell < side) & (first < side)


def moments_body(side_ref, x_ref, b1_ref, gain_ref, bias_ref, out_ref):
    step = pl.program_id(0)
    side = side_ref[0]

    @pl.when(step == 0)
    def _():
        vectors = [b1_ref[...], gain_ref[...], bias_ref[...], jnp.zeros((2, LANES), F32)]
        out_ref[2 * STEPS] = jnp.concatenate(vectors, axis=0)

    for slab in range(STAGE):
        inside = slab_mask(step * STAGE + slab, side)
        value = pad_rows(jnp.where(inside, x_ref[slab], 0.0)).T
        mean = jnp.sum(value, axis=0, keepdims=True) * (1.0 / LANES)
        centered = value - mean
        block, row = step * THIRDS + slab // SLABS, pl.ds(slab % SLABS, 1)
        out_ref[block, row, :] = mean
        out_ref[STEPS + block, row, :] = jnp.sum(centered * centered, axis=0, keepdims=True)


def moments(side, x, b1, gain, bias):
    return call(
        moments_body,
        sds((2 * STEPS + 1, SLABS, LANES)),
        [
            SMEM,
            pl.BlockSpec((STAGE, SMAX, LANES), lambda i: (i, 0, 0)),
            whole((4, LANES)),
            whole((1, LANES)),
            whole((1, LANES)),
        ],
        whole((2 * STEPS + 1, SLABS, LANES)),
        grid=(SMAX // STAGE,),
        cost=us(6),
    )(side, x, b1, gain, bias)


def cotangent_body(side_ref, g_ref, early, late, total):
    chunk = pl.program_id(0)
    side = side_ref[0]

    @pl.when(chunk == 0)
    def _():
        total[...] = jnp.zeros_like(total)

    def emit(out_ref):
        carry = jnp.zeros((8, LANES), F32)
        for part in range(PARTS):
            for slab in range(SLABS):
                first = part * SLABS + slab
                value = jnp.where(slab_mask(chunk * GROUP + first, side), g_ref[first], 0.0)
                out_ref[part, 0, slab] = value
                carry = carry + fold_rows(value)
        total[...] += carry

    @pl.when(chunk < CHUNKS - 1)
    def _():
        emit(early)

    @pl.when(chunk == CHUNKS - 1)
    def _():
        emit(late)


def cotangent_pieces(side, g):
    block = (PARTS, 1, SLABS, SMAX, LANES)
    return call(
        cotangent_body,
        [sds((PARTS, CHUNKS - 1, SLABS, SMAX, LANES)), sds(block), sds((8, LANES))],
        [SMEM, pl.BlockSpec((GROUP, SMAX, LANES), lambda i: (i, 0, 0))],
        [
            pl.BlockSpec(block, lambda i: (0, jnp.minimum(i, CHUNKS - 2), 0, 0, 0)),
            whole(block),
            whole((8, LANES)),
        ],
        grid=(CHUNKS,),
        cost=us(5),
    )(side, g)


def row_stats(means, totals):
    mean = (means[0] + means[1] + means[2] + means[3]) * (1.0 / PARTS)
    total = totals[0] + totals[1] + totals[2] + totals[3]
    for part in range(PARTS):
        gap = means[part] - mean
        total = total + LANES * (gap * gap)
    spread_ = total * (1.0 / C) + EPS
    inverse = lax.rsqrt(spread_)
    inverse = inverse * (1.5 - 0.5 * spread_ * inverse * inverse)
    return mean, inverse


def first_body(side_ref, x_ref, *refs):
    stats = refs[:PARTS]
    gain_ref, bias_ref, f6_ref, b_ref, xn_ref, xhat_ref, r_ref = refs[PARTS:]
    step = pl.program_id(0)
    side = side_ref[0]
    gain, bias = gain_ref[...], bias_ref[...]
    for third in range(THIRDS):
        block = step * THIRDS + third
        mean, inverse = row_stats([ref[block] for ref in stats], [ref[STEPS + block] for ref in stats])
        r_ref[pl.ds(third * SLABS, SLABS), :] = inverse
        means, scales = spread8(mean), spread8(inverse)
        columns = []
        for inner in range(SLABS):
            slab = third * SLABS + inner
            value = jnp.where(slab_mask(step * STAGE + slab, side), x_ref[slab], 0.0)
            centered = value - slab_of(means, inner)
            normal = centered * slab_of(scales, inner)
            normed = normal * gain + bias
            xhat_ref[slab] = normal
            xn_ref[slab] = value + normed
            columns.append(pad_rows(normed))
        out = mm(f6_ref[...], right6(jnp.concatenate(columns, axis=1)))
        for inner in range(SLABS):
            b_ref[third * SLABS + inner] = out[:, part_lanes(inner)]


def first_stage(side, x, stats, gain, bias, f6):
    field = pl.BlockSpec((STAGE, SMAX, LANES), lambda i: (i, 0, 0))
    return call(
        first_body,
        [sds((SMAX, FREQ, LANES)), sds((SMAX, SMAX, LANES)), sds((SMAX, SMAX, LANES)), sds((SMAX, LANES))],
        [SMEM, field]
        + [whole((2 * STEPS + 1, SLABS, LANES))] * PARTS
        + [whole((1, LANES)), whole((1, LANES)), whole((64, 768))],
        [
            pl.BlockSpec((STAGE, FREQ, LANES), lambda i: (i, 0, 0)),
            field,
            field,
            pl.BlockSpec((STAGE, LANES), lambda i: (i, 0)),
        ],
        grid=(SMAX // STAGE,),
        cost=us(3),
    )(side, x, *stats, gain, bias, f6)


def gather_columns(re_ref, im_ref, first):
    zeros = jnp.zeros((LANES - SMAX, LANES), F32)
    re, im = [ref.reshape(SMAX * WIDTH, LANES) for ref in (re_ref, im_ref)]
    columns = []
    for j in range(first, first + BATCH):
        rows = pl.ds(j, SMAX, stride=WIDTH)
        columns.append(jnp.concatenate([re[rows, :], zeros, im[rows, :], zeros], axis=0))
    return jnp.concatenate(columns, axis=1)


def to_rows(out):
    rows = []
    for j in range(BATCH):
        lanes = part_lanes(j)
        for base in (0, 2 * FREQ):
            parts = [out[base : base + FREQ, lanes], out[base + FREQ : base + 2 * FREQ, lanes]]
            rows.append(jnp.concatenate(parts, axis=1))
    return jnp.concatenate(rows, axis=0)


def to_columns(rows):
    columns = []
    for j in range(BATCH):
        parts = []
        for sign in range(2):
            first = (2 * j + sign) * FREQ
            part = rows[first : first + FREQ]
            parts += [part[:, :LANES], part[:, LANES:]]
        columns.append(jnp.concatenate(parts, axis=0))
    return jnp.concatenate(columns, axis=1)


def counted(step, half, shape):
    row = lax.broadcasted_iota(jnp.int32, shape, 0)
    twice = (step == 0) & (half == 0)
    return (row < FREQ) | (row >= 2 * FREQ) | jnp.logical_not(twice)


def scatter_columns(re_ref, im_ref, first, out):
    re, im = [ref.reshape(SMAX * WIDTH, LANES) for ref in (re_ref, im_ref)]
    for j in range(BATCH):
        lanes = slice(j * LANES, (j + 1) * LANES)
        rows = pl.ds(first + j, SMAX, stride=WIDTH)
        re[rows, :] = out[:SMAX, lanes]
        im[rows, :] = out[LANES : LANES + SMAX, lanes]


def shrink(value):
    return jnp.where(
        value > SHRINK,
        value - SHRINK,
        jnp.where(value < -SHRINK, value + SHRINK, jnp.zeros_like(value)),
    )


def mix_body(re_ref, im_ref, g6_ref, w1_ref, b1_ref, w2_ref, b2_ref, gt3_ref, bre, bim, a_out, p_out, o_out):
    for half in range(WIDTH // BATCH):
        rows = pl.ds(half * 2 * BATCH * FREQ, 2 * BATCH * FREQ)
        spectrum = to_rows(mm(g6_ref[...], right6(gather_columns(re_ref, im_ref, BATCH * half))))
        a_out[rows, :] = spectrum
        pre = mm(left6(spectrum), w1_ref[...]) + b1_ref[...]
        p_out[rows, :] = pre
        cdf = 0.5 + 0.5 * lax.erf(pre * math.sqrt(0.5))
        out = mm(left6(pre * cdf), w2_ref[...]) + b2_ref[...]
        o_out[rows, :] = out
        if half == 0:
            out = jnp.where(counted(pl.program_id(0), half, out.shape), out, 0.0)
        scatter_columns(bre, bim, BATCH * half, mm(gt3_ref[...], right3(to_columns(shrink(out)))))


def mix_forward(b, g6, w1c, bias1, w2c, bias2, gt3):
    count = HALF // WIDTH
    re = pl.BlockSpec((SMAX, WIDTH, LANES), lambda j: (0, j, 0))
    im = pl.BlockSpec((SMAX, WIDTH, LANES), lambda j: (0, count + j, 0))
    out = pl.BlockSpec((SMAX, WIDTH, LANES), lambda j: (0, j, 0))
    rows = pl.BlockSpec((2 * WIDTH * FREQ, 256), lambda j: (j, 0))
    half = sds((SMAX, HALF, LANES))
    return call(
        mix_body,
        [half, half] + [sds((4096, 256))] * 3,
        [
            re,
            im,
            whole((256, 1536)),
            whole((1536, 256)),
            whole((1, 256)),
            whole((1536, 256)),
            whole((1, 256)),
            whole((256, 768)),
        ],
        [out, out, rows, rows, rows],
        grid=(count,),
        cost=us(0.1),
    )(b, b, g6, w1c, bias1, w2c, bias2, gt3)


def last_body(own_ref, re_ref, im_ref, xn_ref, ft3_ref, *refs):
    full, outs = refs[-1], refs[-1 - PARTS : -1]
    own = own_ref[0]
    for part in range(PARTS):
        base = (own ^ part) * SLABS
        columns = [jnp.concatenate([re_ref[base + s], im_ref[base + s]], axis=0) for s in range(SLABS)]
        out = mm(ft3_ref[...], right3(jnp.concatenate(columns, axis=1)))[:SMAX]
        for s in range(SLABS):
            value = xn_ref[base + s] + out[:, part_lanes(s)]
            full[base + s] = value
            if len(outs[part].shape) == 3:
                outs[part][s] = value
            else:
                outs[part][0, s] = value


def last_stage(own, bre, bim, xn, ft3, keep, chunk):
    half = pl.BlockSpec((GROUP, HALF, LANES), lambda i: (chunk + i, 0, 0))
    field = pl.BlockSpec((GROUP, SMAX, LANES), lambda i: (chunk + i, 0, 0))
    args = [own, bre, bim, xn, ft3]
    in_specs = [SMEM, half, half, field, whole((128, 192))]
    aliases = {}
    steps = 1 if chunk == 0 else CHUNKS - 1
    if keep is not None:
        aliases[len(args)] = PARTS
        args.append(keep)
        in_specs.append(ANY)
    piece = (SLABS, SMAX, LANES)
    shape = piece if chunk == 0 else (steps,) + piece
    spec = whole(piece)
    if chunk > 0:
        spec = pl.BlockSpec((1,) + piece, lambda i: (i, 0, 0, 0))
    *pieces, full = call(
        last_body,
        [sds(shape)] * PARTS + [sds((SMAX, SMAX, LANES))],
        in_specs,
        [spec] * PARTS + [field],
        grid=(steps,),
        aliases=aliases,
        cost=us(0.1 * steps),
    )(*args)
    return pieces, full


def weights_body(own_ref, *refs):
    own = own_ref[0]
    firsts, seconds, outs = refs[:PARTS], refs[PARTS : 2 * PARTS], refs[2 * PARTS :]
    w1h, w1l, w2h, w2l = outs
    for block in range(PARTS):
        w1h[block], w1l[block] = split2(firsts[block][...].reshape(LANES, HID))
        for part in range(PARTS):
            source = pl.ds(pl.multiple_of((own ^ part) * LANES, LANES), LANES)
            ref = seconds[block]
            value = ref[:, source] if len(ref.shape) == 2 else ref[:, 0, :, source].reshape(LANES, LANES)
            high, low = split2(value)
            w2h[block, :, part_lanes(part)] = high
            w2l[block, :, part_lanes(part)] = low


def split_weights(own, one, two, far):
    depth, height = far[0].shape[0] // PARTS, far[0].shape[2]
    far_block = (depth, 1, height, HID)
    turned = pl.BlockSpec((LANES, HID), lambda i, own_ref: (i ^ own_ref[0], 0))
    straight = pl.BlockSpec((LANES, HID), lambda i, own_ref: (i, 0))
    far_turned = pl.BlockSpec(far_block, lambda i, own_ref: (i ^ own_ref[0], 0, 0, 0))
    far_straight = pl.BlockSpec(far_block, lambda i, own_ref: (i, 1, 0, 0))
    flops, moved = us(0.1)
    return pl.pallas_call(
        weights_body,
        out_shape=[sds((4, 512, 512), BF16)] * 4,
        grid_spec=pltpu.PrefetchScalarGridSpec(
            num_scalar_prefetch=1,
            grid=(PARTS,),
            in_specs=[turned] * 2 + [far_turned] * 2 + [straight] * 2 + [far_straight] * 2,
            out_specs=[pl.BlockSpec((PARTS, LANES, HID), lambda i, own_ref: (0, i, 0))] * 4,
        ),
        compiler_params=pltpu.CompilerParams(vmem_limit_bytes=LIMIT),
        cost_estimate=pl.CostEstimate(flops=flops, bytes_accessed=moved, transcendentals=0),
    )(own, *one, *far, *two, *far)


def row_mean(parts):
    total = parts[0] + parts[1] + parts[2] + parts[3]
    return jnp.sum(total, axis=1, keepdims=True) * (1.0 / C)


def part_lanes(part):
    return slice(part * LANES, (part + 1) * LANES)


def norm_tiles(load, vectors, n_h, n_l, nh, nl, xhat, scale):
    def norm(tile, carry):
        rows = pl.ds(tile * TILE, TILE)
        values = [load(part, rows) for part in range(PARTS)]
        mean = row_mean(values)
        centered = [value - mean for value in values]
        spread_ = row_mean([value * value for value in centered]) + EPS
        inverse = lax.rsqrt(spread_)
        inverse = inverse * (1.5 - 0.5 * spread_ * inverse * inverse)
        scale[rows, :] = jnp.broadcast_to(inverse, (TILE, LANES))
        for part in range(PARTS):
            lanes = part_lanes(part)
            normal = centered[part] * inverse
            xhat[rows, lanes] = normal
            gain, bias = vectors[part][0, 4:5, :], vectors[part][0, 5:6, :]
            high, low = split2(normal * gain + bias)
            n_h[rows, lanes] = high
            n_l[rows, lanes] = low
            nh[rows, lanes] = high
            nl[rows, lanes] = low
        return carry

    lax.fori_loop(0, PIECE // TILE, norm, 0)


def bias_of(vectors, step):
    row = jnp.zeros((4, LANES), F32)
    for part in range(PARTS):
        row = jnp.where(step == part, vectors[part][0, 0:4, :], row)
    return jnp.concatenate([row[i : i + 1] for i in range(4)], axis=1)


def grad_tiles(own, g_ref, vectors, dn, xhat, scale, store, small):
    small[...] = jnp.zeros_like(small)

    def back(tile, carry):
        rows = pl.ds(tile * TILE, TILE)
        inverse = scale[rows, :]
        scaled, normals = [], []
        for part in range(PARTS):
            lanes = part_lanes(part)
            grad = dn[rows, lanes]
            normal = xhat[rows, lanes]
            small[0, :, lanes] += fold_rows(grad * normal)
            small[1, :, lanes] += fold_rows(grad)
            scaled.append(grad * vectors[part][0, 4:5, :])
            normals.append(normal)
        first = row_mean(scaled)
        second = row_mean([s * n for s, n in zip(scaled, normals)])
        for part in range(PARTS):
            delta = inverse * (scaled[part] - first - normals[part] * second)
            store(part, rows, g_ref[own ^ part, rows, :] + delta)
        return carry

    lax.fori_loop(0, PIECE // TILE, back, 0)


def split_cotangent(own, g_ref, g_h, g_l):
    for part in range(PARTS):
        lanes = part_lanes(part)
        g_h[:, lanes], g_l[:, lanes] = split2(g_ref[own ^ part])


def product3(high, low, w_h, w_l, dims=NN):
    return mm(high, w_h[0], dims) + mm(low, w_h[0], dims) + mm(high, w_l[0], dims)


def add_to(ref, step, value):
    ref[...] = jnp.where(step == 0, 0.0, ref[...]) + value


def feed_body(*refs):
    own = refs[0][0]
    x_refs, g_ref = refs[1:5], refs[5]
    w1h, w1l, w2h, w2l = refs[6:10]
    vectors = refs[10:14]
    refs = refs[len(refs) - 21 :]
    hh, hl, nh, nl, out_ref, ph, plo = refs[0:7]
    dx_refs, db1, small = refs[7:11], refs[11], refs[12]
    n_h, n_l, g_h, g_l, xhat, scale, dn, acc = refs[13:21]
    step = pl.program_id(0)

    @pl.when(step == 0)
    def _():
        norm_tiles(lambda part, rows: x_refs[part][rows, :], vectors, n_h, n_l, nh, nl, xhat, scale)
        split_cotangent(own, g_ref, g_h, g_l)

    pre = product3(n_h[...], n_l[...], w1h, w1l) + bias_of(vectors, step)
    dh = product3(g_h[...], g_l[...], w2h, w2l, NT)
    cdf, pdf = phi_pair(pre)
    high, low = split2(pre * cdf)
    hh[...] = high
    hl[...] = low
    grad = dh * (cdf + pre * pdf)
    add_to(acc, step, product3(high, low, w2h, w2l))
    high, low = split2(grad)
    ph[...] = high
    plo[...] = low
    db1[0] = fold_rows(grad)
    add_to(dn, step, product3(high, low, w1h, w1l, NT))

    @pl.when(step == pl.num_programs(0) - 1)
    def _():
        for part in range(PARTS):
            out_ref[own ^ part, 0] = acc[:, part_lanes(part)]

        def store(part, rows, value):
            dx_refs[part][rows, :] = value

        grad_tiles(own, g_ref, vectors, dn, xhat, scale, store, small)


def forward_body(*refs):
    own = refs[0][0]
    x_refs = refs[1:5]
    w1h, w1l, w2h, w2l = refs[5:9]
    vectors = refs[9:13]
    hh, hl, nh, nl, out_ref, slope, xhat, scale, n_h, n_l, acc = refs[len(refs) - 11 :]
    step = pl.program_id(0)

    @pl.when(step == 0)
    def _():
        norm_tiles(lambda part, rows: x_refs[part][rows, :], vectors, n_h, n_l, nh, nl, xhat, scale)

    pre = product3(n_h[...], n_l[...], w1h, w1l) + bias_of(vectors, step)
    cdf, pdf = phi_pair(pre)
    slope[...] = cdf + pre * pdf
    high, low = split2(pre * cdf)
    hh[...] = high
    hl[...] = low
    add_to(acc, step, product3(high, low, w2h, w2l))

    @pl.when(step == pl.num_programs(0) - 1)
    def _():
        for part in range(PARTS):
            out_ref[own ^ part, 0] = acc[:, part_lanes(part)]


def backward_body(*refs):
    own = refs[0][0]
    g_ref, w1h, w1l, w2h, w2l, slope, xhat, scale = refs[1:9]
    vectors = refs[9:13]
    refs = refs[len(refs) - 11 :]
    ph, plo, dx_refs, db1, small = refs[0], refs[1], refs[2:6], refs[6], refs[7]
    g_h, g_l, dn = refs[8:]
    step = pl.program_id(0)

    @pl.when(step == 0)
    def _():
        split_cotangent(own, g_ref, g_h, g_l)

    grad = product3(g_h[...], g_l[...], w2h, w2l, NT) * slope[...]
    high, low = split2(grad)
    ph[...] = high
    plo[...] = low
    db1[0] = fold_rows(grad)
    add_to(dn, step, product3(high, low, w1h, w1l, NT))

    @pl.when(step == pl.num_programs(0) - 1)
    def _():

        def store(part, rows, value):
            dx_refs[part][rows, :] = value

        grad_tiles(own, g_ref, vectors, dn, xhat, scale, store, small)


def feed_call(body, head, heads, weights, stats, local, keep, kinds, chunk, cost):
    rows = PIECE * CHUNKS
    specs = {
        "x": (sds((PIECE, LANES)), whole((PIECE, LANES))),
        "later": (None, pl.BlockSpec((PIECE, LANES), lambda i: (chunk - 1, 0))),
        "g": (None, pl.BlockSpec((PARTS, PIECE, LANES), lambda i: (0, chunk, 0))),
        "g2": (None, whole((PARTS, PIECE, LANES))),
        "out": (
            sds((PARTS, CHUNKS - 1, PIECE, LANES)),
            pl.BlockSpec((PARTS, 1, PIECE, LANES), lambda i: (0, chunk, 0, 0)),
        ),
        "wide": (sds((rows, 2048), BF16), pl.BlockSpec((PIECE, HID), lambda i: (chunk, i))),
        "narrow": (sds((rows, C), BF16), pl.BlockSpec((PIECE, C), lambda i: (chunk, 0))),
        "slope": (sds((PIECE, 2048)), pl.BlockSpec((PIECE, HID), lambda i: (0, i))),
        "tip": (sds((PARTS, 1, PIECE, LANES)), whole((PARTS, 1, PIECE, LANES))),
        "full": (sds((PIECE, C)), whole((PIECE, C))),
        "db1": (sds((4, 8, HID)), pl.BlockSpec((1, 8, HID), lambda i: (i, 0, 0))),
        "small": (sds((2, 8, C)), whole((2, 8, C))),
    }
    weight = pl.BlockSpec((1, 512, 512), lambda i: (i, 0, 0))
    vector = pl.BlockSpec((1, SLABS, LANES), lambda i: (2 * STEPS, 0, 0))
    args = [*head, *weights, *(value for _, value in local), *stats]
    in_specs = [SMEM] + [specs[kind][1] for kind in heads] + [weight] * 4
    in_specs += [specs[kind][1] for kind, _ in local] + [vector] * 4
    aliases = {}
    for index, array in enumerate(keep or ()):
        aliases[len(args)] = index
        args.append(array)
        in_specs.append(ANY)
    bf, big = pltpu.VMEM((PIECE, C), BF16), pltpu.VMEM((PIECE, C), F32)
    scratch = {
        "feed": [bf] * 4 + [big, pltpu.VMEM((PIECE, LANES), F32), big, big],
        "fore": [bf, bf, big],
        "back": [bf, bf, big],
    }[kinds]
    outs = {
        "feed": ["wide"] * 2 + ["narrow"] * 2 + ["out", "wide", "wide"] + ["x"] * 4 + ["db1", "small"],
        "fore": ["wide"] * 2 + ["narrow"] * 2 + ["tip", "slope", "full", "x"],
        "back": ["wide", "wide"] + ["x"] * 4 + ["db1", "small"],
    }[kinds]
    return call(
        body,
        [specs[kind][0] for kind in outs],
        in_specs,
        [specs[kind][1] for kind in outs],
        grid=(4,),
        scratch=scratch,
        aliases=aliases,
        cost=us(cost),
        limit=LIMIT,
    )(*args)


def feed(own, xs, g, weights, stats, keep, chunk):
    head, heads = [own, *xs, g], ["x" if chunk == 0 else "later"] * 4 + ["g"]
    return feed_call(feed_body, head, heads, weights, stats, [], keep, "feed", chunk, 28)


def feed_forward(own, xs, weights, stats, keep, chunk):
    return feed_call(forward_body, [own, *xs], ["later"] * 4, weights, stats, [], keep, "fore", chunk, 18)


def feed_backward(own, g, weights, local, stats, keep, chunk):
    local = list(zip(("slope", "full", "x"), local))
    return feed_call(backward_body, [own, g], ["g2"], weights, stats, local, keep, "back", chunk, 16)


def weight_body(own_ref, place_ref, th, tl, *refs):
    send, held, t_h, t_l = refs[-4:]
    step = pl.program_id(0)
    own, place = own_ref[0], place_ref[0]

    @pl.when(step == 0)
    def _():
        if len(refs[0].shape) == 2:
            t_h[...] = refs[0][...].T
            t_l[...] = refs[1][...].T
        else:
            for part in range(PARTS):
                pieces = [ref[own ^ part] for ref in refs[:2]]
                high, low = split2(jnp.concatenate(pieces, axis=0))
                t_h[part_lanes(part), :] = high.T
                t_l[part_lanes(part), :] = low.T

    out = mm(t_h[...], th[...]) + mm(t_l[...], th[...]) + mm(t_h[...], tl[...])
    count, depth = send.shape[1], send.shape[2]

    def store(ref):
        for index in range(count):
            part, inner = divmod(index, count // PARTS)
            apart = ((own ^ part) * (count // PARTS) + inner) ^ place
            where = (apart & 1) * (count // 2) + (apart >> 1)
            ref[0, where] = out[index * depth : (index + 1) * depth]

    @pl.when(step < 2)
    def _():
        store(send)

    @pl.when(step >= 2)
    def _():
        store(held)


def weight_grads(own, place, dp_size, left, th, tl, cost):
    rows = PIECE * CHUNKS
    wide = pl.BlockSpec((rows, HID), lambda i: (0, (i % 2) * 2 + 1 - i // 2))
    block = (1, dp_size, C // dp_size, HID)
    shape = sds((2,) + block[1:])
    return call(
        weight_body,
        [shape, shape],
        [SMEM, SMEM]
        + [wide] * 2
        + [pl.BlockSpec(v.shape, lambda i, n=v.ndim: (0,) * n, pipeline_mode=pl.Buffered(1)) for v in left],
        [
            pl.BlockSpec(block, lambda i: (jnp.minimum(i, 1), 0, 0, 0)),
            pl.BlockSpec(block, lambda i: (jnp.maximum(i - 2, 0), 0, 0, 0)),
        ],
        grid=(4,),
        scratch=[pltpu.VMEM((C, rows), BF16)] * 2,
        cost=us(cost),
        limit=LIMIT,
    )(own, place, th, tl, *left)


def assemble_body(turn, place_ref, near, far, out_ref, held):
    place = place_ref[0]
    half, depth = near.shape[0], near.shape[1]
    target = held if turn else out_ref
    for side, source in enumerate((near, far)):
        for index in range(half):
            rows = pl.ds(pl.multiple_of((place ^ (2 * index + side)) * depth, depth), depth)
            target[rows, :] = source[index]
    if turn:
        out_ref[...] = held[...].T


def assemble(place, near, far, turn):
    return call(
        functools.partial(assemble_body, turn),
        sds((C, HID)),
        [SMEM] + [VMEM] * 2,
        VMEM,
        scratch=[pltpu.VMEM((C, HID), F32)],
        cost=us(2),
    )(place, near, far)


def first_back_body(own_ref, f6_ref, *refs):
    d_ref, dx_ref = refs[-2:]
    own = own_ref[0]
    for chunk in range(CHUNKS):

        @pl.when(pl.program_id(0) == chunk)
        def _(pieces=refs[PARTS * chunk : PARTS * (chunk + 1)]):
            for part in range(PARTS):
                base = (own ^ part) * SLABS
                columns = [pad_rows(pieces[part][s]) for s in range(SLABS)]
                out = mm(f6_ref[...], right3(jnp.concatenate(columns, axis=1)))
                for s in range(SLABS):
                    d_ref[base + s] = out[:, part_lanes(s)]
                    dx_ref[base + s] = pieces[part][s]


def first_back(own, pieces, f6):
    return call(
        first_back_body,
        [sds((SMAX, FREQ, LANES)), sds((SMAX, SMAX, LANES))],
        [SMEM, whole((64, 384))] + [whole(piece.shape) for piece in pieces],
        [
            pl.BlockSpec((GROUP, FREQ, LANES), lambda i: (i, 0, 0)),
            pl.BlockSpec((GROUP, SMAX, LANES), lambda i: (i, 0, 0)),
        ],
        grid=(CHUNKS,),
        cost=us(8),
    )(own, f6, *pieces)


def rows3(value):
    one, two = split2(value)
    return jnp.concatenate([one, one, two], axis=0)


def mix_back_body(*refs):
    re_ref, im_ref, a_ref, p_ref, o_ref, g3_ref, w1t, w2t, gt3_ref = refs[:9]
    sums = refs[-4:]
    dw1, dw2, db1, db2 = sums
    if len(refs) == 15:
        dre, dim = refs[9:11]
    else:
        gb_ref = refs[13]
        dre, dim, pack = refs[14:17]

    @pl.when(pl.program_id(0) == 0)
    def _():
        for index, ref in enumerate(sums):
            ref[...] = jnp.zeros_like(ref) if len(refs) == 15 else refs[9 + index][...]

    for half in range(WIDTH // BATCH):
        rows = pl.ds(half * 2 * BATCH * FREQ, 2 * BATCH * FREQ)
        dz = to_rows(mm(g3_ref[...], right3(gather_columns(re_ref, im_ref, BATCH * half))))
        do = jnp.where(jnp.abs(o_ref[rows, :]) > SHRINK, dz, 0.0)
        if half == 0 and len(refs) == 15:
            do = jnp.where(counted(pl.program_id(0), half, do.shape), do, 0.0)
        pre = p_ref[rows, :]
        cdf, pdf = phi_pair(pre)
        dw2[...] += mm(rows3(pre * cdf), right3(do), TN)
        db2[...] += fold_rows(do)
        dp = mm(left3(do), w2t[...]) * (cdf + pre * pdf)
        dw1[...] += mm(rows3(a_ref[rows, :]), right3(dp), TN)
        db1[...] += fold_rows(dp)
        dx = mm(left3(dp), w1t[...])
        if half == 0 and len(refs) == 15:
            dx = jnp.where(counted(pl.program_id(0), half, dx.shape), dx, 0.0)
        scatter_columns(dre, dim, BATCH * half, mm(gt3_ref[...], right3(to_columns(dx))))

    if len(refs) == 15:
        return

    @pl.when(pl.program_id(0) == pl.num_programs(0) - 1)
    def _():
        low = lax.broadcasted_iota(jnp.int32, (FREQ, LANES), 1) < FREQ
        for index, ref in enumerate((dw1, dw2)):
            full = ref[...]
            same = full[:LANES, :LANES] + full[LANES:, LANES:]
            cross = full[:LANES, LANES:] - full[LANES:, :LANES]
            for inner, value in enumerate((same, cross)):
                rows = pl.ds((2 * index + inner) * FREQ, FREQ)
                pack[rows, :] = jnp.where(low, value[:FREQ], value[FREQ:])
        sums = [jnp.sum(ref[...], axis=0, keepdims=True) for ref in (db1, db2)]
        lines = [sums[0][:, :LANES], sums[0][:, LANES:], sums[1][:, :LANES], sums[1][:, LANES:]]
        lines.append(jnp.sum(gb_ref[...], axis=0, keepdims=True))
        pack[4 * FREQ : 4 * FREQ + 8] = jnp.concatenate(lines + [jnp.zeros((3, LANES), F32)], axis=0)


def mix_backward(d, a, p, o, g6, w1t, w2t, gt3, carry, grad_b2):
    count = HALF // WIDTH
    skip = 0 if carry is None else count // 2
    re = pl.BlockSpec((SMAX, WIDTH, LANES), lambda j: (0, skip + j, 0))
    im = pl.BlockSpec((SMAX, WIDTH, LANES), lambda j: (0, count + skip + j, 0))
    out = pl.BlockSpec((SMAX, WIDTH, LANES), lambda j: (0, j, 0))
    rows = pl.BlockSpec((2 * WIDTH * FREQ, 256), lambda j: (skip + j, 0))
    half = sds((SMAX, HALF // 2, LANES))
    args = [d, d, a, p, o, g6, w1t, w2t, gt3]
    in_specs = [re, im, rows, rows, rows, whole((256, 768))]
    in_specs += [whole((768, 256)), whole((768, 256)), whole((256, 768))]
    sums = [(256, 256), (256, 256), (8, 256), (8, 256)]
    shapes, out_specs, scratch = [half, half], [out, out], []
    if carry is None:
        shapes += [sds(shape) for shape in sums]
        out_specs += [whole(shape) for shape in sums]
    else:
        args += [*carry, grad_b2]
        in_specs += [whole(shape) for shape in sums] + [whole((8, LANES))]
        shapes.append(sds((PACK, LANES)))
        out_specs.append(whole((PACK, LANES)))
        scratch = [pltpu.VMEM(shape, F32) for shape in sums]
    return call(
        mix_back_body, shapes, in_specs, out_specs, grid=(count // 2,), scratch=scratch, cost=us(13)
    )(*args)


def last_back_body(re0, re1, im0, im1, dx_ref, xhat_ref, gain_ref, ft3_ref, pack_ref, *refs):
    b1_refs, norm_refs = refs[:CHUNKS], refs[CHUNKS : 2 * CHUNKS]
    dn_ref, pack = refs[2 * CHUNKS : 2 * CHUNKS + 2]
    sums, small = refs[-1 - PARTS : -1], refs[-1]
    step = pl.program_id(0)

    @pl.when(step == 0)
    def _():
        small[...] = jnp.zeros_like(small)
        norms = norm_refs[0][...]
        for ref in norm_refs[1:]:
            norms = norms + ref[...]
        norms = [jnp.sum(norms[i], axis=0, keepdims=True) for i in range(2)]
        for part in range(PARTS):
            total = b1_refs[0][part]
            for ref in b1_refs[1:]:
                total = total + ref[part]
            total = jnp.sum(total, axis=0, keepdims=True)
            lines = [total[:, part_lanes(i)] for i in range(4)]
            lines += [value[:, part_lanes(part)] for value in norms]
            lines.append(jnp.zeros((2, LANES), F32))
            sums[part][2 * STEPS] = jnp.concatenate(lines, axis=0)

    gain = gain_ref[...]
    for third in range(THIRDS):
        slabs = [third * SLABS + inner for inner in range(SLABS)]
        columns = [jnp.concatenate([re0[s], re1[s], im0[s], im1[s]], axis=0) for s in slabs]
        out = mm(ft3_ref[...], right3(jnp.concatenate(columns, axis=1)))[:SMAX]
        for index, s in enumerate(slabs):
            grad = dx_ref[s] + out[:, part_lanes(index)]
            dn_ref[s] = grad
            product = grad * xhat_ref[s]
            small[0] += fold_rows(product)
            small[1] += fold_rows(grad)
            for which, value in enumerate((grad, product)):
                row = jnp.sum(pad_rows(value * gain).T, axis=0, keepdims=True)
                for ref in sums:
                    block = which * STEPS + step * THIRDS + s // SLABS
                    ref[block, pl.ds(s % SLABS, 1), :] = row

    @pl.when(step == pl.num_programs(0) - 1)
    def _():
        pack[...] = pack_ref[...]
        for index in range(2):
            where = pl.ds(4 * FREQ + 5 + index, 1)
            pack[where, :] = jnp.sum(small[index], axis=0, keepdims=True)


def last_back(quarters, dx, xhat, gain, ft3, pack, b1s, norms):
    half = pl.BlockSpec((STAGE, HALF // 2, LANES), lambda i: (i, 0, 0))
    field = pl.BlockSpec((STAGE, SMAX, LANES), lambda i: (i, 0, 0))
    shape = (2 * STEPS + 1, SLABS, LANES)
    return call(
        last_back_body,
        [sds((SMAX, SMAX, LANES)), sds((PACK, LANES))] + [sds(shape)] * PARTS,
        [half] * 4
        + [field, field, whole((1, LANES)), whole((128, 192)), whole((PACK, LANES))]
        + [whole((4, 8, HID))] * CHUNKS
        + [whole((2, 8, C))] * CHUNKS,
        [field, whole((PACK, LANES))] + [whole(shape)] * PARTS,
        grid=(SMAX // STAGE,),
        scratch=[pltpu.VMEM((2, 8, LANES), F32)],
        cost=us(13),
    )(*quarters, dx, xhat, gain, ft3, pack, *b1s, *norms)


def final_body(side_ref, dx_ref, dn_ref, xhat_ref, r_ref, gain_ref, *refs):
    sums, out_ref = refs[:PARTS], refs[PARTS]
    step = pl.program_id(0)
    side = side_ref[0]
    for third in range(THIRDS):
        block = step * THIRDS + third
        inverse = r_ref[pl.ds(third * SLABS, SLABS), :]
        total = [sum(ref[which * STEPS + block] for ref in sums) for which in range(2)]
        first = total[0] * (inverse * (1.0 / C))
        second = total[1] * (inverse * (1.0 / C))
        wide = [spread8(value) for value in (inverse, first, second)]
        for inner in range(SLABS):
            slab = third * SLABS + inner
            scaled = dn_ref[slab] * gain_ref[...]
            scale, shift, slope = [slab_of(value, inner) for value in wide]
            value = dx_ref[slab] + (scale * scaled - shift - xhat_ref[slab] * slope)
            out_ref[slab] = jnp.where(slab_mask(step * STAGE + slab, side), value, 0.0)


def final_stage(side, dx, dn, xhat, sums, r, gain):
    field = pl.BlockSpec((STAGE, SMAX, LANES), lambda i: (i, 0, 0))
    return call(
        final_body,
        sds((SMAX, SMAX, LANES)),
        [SMEM, field, field, field, pl.BlockSpec((STAGE, LANES), lambda i: (i, 0)), whole((1, LANES))]
        + [whole((2 * STEPS + 1, SLABS, LANES))] * PARTS,
        field,
        grid=(SMAX // STAGE,),
        cost=us(13),
    )(side, dx, dn, xhat, r, gain, *sums)


def output_body(side_ref, x_ref, y_ref, tip_ref, b2_ref, out_ref):
    step = pl.program_id(0)
    side = side_ref[0]
    for part in range(PARTS):
        for inner in range(SLABS):
            slab = part * SLABS + inner
            branch = jnp.where(step < CHUNKS - 1, y_ref[part, 0, inner], tip_ref[part, inner])
            value = x_ref[slab] + branch + b2_ref[...]
            out_ref[slab] = jnp.where(slab_mask(step * GROUP + slab, side), value, 0.0)


def output_stage(side, x1, y, tip, b2):
    field = pl.BlockSpec((GROUP, SMAX, LANES), lambda i: (i, 0, 0))
    return call(
        output_body,
        sds((SMAX, SMAX, LANES)),
        [
            SMEM,
            field,
            pl.BlockSpec(
                (PARTS, 1, SLABS, SMAX, LANES), lambda i: (0, jnp.minimum(i, CHUNKS - 2), 0, 0, 0)
            ),
            whole((PARTS, SLABS, SMAX, LANES)),
            whole((1, LANES)),
        ],
        field,
        grid=(CHUNKS,),
        cost=us(5),
    )(side, x1, y, tip, b2)


def swap(value, axis, size, distance):
    return lax.ppermute(value, axis, [(i, i ^ distance) for i in range(size)])


def exchange(pieces):
    return [pieces[0]] + [swap(pieces[part], "blk", PARTS, part) for part in range(1, PARTS)]


def after(value, *others):
    return lax.optimization_barrier((value, *others))[0]


def halve(value, size, distance, gate):
    cut = value.shape[0] // 2
    return after(value[:cut], gate) + swap(value[cut:], "dp", size, distance)


def scatter_last(mine, size, gate):
    total = after(mine[0], gate)
    for index in range(1, size // 2):
        total = total + swap(mine[index], "dp", size, 2 * index)
    return total


def gather_near(piece, size, gate):
    return jnp.stack([after(piece, gate)] + [swap(piece, "dp", size, 2 * index) for index in range(1, size // 2)])


def per_device(
    dp_size,
    block_input,
    cotangent,
    item_sides,
    item_modes,
    ln1_gain,
    ln1_bias,
    spec_w1,
    spec_b1,
    spec_w2,
    spec_b2,
    ln2_gain,
    ln2_bias,
    mlp_w1,
    mlp_b1,
    mlp_w2,
    mlp_b2,
):
    own = lax.axis_index("blk").astype(jnp.int32).reshape(1)
    place = lax.axis_index("dp").astype(jnp.int32).reshape(1)
    cube = (SMAX, SMAX, LANES)
    x = block_input.reshape(cube)
    gain1, bias1 = ln1_gain.reshape(1, LANES), ln1_bias.reshape(1, LANES)

    depth = C // dp_size
    share = jnp.stack([lax.dynamic_slice_in_dim(w, place[0] * depth, depth) for w in (mlp_w1, mlp_w2)])
    share = swap(share, "blk", PARTS, 2)
    moment = moments(
        item_sides, x, mlp_b1.reshape(4, LANES), ln2_gain.reshape(1, LANES), ln2_bias.reshape(1, LANES)
    )
    stats = exchange([moment] * PARTS)
    g_parts, g_late, grad_b2 = cotangent_pieces(item_sides, after(cotangent.reshape(cube), moment))
    g = lax.all_to_all(after(g_parts, *stats[1:]), "blk", 0, 0).reshape(PARTS, (CHUNKS - 1) * PIECE, LANES)
    sides = after(item_sides, g_parts)
    f6, g6, ft3, gt3, w1c, w2c, w1t, w2t = prepare(table(sides, item_modes), spec_w1, spec_w2)
    far = lax.all_gather(after(share, moment), "dp", axis=0)
    mlp_w1, mlp_w2, _ = lax.optimization_barrier((mlp_w1, mlp_w2, stats[3]))
    one = [mlp_w1, swap(mlp_w1, "blk", PARTS, 1)]
    two = [mlp_w2, swap(mlp_w2, "blk", PARTS, 1)]

    b, xn, xhat, r = first_stage(item_sides, after(x, g_parts), stats, gain1, bias1, f6)
    bre, bim, a, p, o = mix_forward(
        b, g6, w1c, spec_b1.reshape(1, 256), w2c, spec_b2.reshape(1, 256), gt3
    )
    far = after(far, bre)
    far = [far, swap(far, "blk", PARTS, 1)]
    first_pieces, x1 = last_stage(own, bre, bim, xn, ft3, None, 0)
    x1_first = [piece.reshape(PIECE, LANES) for piece in exchange(first_pieces)]
    weights = split_weights(own, one, two, far)
    field = after(xn, g, *weights)
    pieces, x1 = last_stage(own, bre, bim, field, ft3, x1, 1)
    x1_later = [piece.reshape((CHUNKS - 1) * PIECE, LANES) for piece in exchange(pieces)]

    x1_first[0] = after(x1_first[0], x1)
    keep, b1s, norms, dx_early = None, [], [], []
    for chunk in range(CHUNKS - 1):
        results = feed(own, x1_later if chunk else x1_first, g, weights, stats, keep, chunk)
        keep = results[:7]
        dx_early.append(exchange(results[7:11]))
        if chunk == 0:
            g_late = lax.all_to_all(after(g_late, results[7]), "blk", 0, 0).reshape(PARTS, PIECE, LANES)
        b1s.append(results[11])
        norms.append(results[12])
    x1_now = [after(x1_later[0], g_late), *x1_later[1:]]
    results = feed_forward(own, x1_now, weights, stats, keep[:4], CHUNKS - 1)
    hh, hl, nh, nl, tip = results[:5]
    branch = lax.all_to_all(after(keep[4], hh), "blk", 0, 0)
    send2, held2 = weight_grads(own, place, dp_size, [after(g, *dx_early[0][1:], *dx_early[1][1:]), g_late], hh, hl, 20)
    local = list(results[5:])
    local[1] = after(local[1], held2)
    results = feed_backward(own, g_late, weights, local, stats, keep[5:7], CHUNKS - 1)
    ph, plo = results[:2]
    b1s.append(results[6])
    norms.append(results[7])
    got2 = after(held2, ph) + swap(send2, "blk", PARTS, 1)
    dx_all = dx_early + [exchange(results[2:6])]
    dx_all = [v.reshape(SLABS, SMAX, LANES) for group in dx_all for v in group]
    tip = lax.all_to_all(after(tip, ph), "blk", 0, 0)
    ph = after(ph, got2, branch)
    send1, held1 = weight_grads(own, place, dp_size, [nh, nl], ph, plo, 20)

    half, cut = dp_size // 2, send1.shape[2] // 2
    mine2 = got2[:, :half] + swap(got2[:, half:], "dp", dp_size, 1)
    got1 = after(held1, *dx_all[-3:]) + swap(send1, "blk", PARTS, 1)
    dx_all[0] = after(dx_all[0], mine2, tip)
    d, dx = first_back(own, dx_all, f6)
    mine2 = after(mine2[0], d) + swap(mine2[1], "blk", PARTS, 2)
    block_output = output_stage(
        item_sides,
        after(x1, d),
        branch.reshape(PARTS, CHUNKS - 1, SLABS, SMAX, LANES),
        tip.reshape(PARTS, SLABS, SMAX, LANES),
        mlp_b2.reshape(1, LANES),
    )
    early = mix_backward(after(d, got1, mine2, block_output), a, p, o, g6, w1t, w2t, gt3, None, None)
    kept = after(got1, early[0])
    one = kept[:, :half, :cut] + swap(got1[:, half:, :cut], "dp", dp_size, 1)
    two = kept[0, :, cut:] + swap(got1[1, :, cut:], "blk", PARTS, 2)
    second = scatter_last(after(mine2, d), dp_size, early[0])
    d_late = after(d, early[0], second, one, two)
    late = mix_backward(d_late, a, p, o, g6, w1t, w2t, gt3, early[2:], grad_b2)
    near2 = gather_near(after(second, early[0]), dp_size, late[0])
    one = after(one[0], late[0]) + swap(one[1], "blk", PARTS, 2)
    two = after(two[:half], late[0]) + swap(two[half:], "dp", dp_size, 1)
    quarters = [early[0], late[0], early[1], late[1]]
    dx_gated = after(dx, near2, one, two)
    dn, pack, *sums = last_back(quarters, dx_gated, xhat, gain1, ft3, late[2], b1s, norms)
    first = scatter_last(jnp.concatenate([one, two], axis=1), dp_size, dn)
    far2 = swap(after(near2, late[0]), "dp", dp_size, 1)
    sums = exchange([after(value, first) for value in sums])
    input_grad = final_stage(item_sides, after(dx, far2), dn, xhat, sums, r, gain1)
    tail = sums[0][-1] + sums[1][-1] + sums[2][-1] + sums[3][-1]
    pack = jnp.concatenate([pack, tail], axis=0)
    near1 = gather_near(first, dp_size, input_grad)
    pack = after(pack, input_grad) + swap(pack, "dp", dp_size, 1)
    distance = 2
    while distance < dp_size:
        pack = pack + swap(pack, "dp", dp_size, distance)
        distance *= 2
    far1 = swap(near1, "dp", dp_size, 1)
    w1_grad = assemble(place, near1, far1, False)
    w2_grad = assemble(place, near2, far2, True)

    spec = pack[: 4 * FREQ].reshape(2, 2, FREQ, 2, FREQ).transpose(0, 1, 3, 2, 4)
    rest = pack[4 * FREQ :]
    return (
        block_output.reshape(SMAX * SMAX, LANES),
        input_grad.reshape(SMAX * SMAX, LANES),
        rest[5],
        rest[6],
        spec[0],
        rest[0:2].reshape(2, 2, 64),
        spec[1],
        rest[2:4].reshape(2, 2, 64),
        rest[12],
        rest[13],
        w1_grad,
        rest[8:12].reshape(HID),
        w2_grad,
        rest[4],
    )


def solution(mesh):
    in_specs = (
        P("dp", "blk"),
        P("dp", "blk"),
        P("dp"),
        P("dp"),
        P("blk"),
        P("blk"),
        P(None, "blk", None, None),
        P(None, "blk", None),
        P(None, "blk", None, None),
        P(None, "blk", None),
        P("blk"),
        P("blk"),
        P(None, "blk"),
        P("blk"),
        P("blk", None),
        P("blk"),
    )
    out_specs = (
        P("dp", "blk"),
        P("dp", "blk"),
        P("blk"),
        P("blk"),
        P(None, "blk", None, None),
        P(None, "blk", None),
        P(None, "blk", None, None),
        P(None, "blk", None),
        P("blk"),
        P("blk"),
        P(None, "blk"),
        P("blk"),
        P("blk", None),
        P("blk"),
    )
    return jax.shard_map(
        functools.partial(per_device, mesh.shape["dp"]),
        mesh=mesh,
        in_specs=in_specs,
        out_specs=out_specs,
        check_vma=False,
    )
```
